32 devices in a mesh: dp: 4 (over z), row: 2 (over y), col: 4 (over x, core).
Axes of the slice: x: 2, y: 2, z: 4, core: 2. Of those that a mesh axis runs over, the one named last changes fastest.
Arguments:
- tokens: float32 [8, 2048, 768], P(('dp', 'row'), 'col'), may hold values from -4 to 4
- condition: float32 [8, 128], P(('dp', 'row')), may hold values from -3 to 3
- lengths: int32 [8], P(('dp', 'row')), may hold values from 1024 to 2048, as said below
- condition_weight: float32 [128, 4608], P(None, ('dp', 'row')), may hold values from -0.25 to 0.25
- condition_bias: float32 [4608], replicated, may hold values from -1 to 1
- attention_in: float32 [768, 3, 768], P(('dp', 'row'), None, 'col'), may hold values from -0.21875 to 0.21875
- attention_out: float32 [768, 768], P('col', ('dp', 'row')), may hold values from -0.4375 to 0.4375
- up_weight: float32 [768, 3072], P(('dp', 'row'), 'col'), may hold values from -0.21875 to 0.21875
- up_bias: float32 [3072], replicated, may hold values from -1.5 to 1.5
- down_weight: float32 [3072, 768], P('col', ('dp', 'row')), may hold values from -0.109375 to 0.109375
- down_bias: float32 [768], replicated, may hold values from -1.5 to 1.5
- cotangent: float32 [8, 2048, 768], P(('dp', 'row'), 'col'), may hold values from -4 to 4
Outputs:
- output: float32 [8, 2048, 768], P(('dp', 'row'), 'col')
- gradient_tokens: float32 [8, 2048, 768], P(('dp', 'row'), 'col')
- gradient_condition: float32 [8, 128], P(('dp', 'row'))
- gradient_condition_weight: float32 [128, 4608], P(None, ('dp', 'row'))
- gradient_condition_bias: float32 [4608], replicated
- gradient_attention_in: float32 [768, 3, 768], P(('dp', 'row'), None, 'col')
- gradient_attention_out: float32 [768, 768], P('col', ('dp', 'row'))
- gradient_up_weight: float32 [768, 3072], P(('dp', 'row'), 'col')
- gradient_up_bias: float32 [3072], P('col')
- gradient_down_weight: float32 [3072, 768], P('col', ('dp', 'row'))
- gradient_down_bias: float32 [768], replicated
The draws below stay inside these ranges and needn't reach their ends.
Inputs may be any that keep to these rules, and one draw needn't show every extreme that they name: Row b holds lengths[b] valid tokens in its first slots; some row has 2048 valid tokens and another has 1024.
All inputs are finite; a program needn't handle non-finite values.
Results may differ from the reference program's by a relative error of at most 0.012.
The reference program's roundings to bfloat16 on the way count: a program that leaves them out, or rounds other values in their place, can miss the bound.
Values may be sent and summed in bfloat16 or wider, within the bound.
A program may use at most 128 MiB of HBM per device.

```python
import math
import jax
import jax.numpy as jnp
from jax import lax

D = 768
HEADS = 12
HD = 64
FF = 3072
COND = 128
LEN_MIN = 1024
SEQ = 2048
SEQS = 8


def draw_lengths(key, part):
    least = min(LEN_MIN, SEQ // 2)
    base = jax.random.randint(jax.random.fold_in(key, 11), (SEQS,), least, SEQ + 1)
    place = jax.random.randint(jax.random.fold_in(key, 12), (), 0, SEQS)
    index = jnp.arange(SEQS)
    base = jnp.where(index == place, SEQ, base)
    base = jnp.where(index == (place + 1) % SEQS, least, base)
    return base.astype(jnp.int32)


def block_scale(key, dims, shards, smallest, high):
    loudness = 1.0
    for axis_at, blocks in shards:
        draws = jax.random.uniform(jax.random.fold_in(jax.random.fold_in(key, 6), axis_at), (blocks,), jnp.float32, smallest / len(shards), high / len(shards))
        loudness = loudness * jnp.repeat(jnp.exp(draws), dims[axis_at] // blocks).reshape((-1,) + (1,) * (len(dims) - 1 - axis_at))
    return loudness


def noise(stream_key, extent, scale, most, cuts=(), held_as=jnp.bfloat16):
    factor_of = block_scale(stream_key, extent, cuts, -0.22, 0.18) if cuts else 1.0
    values = jax.random.normal(stream_key, extent, jnp.float32) * scale * factor_of
    return jnp.minimum(jnp.maximum(values, -most), most).astype(held_as)


def setup_inputs(seed: int = 0) -> dict:
    key_list = jax.random.split(jax.random.key(seed), 13)
    return {
        "tokens": noise(key_list[0], (SEQS, SEQ, D), 1.0, 4.0, ((0, 8), (1, 4)), jnp.float32),
        "condition": noise(key_list[1], (SEQS, COND), 1.0, 3.0, ((0, 8),), jnp.float32),
        "lengths": draw_lengths(jax.random.fold_in(key_list[12], 71), 0),
        "condition_weight": noise(key_list[3], (COND, 6 * D), (COND * 4) ** -0.5, 0.25, ((1, 8),), jnp.float32),
        "condition_bias": noise(key_list[4], (6 * D,), 0.3, 1.0, (), jnp.float32),
        "attention_in": noise(key_list[5], (D, 3, D), D ** -0.5, 0.21875, ((0, 8), (2, 4)), jnp.float32),
        "attention_out": noise(key_list[6], (D, D), (D // 4) ** -0.5, 0.4375, ((0, 4), (1, 8)), jnp.float32),
        "up_weight": noise(key_list[7], (D, FF), D ** -0.5, 0.21875, ((0, 8), (1, 4)), jnp.float32),
        "up_bias": noise(key_list[8], (FF,), 0.5, 1.5, (), jnp.float32),
        "down_weight": noise(key_list[9], (FF, D), FF ** -0.5, 0.109375, ((0, 4), (1, 8)), jnp.float32),
        "down_bias": noise(key_list[10], (D,), 0.5, 1.5, (), jnp.float32),
        "cotangent": noise(key_list[11], (SEQS, SEQ, D), 1.0, 4.0, ((0, 8), (1, 4)), jnp.float32),
    }


@jax.custom_vjp
def low(v):
    return lax.optimization_barrier(v.astype(jnp.bfloat16)).astype(jnp.float32)

@jax.custom_vjp
def low_back(v):
    return v

def low_keep(v):
    return (low(v), None)

def low_pass(kept, grad):
    return (grad,)

def back_keep(v):
    return (v, None)

def back_low(kept, grad):
    return (low(grad),)
low.defvjp(low_keep, low_pass)
low_back.defvjp(back_keep, back_low)
EPSILON = 1e-06
MASKED = -1e+30
CUBIC = 0.044715
SLOPE = math.sqrt(2.0 / math.pi)
HIGHEST = lax.Precision.HIGHEST

def product(left, right):
    return jnp.dot(left, right, precision=HIGHEST)

def layer_norm(values):
    center = values - lax.optimization_barrier(jnp.mean(values, axis=-1, keepdims=True))
    spread = lax.optimization_barrier(jnp.mean(center * center, axis=-1, keepdims=True))
    return center * lax.rsqrt(spread + EPSILON)

def norm_shift(values, shift, scale):
    return layer_norm(values) * (1.0 + scale) + shift

def gelu_tanh(values):
    return 0.5 * values * (1.0 + jnp.tanh(SLOPE * (values + CUBIC * values * values * values)))

def rotary_tables(length, head_size):
    half = head_size // 2
    exponent = jnp.arange(half).astype(jnp.float32) * (2.0 / head_size)
    frequency = jnp.exp(-math.log(10000.0) * exponent)
    angle = jnp.arange(length).astype(jnp.float32)[:, None] * frequency[None, :]
    return (jnp.cos(angle)[:, None, :], jnp.sin(angle)[:, None, :])

def rotate(values, cosine, sine):
    half = values.shape[-1] // 2
    first = values[..., :half]
    second = values[..., half:]
    return jnp.concatenate([first * cosine - second * sine, second * cosine + first * sine], axis=-1)

def attend_block(query_block, key_rows, value_rows, key_valid):
    scale = 1.0 / math.sqrt(HD)
    raw = jnp.einsum('qhd,khd->hqk', query_block, key_rows, precision=HIGHEST)
    scores = jnp.where(key_valid[None, None, :], low_back(raw) * scale, MASKED)
    top = lax.optimization_barrier(jnp.max(scores, axis=-1, keepdims=True))
    weights = jnp.exp(scores - top)
    weights = weights / lax.optimization_barrier(jnp.sum(weights, axis=-1, keepdims=True))
    return jnp.einsum('hqk,khd->qhd', low(weights), value_rows, precision=HIGHEST)

def forward_sequence(rows, condition_row, length, condition_weight, condition_bias, attention_in, attention_out, up_weight, up_bias, down_weight, down_bias):
    modulation = product(low(condition_row)[None, :], low(condition_weight))[0] + condition_bias
    parts = modulation.reshape(6, D)
    key_valid = jnp.arange(SEQ) < length
    normed = low(norm_shift(rows, parts[0], parts[1]))
    projected = low_back(jnp.einsum('sd,dte->ste', normed, low(attention_in), precision=HIGHEST))
    cosine, sine = rotary_tables(SEQ, HD)
    query_rows = low(rotate(projected[:, 0].reshape(SEQ, HEADS, HD), cosine, sine))
    key_rows = low(rotate(projected[:, 1].reshape(SEQ, HEADS, HD), cosine, sine))
    value_rows = low(projected[:, 2].reshape(SEQ, HEADS, HD))
    block = min(512, SEQ)
    pieces = query_rows.reshape(SEQ // block, block, HEADS, HD)
    mixed = lax.map(jax.checkpoint(lambda piece: attend_block(piece, key_rows, value_rows, key_valid)), pieces)
    mixed = low(low_back(mixed.reshape(SEQ, D)))
    attention = low_back(product(mixed, low(attention_out)))
    middle = rows + parts[2] * attention
    second = low(norm_shift(middle, parts[3], parts[4]))
    before = low_back(product(second, low(up_weight)) + up_bias)
    hidden = low(gelu_tanh(before))
    feed = low_back(product(hidden, low(down_weight)))
    return middle + parts[5] * (feed + down_bias)

def reference(tokens, condition, lengths, condition_weight, condition_bias, attention_in, attention_out, up_weight, up_bias, down_weight, down_bias, cotangent):
    params = (condition_weight, condition_bias, attention_in, attention_out, up_weight, up_bias, down_weight, down_bias)
    totals = tuple((jnp.zeros_like(entry) for entry in params))

    def one_sequence(carry, item):
        rows, condition_row, length, seed_rows = item

        def closed(rows, condition_row, *weights):
            return forward_sequence(rows, condition_row, length, *weights)
        result, pull = jax.vjp(closed, rows, condition_row, *params)
        valid = (jnp.arange(SEQ) < length).astype(jnp.float32)
        slopes = pull(seed_rows * valid[:, None])
        updated = tuple((total + slope for total, slope in zip(carry, slopes[2:])))
        return (updated, (result, slopes[0], slopes[1]))
    totals, (outputs, tokens_back, condition_back) = lax.scan(one_sequence, totals, (tokens, condition, lengths, cotangent))
    return (outputs, tokens_back, condition_back, totals[0], totals[1], totals[2], totals[3], totals[4], totals[5], totals[6], totals[7])
```

```python
import functools
import math

import jax
import jax.numpy as jnp
import numpy as np
from jax import lax
from jax.experimental import pallas as pl
from jax.experimental.pallas import tpu as pltpu
from jax.sharding import PartitionSpec as P

HD = 64
AUG = 128
EPSILON = 1e-06
MASKED = -1e30
CUBIC = 0.044715
SLOPE = math.sqrt(2.0 / math.pi)
SCALE = 1.0 / math.sqrt(HD)
UNIT = SCALE * math.log2(math.e)
F32 = jnp.float32
BF16 = jnp.bfloat16
VMEM_LIMIT = 60 << 20


def layer_norm(values):
    center = values - jnp.mean(values, axis=-1, keepdims=True)
    spread = jnp.mean(center * center, axis=-1, keepdims=True)
    return center * lax.rsqrt(spread + EPSILON)


def norm_shift(values, shift, scale):
    return layer_norm(values) * (1.0 + scale) + shift


def gelu_tanh(values):
    return 0.5 * values * (1.0 + jnp.tanh(SLOPE * (values + CUBIC * values * values * values)))


def rotary_tables(length):
    half = HD // 2
    exponent = np.arange(half, dtype=np.float32) * np.float32(2.0 / HD)
    frequency = np.exp(np.float32(-math.log(10000.0)) * exponent).astype(np.float32)
    angle = frequency[:, None] * np.arange(length, dtype=np.float32)[None, :]
    angle = angle.astype(np.float32).astype(np.float64)
    return np.cos(angle).astype(np.float32), np.sin(angle).astype(np.float32)


def contract(left, right, left_axis, right_axis):
    return lax.dot_general(
        left,
        right,
        (((left_axis,), (right_axis,)), ((), ())),
        preferred_element_type=F32,
    )


def block_at(index, size):
    return pl.ds(pl.multiple_of(index * size, size), size)


def split_three(values):
    high = values.astype(BF16)
    rest = values - high.astype(F32)
    middle = rest.astype(BF16)
    low = (rest - middle.astype(F32)).astype(BF16)
    return high.astype(F32), middle.astype(F32), low.astype(F32)


def augment(rows, extras):
    n = rows.shape[1]
    extras = [jnp.broadcast_to(e, (1, n)) for e in extras]
    pad = jnp.zeros((AUG - HD - len(extras), n), F32)
    return jnp.concatenate([rows] + extras + [pad], axis=0)


def project_rotate(heads, size, normed, weight_t, cosine, sine, bias, qkv, query, key):
    length = normed.shape[0]
    half = HD // 2

    def step(i, _):
        here = block_at(i, size)
        both = contract(weight_t[...], normed[here, :], 1, 1)
        c, s = cosine[:, here], sine[:, here]
        one = jnp.ones((1, size), F32)
        for h in range(heads):
            for t in range(3):
                at = (t * heads + h) * HD
                if t == 2:
                    qkv[t * heads + h, :, here] = both[at : at + HD].astype(BF16)
                    continue
                a, b = both[at : at + half], both[at + half : at + HD]
                turned = jnp.concatenate([a * c - b * s, b * c + a * s], axis=0)
                qkv[t * heads + h, :, here] = turned.astype(BF16)
                if t == 0:
                    query[h, :, here] = augment(turned, [one]).astype(BF16)
                else:
                    wide = augment(turned, [bias[:, here], one, one, one])
                    key[h, here, :] = wide.T.astype(BF16)
        return 0

    lax.fori_loop(0, length // size, step, 0)


def attend_block(heads, here, query, key, value_t, mixed_t, log_total):
    scores = [contract(key[h], query[h, :, here], 1, 0) for h in range(heads)]
    for h in range(heads):
        top = jnp.max(scores[h], axis=0, keepdims=True)
        weights = jnp.exp2((scores[h] - top) * UNIT)
        total = jnp.sum(weights, axis=0, keepdims=True)
        out = contract(value_t[h], weights.astype(BF16), 1, 0) * (1.0 / total)
        mixed_t[h, :, here] = out.astype(BF16)
        log_total[h, :, here] = top * UNIT + jnp.log2(total)


def attention_forward_kernel(
    heads, normed, weight, cosine, sine, bias, qkv, mixed_t, log_total, weight_t, query, key
):
    length = normed.shape[0]
    weight_t[...] = weight[...].astype(F32).T.astype(BF16)
    size = min(512, length)
    project_rotate(heads, size, normed, weight_t, cosine, sine, bias, qkv, query, key)

    def step(i, _):
        attend_block(
            heads, block_at(i, size), query, key, qkv.at[pl.ds(2 * heads, heads)], mixed_t, log_total
        )
        return 0

    lax.fori_loop(0, length // size, step, 0)


def attention_forward(heads, normed, weight, cosine, sine, bias):
    length, width = normed.shape
    vmem = pl.BlockSpec(memory_space=pltpu.VMEM)
    return pl.pallas_call(
        functools.partial(attention_forward_kernel, heads),
        out_shape=[
            jax.ShapeDtypeStruct((3 * heads, HD, length), BF16),
            jax.ShapeDtypeStruct((heads, HD, length), BF16),
            jax.ShapeDtypeStruct((heads, 1, length), F32),
        ],
        in_specs=[vmem] * 5,
        out_specs=[vmem] * 3,
        scratch_shapes=[
            pltpu.VMEM((3 * heads * HD, width), BF16),
            pltpu.VMEM((heads, AUG, length), BF16),
            pltpu.VMEM((heads, length, AUG), BF16),
        ],
        compiler_params=pltpu.CompilerParams(vmem_limit_bytes=VMEM_LIMIT),
    )(normed, weight, cosine, sine, bias)


def prepare_backward(heads, h, size, length, qkv, bias, log_total, mixed_t, back_t, query, key, value, back):
    def step(i, _):
        here = block_at(i, size)
        one = jnp.ones((1, size), F32)
        zero = jnp.zeros((1, size), F32)
        logs = split_three(log_total[h, :, here] * (-1.0 / UNIT))
        query[h, :, here] = augment(qkv[h, :, here].astype(F32), [one, *logs]).astype(BF16)
        keys = augment(qkv[heads + h, :, here].astype(F32), [bias[:, here], one, one, one])
        key[h, here, :] = keys.T.astype(BF16)
        values = augment(qkv[2 * heads + h, :, here].astype(F32), [zero, one, one, one])
        value[h, here, :] = values.T.astype(BF16)
        grad = back_t[h, :, here].astype(F32)
        center = jnp.sum(grad * mixed_t[h, :, here].astype(F32), axis=0, keepdims=True)
        back[h, :, here] = augment(grad, [zero, *split_three(-center)]).astype(BF16)
        return 0

    lax.fori_loop(0, length // size, step, 0)


def attention_backward_kernel(
    heads, qkv, bias, log_total, mixed_t, back_t, cosine, sine, out, query, key, value, back, key_sum, value_sum
):
    length = qkv.shape[2]
    size = min(512, length)
    half = HD // 2

    def turn_back(rows, here):
        c, s = cosine[:, here], sine[:, here]
        a, b = rows[:half], rows[half:]
        return jnp.concatenate([a * c + b * s, b * c - a * s], axis=0)

    for h in range(heads):
        prepare_backward(heads, h, size, length, qkv, bias, log_total, mixed_t, back_t, query, key, value, back)
    key_sum[...] = jnp.zeros_like(key_sum)
    value_sum[...] = jnp.zeros_like(value_sum)

    def step(i, _):
        here = block_at(i, size)
        for h in range(heads):
            q, d = query[h, :, here], back[h, :, here]
            weights = jnp.exp2(contract(key[h], q, 1, 0) * UNIT)
            grads = (weights * contract(value[h], d, 1, 0)).astype(BF16)
            value_sum[h] += contract(d[:HD], weights.astype(BF16), 1, 1)
            key_sum[h] += contract(q[:HD], grads, 1, 1)
            query_back = contract(qkv[heads + h], grads, 1, 0) * SCALE
            out[h, :, here] = turn_back(query_back, here).astype(BF16)
        return 0

    lax.fori_loop(0, length // size, step, 0)

    def finish(i, _):
        here = block_at(i, size)
        for h in range(heads):
            out[heads + h, :, here] = turn_back(key_sum[h, :, here] * SCALE, here).astype(BF16)
            out[2 * heads + h, :, here] = value_sum[h, :, here].astype(BF16)
        return 0

    lax.fori_loop(0, length // size, finish, 0)


def attention_backward(heads, qkv, bias, log_total, mixed_t, back_t, cosine, sine):
    length = qkv.shape[2]
    vmem = pl.BlockSpec(memory_space=pltpu.VMEM)
    return pl.pallas_call(
        functools.partial(attention_backward_kernel, heads),
        out_shape=jax.ShapeDtypeStruct((3 * heads, HD, length), BF16),
        in_specs=[vmem] * 7,
        out_specs=vmem,
        scratch_shapes=[
            pltpu.VMEM((heads, AUG, length), BF16),
            pltpu.VMEM((heads, length, AUG), BF16),
            pltpu.VMEM((heads, length, AUG), BF16),
            pltpu.VMEM((heads, AUG, length), BF16),
            pltpu.VMEM((heads, HD, length), F32),
            pltpu.VMEM((heads, HD, length), F32),
        ],
        compiler_params=pltpu.CompilerParams(vmem_limit_bytes=VMEM_LIMIT),
    )(qkv, bias, log_total, mixed_t, back_t, cosine, sine)


def shards(
    tokens,
    condition,
    lengths,
    condition_weight,
    condition_bias,
    attention_in,
    attention_out,
    up_weight,
    up_bias,
    down_weight,
    down_bias,
    cotangent,
):
    columns = lax.axis_size("col")
    column_index = lax.axis_index("col")
    rows = tokens.shape[1]
    width = tokens.shape[2]
    length_all = rows * columns
    local_width = attention_in.shape[2]
    heads = local_width // HD
    group = ("dp", "row")
    in_full, out_full, up_full, down_full = (
        lax.all_gather(attention_in.astype(BF16), group, axis=0, tiled=True),
        lax.all_gather(attention_out.astype(BF16), group, axis=1, tiled=True),
        lax.all_gather(up_weight.astype(BF16), group, axis=0, tiled=True),
        lax.all_gather(down_weight.astype(BF16), group, axis=1, tiled=True),
    )
    condition_low = condition.astype(BF16)
    condition_all = lax.all_gather(condition_low, group, axis=0, tiled=True)
    weight_low = condition_weight.astype(BF16)
    pieces = jnp.dot(condition_all, weight_low, preferred_element_type=F32)
    modulation = lax.all_to_all(pieces, group, 0, 0, tiled=True).reshape(-1) + condition_bias
    parts = modulation.reshape(6, width)
    own_rows = tokens[0]
    length = lengths[0]
    position = column_index * rows + jnp.arange(rows)
    valid = (position < length).astype(F32)
    bias = jnp.where(jnp.arange(length_all) < length, 0.0, MASKED).astype(F32)[None]
    cosine, sine = (jnp.asarray(table) for table in rotary_tables(length_all))
    normed, first_pull = jax.vjp(norm_shift, own_rows, parts[0], parts[1])
    normed_all = lax.all_gather(normed.astype(BF16), "col", axis=0, tiled=True)
    qkv, mixed_t, log_total = attention_forward(
        heads, normed_all, in_full.reshape(width, 3 * local_width), cosine, sine, bias
    )
    mixed_rows = mixed_t.reshape(local_width, length_all)
    attention = lax.psum_scatter(
        jnp.einsum("cs,cd->sd", mixed_rows, out_full, preferred_element_type=F32).astype(BF16),
        "col",
        scatter_dimension=0,
        tiled=True,
    ).astype(F32)
    middle = own_rows + parts[2] * attention
    second, second_pull = jax.vjp(norm_shift, middle, parts[3], parts[4])
    second_low = second.astype(BF16)
    hidden_cols = up_full.shape[1]
    second_all = lax.all_gather(second_low, "col", axis=0, tiled=True)
    bias_part = lax.dynamic_slice_in_dim(up_bias, column_index * hidden_cols, hidden_cols)
    before = jnp.dot(second_all, up_full, preferred_element_type=F32) + bias_part
    hidden, gelu_pull = jax.vjp(gelu_tanh, before)
    hidden_low = hidden.astype(BF16)
    feed = lax.psum_scatter(
        jnp.dot(hidden_low, down_full, preferred_element_type=F32).astype(BF16),
        "col",
        scatter_dimension=0,
        tiled=True,
    ).astype(F32)
    result = middle + parts[5] * (feed + down_bias)
    incoming = cotangent[0] * valid[:, None]
    down_bias_part = jnp.sum(parts[5] * incoming, axis=0)
    gate_feed = jnp.sum(incoming * (feed + down_bias), axis=0)
    feed_back = (parts[5] * incoming).astype(BF16)
    feed_back_all = lax.all_gather(feed_back, "col", axis=0, tiled=True)
    hidden_back = jnp.einsum("sd,fd->sf", feed_back_all, down_full, preferred_element_type=F32)
    down_grad = jnp.einsum("sf,sd->fd", hidden_low, feed_back_all, preferred_element_type=F32)
    before_back = gelu_pull(hidden_back)[0].astype(BF16)
    up_grad = jnp.einsum("sd,sf->df", second_all, before_back, preferred_element_type=F32)
    up_bias_part = jnp.sum(before_back.astype(F32), axis=0)
    second_back = lax.psum_scatter(
        jnp.einsum("sf,df->sd", before_back, up_full, preferred_element_type=F32).astype(BF16),
        "col",
        scatter_dimension=0,
        tiled=True,
    ).astype(F32)
    middle_part, shift_feed, scale_feed = second_pull(second_back)
    middle_back = incoming + middle_part
    gate_attention = jnp.sum(middle_back * attention, axis=0)
    attention_back = (parts[2] * middle_back).astype(BF16)
    attention_back_all = lax.all_gather(attention_back, "col", axis=0, tiled=True)
    out_grad = jnp.einsum("cs,sd->cd", mixed_rows, attention_back_all, preferred_element_type=F32)
    mixed_back = jnp.einsum("sd,cd->cs", attention_back_all, out_full, preferred_element_type=F32)
    projected_back = attention_backward(
        heads,
        qkv,
        bias,
        log_total,
        mixed_t,
        mixed_back.astype(BF16).reshape(heads, HD, length_all),
        cosine,
        sine,
    ).reshape(3, local_width, length_all)
    in_grad = jnp.einsum("sd,tes->dte", normed_all, projected_back, preferred_element_type=F32)
    normed_back = lax.psum_scatter(
        jnp.einsum("tes,dte->sd", projected_back, in_full, preferred_element_type=F32).astype(BF16),
        "col",
        scatter_dimension=0,
        tiled=True,
    ).astype(F32)
    rows_part, shift_attention, scale_attention = first_pull(normed_back)
    tokens_back = middle_back + rows_part
    modulation_part = jnp.concatenate(
        [shift_attention, scale_attention, gate_attention, shift_feed, scale_feed, gate_feed]
    )
    modulation_back, down_bias_column = lax.psum((modulation_part, down_bias_part), "col")
    count = lax.axis_size(group)
    spread = modulation_back.reshape(count, -1)
    mine = lax.all_to_all(spread, group, 0, 0, tiled=True)
    highest = lax.Precision.HIGHEST
    condition_grad = jnp.einsum("bc,bm->cm", condition_all.astype(F32), mine, precision=highest)
    condition_back = lax.psum_scatter(
        jnp.einsum("bm,cm->bc", mine, weight_low.astype(F32), precision=highest),
        group,
        scatter_dimension=0,
        tiled=True,
    )
    in_grad, out_grad, up_grad, down_grad = (
        lax.psum_scatter(in_grad.astype(BF16), group, scatter_dimension=0, tiled=True).astype(F32),
        lax.psum_scatter(out_grad.astype(BF16), group, scatter_dimension=1, tiled=True).astype(F32),
        lax.psum_scatter(up_grad.astype(BF16), group, scatter_dimension=0, tiled=True).astype(F32),
        lax.psum_scatter(down_grad.astype(BF16), group, scatter_dimension=1, tiled=True).astype(F32),
    )
    bias_grad, up_bias_grad, down_bias_grad = lax.psum(
        (modulation_back, up_bias_part, down_bias_column), group
    )
    return (
        result[None],
        tokens_back[None],
        condition_back,
        condition_grad,
        bias_grad,
        in_grad,
        out_grad,
        up_grad,
        up_bias_grad,
        down_grad,
        down_bias_grad,
    )


def solution(mesh):
    in_specs = (
        P(("dp", "row"), "col", None),
        P(("dp", "row"), None),
        P(("dp", "row")),
        P(None, ("dp", "row")),
        P(),
        P(("dp", "row"), None, "col"),
        P("col", ("dp", "row")),
        P(("dp", "row"), "col"),
        P(),
        P("col", ("dp", "row")),
        P(),
        P(("dp", "row"), "col", None),
    )
    out_specs = (
        P(("dp", "row"), "col", None),
        P(("dp", "row"), "col", None),
        P(("dp", "row"), None),
        P(None, ("dp", "row")),
        P(),
        P(("dp", "row"), None, "col"),
        P("col", ("dp", "row")),
        P(("dp", "row"), "col"),
        P("col"),
        P("col", ("dp", "row")),
        P(),
    )
    return jax.shard_map(shards, mesh=mesh, in_specs=in_specs, out_specs=out_specs, check_vma=False)
```

```python
import functools
import math

import jax
import jax.numpy as jnp
import numpy as np
from jax import lax
from jax.experimental import pallas as pl
from jax.experimental.pallas import tpu as pltpu
from jax.sharding import PartitionSpec as P

HD = 64
AUG = 128
EPSILON = 1e-06
MASKED = -1e30
CUBIC = 0.044715
SLOPE = math.sqrt(2.0 / math.pi)
SCALE = 1.0 / math.sqrt(HD)
UNIT = SCALE * math.log2(math.e)
F32 = jnp.float32
BF16 = jnp.bfloat16
VMEM_LIMIT = 60 << 20


def layer_norm(values):
    center = values - jnp.mean(values, axis=-1, keepdims=True)
    spread = jnp.mean(center * center, axis=-1, keepdims=True)
    return center * lax.rsqrt(spread + EPSILON)


def norm_shift(values, shift, scale):
    return layer_norm(values) * (1.0 + scale) + shift


def gelu_tanh(values):
    return 0.5 * values * (1.0 + jnp.tanh(SLOPE * (values + CUBIC * values * values * values)))


def rotary_tables(length):
    half = HD // 2
    exponent = np.arange(half, dtype=np.float32) * np.float32(2.0 / HD)
    frequency = np.exp(np.float32(-math.log(10000.0)) * exponent).astype(np.float32)
    angle = frequency[:, None] * np.arange(length, dtype=np.float32)[None, :]
    angle = angle.astype(np.float32).astype(np.float64)
    return np.cos(angle).astype(np.float32), np.sin(angle).astype(np.float32)


def contract(left, right, left_axis, right_axis):
    return lax.dot_general(
        left,
        right,
        (((left_axis,), (right_axis,)), ((), ())),
        preferred_element_type=F32,
    )


def block_at(index, size):
    return pl.ds(pl.multiple_of(index * size, size), size)


def split_three(values):
    high = values.astype(BF16)
    rest = values - high.astype(F32)
    middle = rest.astype(BF16)
    low = (rest - middle.astype(F32)).astype(BF16)
    return high.astype(F32), middle.astype(F32), low.astype(F32)


def augment(rows, extras):
    n = rows.shape[1]
    extras = [jnp.broadcast_to(e, (1, n)) for e in extras]
    pad = jnp.zeros((AUG - HD - len(extras), n), F32)
    return jnp.concatenate([rows] + extras + [pad], axis=0)


def attend_block(heads, here, query, key, value_t, mixed_t, log_total):
    scores = [contract(key[h], query[h, :, here], 1, 0) for h in range(heads)]
    for h in range(heads):
        top = jnp.max(scores[h], axis=0, keepdims=True)
        weights = jnp.exp2((scores[h] - top) * UNIT)
        total = jnp.sum(weights, axis=0, keepdims=True)
        out = contract(value_t[h], weights.astype(BF16), 1, 0) * (1.0 / total)
        mixed_t[h, :, here] = out.astype(BF16)
        log_total[h, :, here] = top * UNIT + jnp.log2(total)


def prepare_backward(heads, h, size, length, qkv, bias, log_total, mixed_t, back_t, query, key, value, back):
    def step(i, _):
        here = block_at(i, size)
        one = jnp.ones((1, size), F32)
        zero = jnp.zeros((1, size), F32)
        logs = split_three(log_total[h, :, here] * (-1.0 / UNIT))
        query[h, :, here] = augment(qkv[h, :, here].astype(F32), [one, *logs]).astype(BF16)
        keys = augment(qkv[heads + h, :, here].astype(F32), [bias[:, here], one, one, one])
        key[h, here, :] = keys.T.astype(BF16)
        values = augment(qkv[2 * heads + h, :, here].astype(F32), [zero, one, one, one])
        value[h, here, :] = values.T.astype(BF16)
        grad = back_t[h, :, here].astype(F32)
        center = jnp.sum(grad * mixed_t[h, :, here].astype(F32), axis=0, keepdims=True)
        back[h, :, here] = augment(grad, [zero, *split_three(-center)]).astype(BF16)
        return 0

    lax.fori_loop(0, length // size, step, 0)


def attention_backward_kernel(
    heads, qkv, bias, log_total, mixed_t, back_t, cosine, sine, out, query, key, value, back, key_sum, value_sum
):
    length = qkv.shape[2]
    size = min(512, length)
    half = HD // 2

    def turn_back(rows, here):
        c, s = cosine[:, here], sine[:, here]
        a, b = rows[:half], rows[half:]
        return jnp.concatenate([a * c + b * s, b * c - a * s], axis=0)

    for h in range(heads):
        prepare_backward(heads, h, size, length, qkv, bias, log_total, mixed_t, back_t, query, key, value, back)
    key_sum[...] = jnp.zeros_like(key_sum)
    value_sum[...] = jnp.zeros_like(value_sum)

    def step(i, _):
        here = block_at(i, size)
        for h in range(heads):
            q, d = query[h, :, here], back[h, :, here]
            weights = jnp.exp2(contract(key[h], q, 1, 0) * UNIT)
            grads = (weights * contract(value[h], d, 1, 0)).astype(BF16)
            value_sum[h] += contract(d[:HD], weights.astype(BF16), 1, 1)
            key_sum[h] += contract(q[:HD], grads, 1, 1)
            query_back = contract(qkv[heads + h], grads, 1, 0) * SCALE
            out[h, :, here] = turn_back(query_back, here).astype(BF16)
        return 0

    lax.fori_loop(0, length // size, step, 0)

    def finish(i, _):
        here = block_at(i, size)
        for h in range(heads):
            out[heads + h, :, here] = turn_back(key_sum[h, :, here] * SCALE, here).astype(BF16)
            out[2 * heads + h, :, here] = value_sum[h, :, here].astype(BF16)
        return 0

    lax.fori_loop(0, length // size, finish, 0)


def attention_backward(heads, qkv, bias, log_total, mixed_t, back_t, cosine, sine):
    length = qkv.shape[2]
    vmem = pl.BlockSpec(memory_space=pltpu.VMEM)
    return pl.pallas_call(
        functools.partial(attention_backward_kernel, heads),
        out_shape=jax.ShapeDtypeStruct((3 * heads, HD, length), BF16),
        in_specs=[vmem] * 7,
        out_specs=vmem,
        scratch_shapes=[
            pltpu.VMEM((heads, AUG, length), BF16),
            pltpu.VMEM((heads, length, AUG), BF16),
            pltpu.VMEM((heads, length, AUG), BF16),
            pltpu.VMEM((heads, AUG, length), BF16),
            pltpu.VMEM((heads, HD, length), F32),
            pltpu.VMEM((heads, HD, length), F32),
        ],
        compiler_params=pltpu.CompilerParams(vmem_limit_bytes=VMEM_LIMIT),
    )(qkv, bias, log_total, mixed_t, back_t, cosine, sine)


MESH = pl.DeviceIdType.MESH


def flip(index, bit):
    return index + bit - 2 * bit * lax.rem(lax.div(index, bit), 2)


def flips(index, bits):
    for bit in bits:
        index = flip(index, bit)
    return index


def doubling(sizes):
    steps = []
    for axis, stride in (("dp", sizes["row"]), ("row", 1)):
        bit = sizes[axis] // 2
        while bit:
            steps.append((axis, bit, bit * stride))
            bit //= 2
    return steps


def subsets(bits):
    out = [()]
    for bit in bits:
        out = out + [kept + (bit,) for kept in out]
    return out


def send_copy(source, target, send, receive, peer):
    return pltpu.make_async_remote_copy(
        src_ref=source, dst_ref=target, send_sem=send, recv_sem=receive, device_id=peer, device_id_type=MESH
    )


def greet(peers):
    barrier = pltpu.get_barrier_semaphore()
    for peer in peers:
        pl.semaphore_signal(barrier, inc=1, device_id=peer, device_id_type=MESH)
    pl.semaphore_wait(barrier, len(peers))


def shard_number(sizes):
    return lax.axis_index("dp") * sizes["row"] + lax.axis_index("row")


def doubling_peers(sizes):
    return [{axis: flip(lax.axis_index(axis), bit)} for axis, bit, _ in doubling(sizes)]


def col_peers():
    me = lax.axis_index("col")
    return [{"col": flip(me, 1)}, {"col": flip(me, 2)}]


class ShardGather:
    def __init__(self, sizes, shard, full, sems):
        self.steps = doubling(sizes)
        self.rows = shard.shape[0]
        self.shard, self.full, self.sems = shard, full, sems
        self.me = shard_number(sizes)

    def slot(self, number):
        return self.full.at[pl.ds(pl.multiple_of(number * self.rows, self.rows), self.rows), :]

    def copies(self, k, arriving):
        axis, bit, stride = self.steps[k]
        peer = {axis: flip(lax.axis_index(axis), bit)}
        out = []
        for i, kept in enumerate(subsets([s[2] for s in self.steps[:k]])):
            number = flips(self.me, kept + ((stride,) if arriving else ()))
            source = self.slot(number)
            if not arriving and not kept:
                source = self.shard
            at = 2**k - 1 + i
            out.append(send_copy(source, self.slot(number), self.sems.at[0, at], self.sems.at[1, at], peer))
        return out

    def keep(self):
        self.slot(self.me)[...] = self.shard[...]

    def start(self, k):
        for copy in self.copies(k, False):
            copy.start()

    def arrived(self, k):
        for copy in self.copies(k, True):
            copy.wait_recv()

    def advance(self, k):
        if 0 < k <= len(self.steps):
            self.arrived(k - 1)
        if k < len(self.steps):
            self.start(k)

    def close(self):
        for k in range(len(self.steps)):
            for copy in self.copies(k, False):
                copy.wait_send()

    @staticmethod
    def semaphores(count):
        return pltpu.SemaphoreType.DMA((2, count - 1))


class ShardScatter:
    def __init__(self, sizes, total, out_buf, in_buf, sems):
        self.steps = doubling(sizes)[::-1]
        self.rows = out_buf.shape[1]
        self.total, self.out_buf, self.in_buf, self.sems = total, out_buf, in_buf, sems
        self.me = shard_number(sizes)
        self.first = [0]
        for k in range(len(self.steps)):
            self.first.append(self.first[-1] + 2 ** (len(self.steps) - 1 - k))

    def part(self, number):
        return pl.ds(pl.multiple_of(number * self.rows, self.rows), self.rows)

    def rest(self, k):
        return subsets([s[2] for s in self.steps[k + 1 :]])

    def copy(self, k, i):
        axis, bit, _ = self.steps[k]
        at = self.first[k] + i
        peer = {axis: flip(lax.axis_index(axis), bit)}
        return send_copy(self.out_buf.at[at], self.in_buf.at[at], self.sems.at[0, at], self.sems.at[1, at], peer)

    def start(self, k):
        stride = self.steps[k][2]
        for i, kept in enumerate(self.rest(k)):
            number = flips(self.me, (stride,) + kept)
            self.out_buf[self.first[k] + i] = self.total[self.part(number), :].astype(BF16)
            copy = self.copy(k, i)
            copy.start()

    def arrived(self, k):
        for i, kept in enumerate(self.rest(k)):
            self.copy(k, i).wait_recv()
            here = self.part(flips(self.me, kept))
            self.total[here, :] = self.total[here, :] + self.in_buf[self.first[k] + i].astype(F32)

    def advance(self, k):
        if 0 < k <= len(self.steps):
            self.arrived(k - 1)
        if k < len(self.steps):
            self.start(k)

    def close(self):
        for k in range(len(self.steps)):
            for i in range(len(self.rest(k))):
                self.copy(k, i).wait_send()

    @staticmethod
    def scratch(count, rows, width):
        return [
            pltpu.VMEM((count - 1, rows, width), BF16),
            pltpu.VMEM((count - 1, rows, width), BF16),
            pltpu.SemaphoreType.DMA((2, count - 1)),
        ]


class ColumnGather:
    def __init__(self, full, chunks, sems):
        self.full, self.chunks, self.sems = full, chunks, sems
        self.me = lax.axis_index("col")
        self.rows = full.shape[1] // chunks

    def chunk(self, slot, j):
        return self.full.at[slot, pl.ds(j * self.rows, self.rows), :]

    def copy(self, kind, j, slot):
        peer = {"col": flip(self.me, 2 if kind == 1 else 1)}
        here = self.chunk(slot, j)
        return send_copy(here, here, self.sems.at[0, kind, j], self.sems.at[1, kind, j], peer)

    def start(self, j):
        for kind in (1, 0):
            copy = self.copy(kind, j, self.me)
            copy.start()

    def partner(self, j):
        self.copy(0, j, flip(self.me, 1)).wait_recv()

    def across(self, j):
        there = flip(self.me, 2)
        self.copy(1, j, there).wait_recv()
        copy = self.copy(2, j, there)
        copy.start()

    def diagonal(self, j):
        self.copy(2, j, flips(self.me, (1, 2))).wait_recv()

    def close(self):
        for j in range(self.chunks):
            for kind in range(3):
                self.copy(kind, j, self.me).wait_send()

    @staticmethod
    def semaphores(chunks):
        return pltpu.SemaphoreType.DMA((2, 3, chunks))


class ColumnScatter:
    def __init__(self, pair_out, pair_in, far_out, far_in, kept, chunks, sems):
        self.pair_out, self.pair_in, self.far_out, self.far_in = pair_out, pair_in, far_out, far_in
        self.kept, self.chunks, self.sems = kept, chunks, sems
        self.rows = kept.shape[0] // chunks
        me = lax.axis_index("col")
        self.near, self.far = {"col": flip(me, 1)}, {"col": flip(me, 2)}

    def at(self, j):
        return pl.ds(j * self.rows, self.rows)

    def pair(self, which, j):
        return send_copy(
            self.pair_out.at[which, self.at(j), :],
            self.pair_in.at[which, self.at(j), :],
            self.sems.at[0, which, j],
            self.sems.at[1, which, j],
            self.near,
        )

    def cross(self, j):
        return send_copy(
            self.far_out.at[self.at(j), :],
            self.far_in.at[self.at(j), :],
            self.sems.at[0, 2, j],
            self.sems.at[1, 2, j],
            self.far,
        )

    def begin(self, copy):
        copy.start()

    def give_diagonal(self, j, value):
        self.pair_out[1, self.at(j), :] = value.astype(BF16)
        self.begin(self.pair(1, j))

    def give_across(self, j, value):
        self.pair(1, j).wait_recv()
        self.far_out[self.at(j), :] = (value + self.pair_in[1, self.at(j), :].astype(F32)).astype(BF16)
        self.begin(self.cross(j))

    def give_partner(self, j, value):
        self.pair_out[0, self.at(j), :] = value.astype(BF16)
        self.begin(self.pair(0, j))

    def give_own(self, j, value):
        self.pair(0, j).wait_recv()
        self.kept[self.at(j), :] = value + self.pair_in[0, self.at(j), :].astype(F32)

    def result(self, j):
        self.cross(j).wait_recv()
        return self.kept[self.at(j), :] + self.far_in[self.at(j), :].astype(F32)

    def close(self):
        for j in range(self.chunks):
            self.pair(0, j).wait_send()
            self.pair(1, j).wait_send()
            self.cross(j).wait_send()

    @staticmethod
    def scratch(rows, width, chunks):
        return [
            pltpu.VMEM((2, rows, width), BF16),
            pltpu.VMEM((2, rows, width), BF16),
            pltpu.VMEM((rows, width), BF16),
            pltpu.VMEM((rows, width), BF16),
            pltpu.VMEM((rows, width), F32),
            pltpu.SemaphoreType.DMA((2, 3, chunks)),
        ]


def other_peers(sizes):
    number = shard_number(sizes)
    total = sizes["dp"] * sizes["row"]
    bits = [stride for _, _, stride in doubling(sizes)]
    out = []
    for kept in subsets(bits)[1:]:
        peer = {}
        for axis, bit, stride in doubling(sizes):
            if stride in kept:
                peer[axis] = flip(peer.get(axis, lax.axis_index(axis)), bit)
        out.append((flips(number, kept), peer))
    assert len(out) == total - 1
    return out


def start_kernel(
    sizes, heads, chunks,
    condition, condition_weight, condition_bias, tokens, in_shard, out_shard, cosine, sine, cotangent, valid,
    modulation, normed, qkv, out_full, feed_back, bias_part,
    condition_all, pieces, arrived, in_full, out_t, in_t, unit, sems_tiny, sems_in, sems_out, sems_col,
):
    count = sizes["dp"] * sizes["row"]
    number = shard_number(sizes)
    rows, width = tokens.shape
    others = other_peers(sizes)
    greet([peer for _, peer in others] + col_peers())
    gather_in = ShardGather(sizes, in_shard, in_full, sems_in)
    gather_out = ShardGather(sizes, out_shard, out_t, sems_out)
    gather_col = ColumnGather(normed, chunks, sems_col)

    def condition_copy(i, slot):
        return send_copy(
            condition, condition_all.at[slot], sems_tiny.at[0, i], sems_tiny.at[1, i], others[i][1]
        )

    def piece_copy(i, mine, slot):
        return send_copy(
            pieces.at[mine], arrived.at[slot], sems_tiny.at[2, i], sems_tiny.at[3, i], others[i][1]
        )

    for i in range(count - 1):
        condition_copy(i, number).start()
    gather_in.start(0)
    gather_out.start(0)
    condition_all[number] = condition[...]
    gather_in.keep()
    gather_out.keep()
    size = rows // chunks

    def normal(j, _):
        here = block_at(j, size)
        unit[here, :] = layer_norm(tokens[here, :])
        return 0

    lax.fori_loop(0, chunks, normal, 0)
    for i in range(count - 1):
        condition_copy(i, others[i][0]).wait_recv()
    stacked = jnp.concatenate([condition_all[b] for b in range(count)], axis=0)
    product = contract(stacked.astype(BF16), condition_weight[...], 1, 0)
    for b in range(count):
        pieces[b] = product[b : b + 1]
    for i in range(count - 1):
        piece_copy(i, others[i][0], number).start()
    arrived[number] = pieces[number]
    gather_in.advance(1)
    gather_out.advance(1)
    for i in range(count - 1):
        piece_copy(i, number, others[i][0]).wait_recv()
    line = jnp.concatenate([arrived[b] for b in range(count)], axis=1) + condition_bias[...]
    parts = [line[:, t * width : (t + 1) * width] for t in range(6)]
    for t in range(6):
        modulation[t : t + 1, :] = parts[t]
    for j in range(chunks):
        here = pl.ds(j * size, size)
        value = unit[here, :] * (1.0 + parts[1]) + parts[0]
        normed[gather_col.me, here, :] = value.astype(BF16)
        gather_col.start(j)
    gather_in.advance(2)
    gather_out.advance(2)
    total = jnp.zeros((1, width), F32)
    for j in range(chunks):
        here = pl.ds(j * size, size)
        value = parts[5] * (cotangent[here, :] * valid[here, :])
        feed_back[here, :] = value.astype(BF16)
        total = total + jnp.sum(value, axis=0, keepdims=True)
    bias_part[...] = total
    steps = len(gather_in.steps)
    for k in range(3, steps + 1):
        gather_in.advance(k)
        gather_out.advance(k)
    in_t[...] = in_full[...].astype(F32).T.astype(BF16)
    out_full[...] = out_t[...].astype(F32).T.astype(BF16)

    def project(slot):
        here = pl.ds(pl.multiple_of(slot * rows, rows), rows)
        both = contract(in_t[...], normed[slot], 1, 1)
        half = HD // 2
        c, s = cosine[:, here], sine[:, here]
        for h in range(heads):
            for t in range(3):
                at = (t * heads + h) * HD
                a, b = both[at : at + half], both[at + half : at + HD]
                if t < 2:
                    a, b = a * c - b * s, b * c + a * s
                qkv[t * heads + h, :, here] = jnp.concatenate([a, b], axis=0).astype(BF16)

    me = gather_col.me
    far = flip(me, 2)

    def steps_of(i, _):
        @pl.when(i == 1)
        def _():
            for j in range(chunks):
                gather_col.partner(j)

        @pl.when(i == 2)
        def _():
            for j in range(chunks):
                gather_col.across(j)

        @pl.when(i == 3)
        def _():
            for j in range(chunks):
                gather_col.diagonal(j)

        project(flip_by(me, i))
        return 0

    lax.fori_loop(0, 4, steps_of, 0)
    for i in range(count - 1):
        condition_copy(i, number).wait_send()
        piece_copy(i, others[i][0], number).wait_send()
    gather_in.close()
    gather_out.close()
    gather_col.close()


def flip_by(index, pattern):
    out = 0
    for bit in (1, 2):
        a, b = lax.rem(lax.div(index, bit), 2), lax.rem(lax.div(pattern, bit), 2)
        out = out + bit * (a + b - 2 * a * b)
    return out


def start(sizes, heads, condition, condition_weight, condition_bias, tokens, in_shard, out_shard, cosine, sine, cotangent, valid):
    count = sizes["dp"] * sizes["row"]
    rows, width = tokens.shape
    length = cosine.shape[1]
    chunks = 2
    vmem = pl.BlockSpec(memory_space=pltpu.VMEM)
    piece = condition_weight.shape[1]
    local = heads * HD
    return pl.pallas_call(
        functools.partial(start_kernel, sizes, heads, chunks),
        out_shape=[
            jax.ShapeDtypeStruct((6, width), F32),
            jax.ShapeDtypeStruct((4, rows, width), BF16),
            jax.ShapeDtypeStruct((3 * heads, HD, length), BF16),
            jax.ShapeDtypeStruct((local, width), BF16),
            jax.ShapeDtypeStruct((rows, width), BF16),
            jax.ShapeDtypeStruct((1, width), F32),
        ],
        in_specs=[vmem] * 10,
        out_specs=[vmem] * 6,
        scratch_shapes=[
            pltpu.VMEM((count,) + condition.shape, F32),
            pltpu.VMEM((count, 1, piece), F32),
            pltpu.VMEM((count, 1, piece), F32),
            pltpu.VMEM((width, 3 * local), BF16),
            pltpu.VMEM((width, local), BF16),
            pltpu.VMEM((3 * local, width), BF16),
            pltpu.VMEM((rows, width), F32),
            pltpu.SemaphoreType.DMA((4, count - 1)),
            ShardGather.semaphores(count),
            ShardGather.semaphores(count),
            ColumnGather.semaphores(chunks),
        ],
        compiler_params=pltpu.CompilerParams(
            vmem_limit_bytes=VMEM_LIMIT, collective_id=0, has_side_effects=True
        ),
    )(condition, condition_weight, condition_bias, tokens, in_shard, out_shard, cosine, sine, cotangent, valid)


def attention_kernel(
    sizes, heads, chunks,
    qkv, bias, out_full, feed_back, up_shard, down_shard,
    attention, mixed_t, log_total, feed_back_all, up_full, down_t,
    query, key, pair_out, pair_in, far_out, far_in, kept, sems_scatter, sems_col, sems_up, sems_down,
):
    rows = feed_back.shape[0]
    length = qkv.shape[2]
    greet(doubling_peers(sizes) + col_peers())
    gather_up = ShardGather(sizes, up_shard, up_full, sems_up)
    gather_down = ShardGather(sizes, down_shard, down_t, sems_down)
    gather_col = ColumnGather(feed_back_all, chunks, sems_col)
    scatter = ColumnScatter(pair_out, pair_in, far_out, far_in, kept, 1, sems_scatter)
    me = gather_col.me
    gather_up.start(0)
    gather_down.start(0)
    feed_back_all[me] = feed_back[...]
    for j in range(chunks):
        gather_col.start(j)
    gather_up.keep()
    gather_down.keep()

    def prepare(i, _):
        here = block_at(i, rows)
        one = jnp.ones((1, rows), F32)
        for h in range(heads):
            query[h, :, here] = augment(qkv[h, :, here].astype(F32), [one]).astype(BF16)
            keys = augment(qkv[heads + h, :, here].astype(F32), [bias[:, here], one, one, one])
            key[h, here, :] = keys.T.astype(BF16)
        return 0

    lax.fori_loop(0, length // rows, prepare, 0)
    steps = len(gather_up.steps)

    def step(i, _):
        here = block_at(flip_by(me, 3 - i), rows)
        attend_block(heads, here, query, key, qkv.at[pl.ds(2 * heads, heads)], mixed_t, log_total)
        value = contract(mixed_t[:, :, here].reshape(heads * HD, rows), out_full[...], 0, 0)
        for order, give in enumerate(
            (scatter.give_diagonal, scatter.give_across, scatter.give_partner, scatter.give_own)
        ):

            @pl.when(i == order)
            def _():
                give(0, value)
                if order < 3:
                    gather_up.advance(order + 1)
                    gather_down.advance(order + 1)

        return 0

    lax.fori_loop(0, 4, step, 0)
    for k in range(4, steps + 1):
        gather_up.advance(k)
        gather_down.advance(k)
    for j in range(chunks):
        gather_col.across(j)
    for j in range(chunks):
        gather_col.partner(j)
        gather_col.diagonal(j)
    attention[...] = scatter.result(0)
    gather_up.close()
    gather_down.close()
    gather_col.close()
    scatter.close()


def attend(sizes, heads, qkv, bias, out_full, feed_back, up_shard, down_shard):
    count = sizes["dp"] * sizes["row"]
    rows, width = feed_back.shape
    length = qkv.shape[2]
    chunks = 2
    hidden = up_shard.shape[1]
    vmem = pl.BlockSpec(memory_space=pltpu.VMEM)
    return pl.pallas_call(
        functools.partial(attention_kernel, sizes, heads, chunks),
        out_shape=[
            jax.ShapeDtypeStruct((rows, width), F32),
            jax.ShapeDtypeStruct((heads, HD, length), BF16),
            jax.ShapeDtypeStruct((heads, 1, length), F32),
            jax.ShapeDtypeStruct((4, rows, width), BF16),
            jax.ShapeDtypeStruct((width, hidden), BF16),
            jax.ShapeDtypeStruct((width, hidden), BF16),
        ],
        in_specs=[vmem] * 6,
        out_specs=[vmem] * 6,
        scratch_shapes=[
            pltpu.VMEM((heads, AUG, length), BF16),
            pltpu.VMEM((heads, length, AUG), BF16),
            *ColumnScatter.scratch(rows, width, 1),
            ColumnGather.semaphores(chunks),
            ShardGather.semaphores(count),
            ShardGather.semaphores(count),
        ],
        compiler_params=pltpu.CompilerParams(
            vmem_limit_bytes=VMEM_LIMIT, collective_id=1, has_side_effects=True
        ),
    )(qkv, bias, out_full, feed_back, up_shard, down_shard)


def shards(
    sizes,
    tokens,
    condition,
    lengths,
    condition_weight,
    condition_bias,
    attention_in,
    attention_out,
    up_weight,
    up_bias,
    down_weight,
    down_bias,
    cotangent,
):
    columns = lax.axis_size("col")
    column_index = lax.axis_index("col")
    rows = tokens.shape[1]
    width = tokens.shape[2]
    length_all = rows * columns
    local_width = attention_in.shape[2]
    heads = local_width // HD
    group = ("dp", "row")
    in_shard = attention_in.reshape(attention_in.shape[0], 3 * local_width).astype(BF16)
    out_shard = attention_out.T.astype(BF16)
    up_shard = up_weight.astype(BF16)
    down_shard = down_weight.T.astype(BF16)
    condition_low = condition.astype(BF16)
    weight_low = condition_weight.astype(BF16)
    own_rows = tokens[0]
    length = lengths[0]
    position = column_index * rows + jnp.arange(rows)
    valid = (position < length).astype(F32)
    bias = jnp.where(jnp.arange(length_all) < length, 0.0, MASKED).astype(F32)[None]
    cosine, sine = (jnp.asarray(table) for table in rotary_tables(length_all))
    parts, normed_blocks, qkv, out_full, feed_back, down_bias_part = start(
        sizes, heads, condition_low.astype(F32), weight_low, condition_bias[None], own_rows,
        in_shard, out_shard, cosine, sine, cotangent[0], valid[:, None],
    )
    down_bias_part = down_bias_part[0]
    normed_all = normed_blocks.reshape(length_all, width)
    _, first_pull = jax.vjp(norm_shift, own_rows, parts[0], parts[1])
    attention, mixed_t, log_total, feed_back_blocks, up_full, down_t = attend(
        sizes, heads, qkv, bias, out_full, feed_back, up_shard, down_shard
    )
    in_full = lax.all_gather(in_shard, group, axis=0, tiled=True).reshape(width, 3, local_width)
    condition_all = lax.all_gather(condition_low, group, axis=0, tiled=True)
    mixed_rows = mixed_t.reshape(local_width, length_all)
    down_full = down_t.T
    feed_back_all = feed_back_blocks.reshape(length_all, width)
    middle = own_rows + parts[2] * attention
    second, second_pull = jax.vjp(norm_shift, middle, parts[3], parts[4])
    second_low = second.astype(BF16)
    hidden_cols = up_full.shape[1]
    second_all = lax.all_gather(second_low, "col", axis=0, tiled=True)
    bias_part = lax.dynamic_slice_in_dim(up_bias, column_index * hidden_cols, hidden_cols)
    before = jnp.dot(second_all, up_full, preferred_element_type=F32) + bias_part
    hidden, gelu_pull = jax.vjp(gelu_tanh, before)
    hidden_low = hidden.astype(BF16)
    feed = lax.psum_scatter(
        jnp.dot(hidden_low, down_full, preferred_element_type=F32).astype(BF16),
        "col",
        scatter_dimension=0,
        tiled=True,
    ).astype(F32)
    result = middle + parts[5] * (feed + down_bias)
    incoming = cotangent[0] * valid[:, None]
    gate_feed = jnp.sum(incoming * (feed + down_bias), axis=0)
    hidden_back = jnp.einsum("sd,fd->sf", feed_back_all, down_full, preferred_element_type=F32)
    down_grad = jnp.einsum("sf,sd->fd", hidden_low, feed_back_all, preferred_element_type=F32)
    before_back = gelu_pull(hidden_back)[0].astype(BF16)
    up_grad = jnp.einsum("sd,sf->df", second_all, before_back, preferred_element_type=F32)
    up_bias_part = jnp.sum(before_back.astype(F32), axis=0)
    second_back = lax.psum_scatter(
        jnp.einsum("sf,df->sd", before_back, up_full, preferred_element_type=F32).astype(BF16),
        "col",
        scatter_dimension=0,
        tiled=True,
    ).astype(F32)
    middle_part, shift_feed, scale_feed = second_pull(second_back)
    middle_back = incoming + middle_part
    gate_attention = jnp.sum(middle_back * attention, axis=0)
    attention_back = (parts[2] * middle_back).astype(BF16)
    attention_back_all = lax.all_gather(attention_back, "col", axis=0, tiled=True)
    out_grad = jnp.einsum("cs,sd->cd", mixed_rows, attention_back_all, preferred_element_type=F32)
    mixed_back = jnp.einsum("sd,cd->cs", attention_back_all, out_full, preferred_element_type=F32)
    projected_back = attention_backward(
        heads,
        qkv,
        bias,
        log_total,
        mixed_t,
        mixed_back.astype(BF16).reshape(heads, HD, length_all),
        cosine,
        sine,
    ).reshape(3, local_width, length_all)
    in_grad = jnp.einsum("sd,tes->dte", normed_all, projected_back, preferred_element_type=F32)
    normed_back = lax.psum_scatter(
        jnp.einsum("tes,dte->sd", projected_back, in_full, preferred_element_type=F32).astype(BF16),
        "col",
        scatter_dimension=0,
        tiled=True,
    ).astype(F32)
    rows_part, shift_attention, scale_attention = first_pull(normed_back)
    tokens_back = middle_back + rows_part
    modulation_part = jnp.concatenate(
        [shift_attention, scale_attention, gate_attention, shift_feed, scale_feed, gate_feed]
    )
    modulation_back, down_bias_column = lax.psum((modulation_part, down_bias_part), "col")
    count = lax.axis_size(group)
    spread = modulation_back.reshape(count, -1)
    mine = lax.all_to_all(spread, group, 0, 0, tiled=True)
    highest = lax.Precision.HIGHEST
    condition_grad = jnp.einsum("bc,bm->cm", condition_all.astype(F32), mine, precision=highest)
    condition_back = lax.psum_scatter(
        jnp.einsum("bm,cm->bc", mine, weight_low.astype(F32), precision=highest),
        group,
        scatter_dimension=0,
        tiled=True,
    )
    in_grad, out_grad, up_grad, down_grad = (
        lax.psum_scatter(in_grad.astype(BF16), group, scatter_dimension=0, tiled=True).astype(F32),
        lax.psum_scatter(out_grad.astype(BF16), group, scatter_dimension=1, tiled=True).astype(F32),
        lax.psum_scatter(up_grad.astype(BF16), group, scatter_dimension=0, tiled=True).astype(F32),
        lax.psum_scatter(down_grad.astype(BF16), group, scatter_dimension=1, tiled=True).astype(F32),
    )
    bias_grad, up_bias_grad, down_bias_grad = lax.psum(
        (modulation_back, up_bias_part, down_bias_column), group
    )
    return (
        result[None],
        tokens_back[None],
        condition_back,
        condition_grad,
        bias_grad,
        in_grad,
        out_grad,
        up_grad,
        up_bias_grad,
        down_grad,
        down_bias_grad,
    )


def solution(mesh):
    sizes = {axis: mesh.shape[axis] for axis in ("dp", "row", "col")}
    in_specs = (
        P(("dp", "row"), "col", None),
        P(("dp", "row"), None),
        P(("dp", "row")),
        P(None, ("dp", "row")),
        P(),
        P(("dp", "row"), None, "col"),
        P("col", ("dp", "row")),
        P(("dp", "row"), "col"),
        P(),
        P("col", ("dp", "row")),
        P(),
        P(("dp", "row"), "col", None),
    )
    out_specs = (
        P(("dp", "row"), "col", None),
        P(("dp", "row"), "col", None),
        P(("dp", "row"), None),
        P(None, ("dp", "row")),
        P(),
        P(("dp", "row"), None, "col"),
        P("col", ("dp", "row")),
        P(("dp", "row"), "col"),
        P("col"),
        P("col", ("dp", "row")),
        P(),
    )
    return jax.shard_map(functools.partial(shards, sizes), mesh=mesh, in_specs=in_specs, out_specs=out_specs, check_vma=False)
```

```python
import functools
import math

import jax
import jax.numpy as jnp
import numpy as np
from jax import lax
from jax.experimental import pallas as pl
from jax.experimental.pallas import tpu as pltpu
from jax.sharding import PartitionSpec as P

HD = 64
AUG = 128
EPSILON = 1e-06
MASKED = -1e30
CUBIC = 0.044715
SLOPE = math.sqrt(2.0 / math.pi)
SCALE = 1.0 / math.sqrt(HD)
UNIT = SCALE * math.log2(math.e)
F32 = jnp.float32
BF16 = jnp.bfloat16
VMEM_LIMIT = 60 << 20


def layer_norm(values):
    center = values - jnp.mean(values, axis=-1, keepdims=True)
    spread = jnp.mean(center * center, axis=-1, keepdims=True)
    return center * lax.rsqrt(spread + EPSILON)


def norm_shift(values, shift, scale):
    return layer_norm(values) * (1.0 + scale) + shift


def gelu_tanh(values):
    return 0.5 * values * (1.0 + jnp.tanh(SLOPE * (values + CUBIC * values * values * values)))


def rotary_tables(length):
    half = HD // 2
    exponent = np.arange(half, dtype=np.float32) * np.float32(2.0 / HD)
    frequency = np.exp(np.float32(-math.log(10000.0)) * exponent).astype(np.float32)
    angle = frequency[:, None] * np.arange(length, dtype=np.float32)[None, :]
    angle = angle.astype(np.float32).astype(np.float64)
    return np.cos(angle).astype(np.float32), np.sin(angle).astype(np.float32)


def contract(left, right, left_axis, right_axis):
    return lax.dot_general(
        left,
        right,
        (((left_axis,), (right_axis,)), ((), ())),
        preferred_element_type=F32,
    )


def block_at(index, size):
    return pl.ds(pl.multiple_of(index * size, size), size)


def split_three(values):
    high = values.astype(BF16)
    rest = values - high.astype(F32)
    middle = rest.astype(BF16)
    low = (rest - middle.astype(F32)).astype(BF16)
    return high.astype(F32), middle.astype(F32), low.astype(F32)


def augment(rows, extras):
    n = rows.shape[1]
    extras = [jnp.broadcast_to(e, (1, n)) for e in extras]
    pad = jnp.zeros((AUG - HD - len(extras), n), F32)
    return jnp.concatenate([rows] + extras + [pad], axis=0)


def attend_block(heads, here, query, key, value_t, mixed_t, log_total):
    scores = [contract(key[h], query[h, :, here], 1, 0) for h in range(heads)]
    for h in range(heads):
        top = jnp.max(scores[h], axis=0, keepdims=True)
        weights = jnp.exp2((scores[h] - top) * UNIT)
        total = jnp.sum(weights, axis=0, keepdims=True)
        out = contract(value_t[h], weights.astype(BF16), 1, 0) * (1.0 / total)
        mixed_t[h, :, here] = out.astype(BF16)
        log_total[h, :, here] = top * UNIT + jnp.log2(total)


def prepare_backward(heads, h, size, length, qkv, bias, log_total, mixed_t, back_t, query, key, value, back):
    def step(i, _):
        here = block_at(i, size)
        one = jnp.ones((1, size), F32)
        zero = jnp.zeros((1, size), F32)
        logs = split_three(log_total[h, :, here] * (-1.0 / UNIT))
        query[h, :, here] = augment(qkv[h, :, here].astype(F32), [one, *logs]).astype(BF16)
        keys = augment(qkv[heads + h, :, here].astype(F32), [bias[:, here], one, one, one])
        key[h, here, :] = keys.T.astype(BF16)
        values = augment(qkv[2 * heads + h, :, here].astype(F32), [zero, one, one, one])
        value[h, here, :] = values.T.astype(BF16)
        grad = back_t[h, :, here].astype(F32)
        center = jnp.sum(grad * mixed_t[h, :, here].astype(F32), axis=0, keepdims=True)
        back[h, :, here] = augment(grad, [zero, *split_three(-center)]).astype(BF16)
        return 0

    lax.fori_loop(0, length // size, step, 0)


MESH = pl.DeviceIdType.MESH


def flip(index, bit):
    return index + bit - 2 * bit * lax.rem(lax.div(index, bit), 2)


def flips(index, bits):
    for bit in bits:
        index = flip(index, bit)
    return index


def doubling(sizes):
    steps = []
    for axis, stride in (("dp", sizes["row"]), ("row", 1)):
        bit = sizes[axis] // 2
        while bit:
            steps.append((axis, bit, bit * stride))
            bit //= 2
    return steps


def subsets(bits):
    out = [()]
    for bit in bits:
        out = out + [kept + (bit,) for kept in out]
    return out


def send_copy(source, target, send, receive, peer):
    return pltpu.make_async_remote_copy(
        src_ref=source, dst_ref=target, send_sem=send, recv_sem=receive, device_id=peer, device_id_type=MESH
    )


def greet(peers):
    barrier = pltpu.get_barrier_semaphore()
    for peer in peers:
        pl.semaphore_signal(barrier, inc=1, device_id=peer, device_id_type=MESH)
    pl.semaphore_wait(barrier, len(peers))


def shard_number(sizes):
    return lax.axis_index("dp") * sizes["row"] + lax.axis_index("row")


def doubling_peers(sizes):
    return [{axis: flip(lax.axis_index(axis), bit)} for axis, bit, _ in doubling(sizes)]


def col_peers():
    me = lax.axis_index("col")
    return [{"col": flip(me, 1)}, {"col": flip(me, 2)}]


class ShardGather:
    def __init__(self, sizes, shard, full, sems):
        self.steps = doubling(sizes)
        self.rows = shard.shape[0]
        self.shard, self.full, self.sems = shard, full, sems
        self.me = shard_number(sizes)

    def slot(self, number):
        return self.full.at[pl.ds(pl.multiple_of(number * self.rows, self.rows), self.rows), :]

    def copies(self, k, arriving):
        axis, bit, stride = self.steps[k]
        peer = {axis: flip(lax.axis_index(axis), bit)}
        out = []
        for i, kept in enumerate(subsets([s[2] for s in self.steps[:k]])):
            number = flips(self.me, kept + ((stride,) if arriving else ()))
            source = self.slot(number)
            if not arriving and not kept:
                source = self.shard
            at = 2**k - 1 + i
            out.append(send_copy(source, self.slot(number), self.sems.at[0, at], self.sems.at[1, at], peer))
        return out

    def keep(self):
        self.slot(self.me)[...] = self.shard[...]

    def start(self, k):
        for copy in self.copies(k, False):
            copy.start()

    def arrived(self, k):
        for copy in self.copies(k, True):
            copy.wait_recv()

    def advance(self, k):
        if 0 < k <= len(self.steps):
            self.arrived(k - 1)
        if k < len(self.steps):
            self.start(k)

    def close(self):
        for k in range(len(self.steps)):
            for copy in self.copies(k, False):
                copy.wait_send()

    @staticmethod
    def semaphores(count):
        return pltpu.SemaphoreType.DMA((2, count - 1))


class ShardScatter:
    def __init__(self, sizes, source, total, out_buf, in_buf, sems):
        self.steps = doubling(sizes)[::-1]
        self.rows = out_buf.shape[1]
        self.source, self.total, self.out_buf, self.in_buf, self.sems = source, total, out_buf, in_buf, sems
        self.me = shard_number(sizes)
        self.first = [0]
        for k in range(len(self.steps)):
            self.first.append(self.first[-1] + 2 ** (len(self.steps) - 1 - k))

    def part(self, number):
        return pl.ds(pl.multiple_of(number * self.rows, self.rows), self.rows)

    def rest(self, k):
        return subsets([s[2] for s in self.steps[k + 1 :]])

    def copy(self, k, i):
        axis, bit, _ = self.steps[k]
        at = self.first[k] + i
        peer = {axis: flip(lax.axis_index(axis), bit)}
        return send_copy(self.out_buf.at[at], self.in_buf.at[at], self.sems.at[0, at], self.sems.at[1, at], peer)

    def held(self, k):
        return self.source if k == 0 else self.total

    def start(self, k):
        stride = self.steps[k][2]
        for i, kept in enumerate(self.rest(k)):
            number = flips(self.me, (stride,) + kept)
            self.out_buf[self.first[k] + i] = self.held(k)[self.part(number), :].astype(BF16)
            self.copy(k, i).start()

    def arrived(self, k):
        for i, kept in enumerate(self.rest(k)):
            self.copy(k, i).wait_recv()
            here = self.part(flips(self.me, kept))
            self.total[here, :] = self.held(k)[here, :].astype(F32) + self.in_buf[self.first[k] + i].astype(F32)

    def advance(self, k):
        if 0 < k <= len(self.steps):
            self.arrived(k - 1)
        if k < len(self.steps):
            self.start(k)

    def result(self):
        return self.total[self.part(self.me), :]

    def close(self):
        for k in range(len(self.steps)):
            for i in range(len(self.rest(k))):
                self.copy(k, i).wait_send()

    @staticmethod
    def scratch(count, rows, width):
        return [
            pltpu.VMEM((count * rows, width), F32),
            pltpu.VMEM((count - 1, rows, width), BF16),
            pltpu.VMEM((count - 1, rows, width), BF16),
            pltpu.SemaphoreType.DMA((2, count - 1)),
        ]


class ColumnGather:
    def __init__(self, full, chunks, sems):
        self.full, self.chunks, self.sems = full, chunks, sems
        self.me = lax.axis_index("col")
        self.rows = full.shape[1] // chunks

    def chunk(self, slot, j):
        return self.full.at[slot, pl.ds(j * self.rows, self.rows), :]

    def copy(self, kind, j, slot):
        peer = {"col": flip(self.me, 2 if kind == 1 else 1)}
        here = self.chunk(slot, j)
        return send_copy(here, here, self.sems.at[0, kind, j], self.sems.at[1, kind, j], peer)

    def start(self, j):
        for kind in (1, 0):
            copy = self.copy(kind, j, self.me)
            copy.start()

    def partner(self, j):
        self.copy(0, j, flip(self.me, 1)).wait_recv()

    def across(self, j):
        there = flip(self.me, 2)
        self.copy(1, j, there).wait_recv()
        copy = self.copy(2, j, there)
        copy.start()

    def diagonal(self, j):
        self.copy(2, j, flips(self.me, (1, 2))).wait_recv()

    def close(self):
        for j in range(self.chunks):
            for kind in range(3):
                self.copy(kind, j, self.me).wait_send()

    @staticmethod
    def semaphores(chunks):
        return pltpu.SemaphoreType.DMA((2, 3, chunks))


class ColumnScatter:
    def __init__(self, pair_out, pair_in, far_out, far_in, kept, chunks, sems):
        self.pair_out, self.pair_in, self.far_out, self.far_in = pair_out, pair_in, far_out, far_in
        self.kept, self.chunks, self.sems = kept, chunks, sems
        self.rows = kept.shape[0] // chunks
        me = lax.axis_index("col")
        self.near, self.far = {"col": flip(me, 1)}, {"col": flip(me, 2)}

    def at(self, j):
        return pl.ds(j * self.rows, self.rows)

    def pair(self, which, j):
        return send_copy(
            self.pair_out.at[which, self.at(j), :],
            self.pair_in.at[which, self.at(j), :],
            self.sems.at[0, which, j],
            self.sems.at[1, which, j],
            self.near,
        )

    def cross(self, j):
        return send_copy(
            self.far_out.at[self.at(j), :],
            self.far_in.at[self.at(j), :],
            self.sems.at[0, 2, j],
            self.sems.at[1, 2, j],
            self.far,
        )

    def begin(self, copy):
        copy.start()

    def give_diagonal(self, j, value):
        self.pair_out[1, self.at(j), :] = value.astype(BF16)
        self.begin(self.pair(1, j))

    def give_across(self, j, value):
        self.pair(1, j).wait_recv()
        self.far_out[self.at(j), :] = (value + self.pair_in[1, self.at(j), :].astype(F32)).astype(BF16)
        self.begin(self.cross(j))

    def give_partner(self, j, value):
        self.pair_out[0, self.at(j), :] = value.astype(BF16)
        self.begin(self.pair(0, j))

    def give_own(self, j, value):
        self.pair(0, j).wait_recv()
        self.kept[self.at(j), :] = value + self.pair_in[0, self.at(j), :].astype(F32)

    def result(self, j):
        self.cross(j).wait_recv()
        return self.kept[self.at(j), :] + self.far_in[self.at(j), :].astype(F32)

    def close(self):
        for j in range(self.chunks):
            self.pair(0, j).wait_send()
            self.pair(1, j).wait_send()
            self.cross(j).wait_send()

    @staticmethod
    def scratch(rows, width, chunks):
        return [
            pltpu.VMEM((2, rows, width), BF16),
            pltpu.VMEM((2, rows, width), BF16),
            pltpu.VMEM((rows, width), BF16),
            pltpu.VMEM((rows, width), BF16),
            pltpu.VMEM((rows, width), F32),
            pltpu.SemaphoreType.DMA((2, 3, chunks)),
        ]


def other_peers(sizes):
    number = shard_number(sizes)
    total = sizes["dp"] * sizes["row"]
    bits = [stride for _, _, stride in doubling(sizes)]
    out = []
    for kept in subsets(bits)[1:]:
        peer = {}
        for axis, bit, stride in doubling(sizes):
            if stride in kept:
                peer[axis] = flip(peer.get(axis, lax.axis_index(axis)), bit)
        out.append((flips(number, kept), peer))
    assert len(out) == total - 1
    return out


def start_kernel(
    sizes, heads, chunks,
    condition, condition_weight, condition_bias, tokens, in_shard, out_shard, cosine, sine, cotangent, valid,
    modulation, normed, qkv, out_full, feed_back, bias_part, in_t, condition_all,
    pieces, arrived, in_full, out_t, unit, sems_tiny, sems_in, sems_out, sems_col,
):
    count = sizes["dp"] * sizes["row"]
    number = shard_number(sizes)
    rows, width = tokens.shape
    others = other_peers(sizes)
    greet([peer for _, peer in others] + col_peers())
    gather_in = ShardGather(sizes, in_shard, in_full, sems_in)
    gather_out = ShardGather(sizes, out_shard, out_t, sems_out)
    gather_col = ColumnGather(normed, chunks, sems_col)

    def condition_copy(i, slot):
        return send_copy(
            condition, condition_all.at[slot], sems_tiny.at[0, i], sems_tiny.at[1, i], others[i][1]
        )

    def piece_copy(i, mine, slot):
        return send_copy(
            pieces.at[mine], arrived.at[slot], sems_tiny.at[2, i], sems_tiny.at[3, i], others[i][1]
        )

    for i in range(count - 1):
        condition_copy(i, number).start()
    gather_in.start(0)
    gather_out.start(0)
    condition_all[number] = condition[...]
    gather_in.keep()
    gather_out.keep()
    size = rows // chunks

    def normal(j, _):
        here = block_at(j, size)
        unit[here, :] = layer_norm(tokens[here, :])
        return 0

    lax.fori_loop(0, chunks, normal, 0)
    for i in range(count - 1):
        condition_copy(i, others[i][0]).wait_recv()
    stacked = jnp.concatenate([condition_all[b] for b in range(count)], axis=0)
    product = contract(stacked.astype(BF16), condition_weight[...], 1, 0)
    for b in range(count):
        pieces[b] = product[b : b + 1]
    for i in range(count - 1):
        piece_copy(i, others[i][0], number).start()
    arrived[number] = pieces[number]
    gather_in.advance(1)
    gather_out.advance(1)
    for i in range(count - 1):
        piece_copy(i, number, others[i][0]).wait_recv()
    line = jnp.concatenate([arrived[b] for b in range(count)], axis=1) + condition_bias[...]
    parts = [line[:, t * width : (t + 1) * width] for t in range(6)]
    for t in range(6):
        modulation[t : t + 1, :] = parts[t]
    for j in range(chunks):
        here = pl.ds(j * size, size)
        value = unit[here, :] * (1.0 + parts[1]) + parts[0]
        normed[gather_col.me, here, :] = value.astype(BF16)
        gather_col.start(j)
    gather_in.advance(2)
    gather_out.advance(2)
    total = jnp.zeros((1, width), F32)
    for j in range(chunks):
        here = pl.ds(j * size, size)
        value = parts[5] * (cotangent[here, :] * valid[here, :])
        feed_back[here, :] = value.astype(BF16)
        total = total + jnp.sum(value, axis=0, keepdims=True)
    bias_part[...] = total
    steps = len(gather_in.steps)
    for k in range(3, steps + 1):
        gather_in.advance(k)
        gather_out.advance(k)
    in_t[...] = in_full[...].astype(F32).T.astype(BF16)
    out_full[...] = out_t[...].astype(F32).T.astype(BF16)

    def project(slot):
        here = pl.ds(pl.multiple_of(slot * rows, rows), rows)
        both = contract(in_t[...], normed[slot], 1, 1)
        half = HD // 2
        c, s = cosine[:, here], sine[:, here]
        for h in range(heads):
            for t in range(3):
                at = (t * heads + h) * HD
                a, b = both[at : at + half], both[at + half : at + HD]
                if t < 2:
                    a, b = a * c - b * s, b * c + a * s
                qkv[t * heads + h, :, here] = jnp.concatenate([a, b], axis=0).astype(BF16)

    me = gather_col.me
    far = flip(me, 2)

    def steps_of(i, _):
        @pl.when(i == 1)
        def _():
            for j in range(chunks):
                gather_col.partner(j)

        @pl.when(i == 2)
        def _():
            for j in range(chunks):
                gather_col.across(j)

        @pl.when(i == 3)
        def _():
            for j in range(chunks):
                gather_col.diagonal(j)

        project(flip_by(me, i))
        return 0

    lax.fori_loop(0, 4, steps_of, 0)
    for i in range(count - 1):
        condition_copy(i, number).wait_send()
        piece_copy(i, others[i][0], number).wait_send()
    gather_in.close()
    gather_out.close()
    gather_col.close()


def flip_by(index, pattern):
    out = 0
    for bit in (1, 2):
        a, b = lax.rem(lax.div(index, bit), 2), lax.rem(lax.div(pattern, bit), 2)
        out = out + bit * (a + b - 2 * a * b)
    return out


def start(sizes, heads, condition, condition_weight, condition_bias, tokens, in_shard, out_shard, cosine, sine, cotangent, valid):
    count = sizes["dp"] * sizes["row"]
    rows, width = tokens.shape
    length = cosine.shape[1]
    chunks = 2
    vmem = pl.BlockSpec(memory_space=pltpu.VMEM)
    piece = condition_weight.shape[1]
    local = heads * HD
    return pl.pallas_call(
        functools.partial(start_kernel, sizes, heads, chunks),
        out_shape=[
            jax.ShapeDtypeStruct((6, width), F32),
            jax.ShapeDtypeStruct((4, rows, width), BF16),
            jax.ShapeDtypeStruct((3 * heads, HD, length), BF16),
            jax.ShapeDtypeStruct((local, width), BF16),
            jax.ShapeDtypeStruct((rows, width), BF16),
            jax.ShapeDtypeStruct((1, width), F32),
            jax.ShapeDtypeStruct((3 * local, width), BF16),
            jax.ShapeDtypeStruct((count,) + condition.shape, F32),
        ],
        in_specs=[vmem] * 10,
        out_specs=[vmem] * 8,
        scratch_shapes=[
            pltpu.VMEM((count, 1, piece), F32),
            pltpu.VMEM((count, 1, piece), F32),
            pltpu.VMEM((width, 3 * local), BF16),
            pltpu.VMEM((width, local), BF16),
            pltpu.VMEM((rows, width), F32),
            pltpu.SemaphoreType.DMA((4, count - 1)),
            ShardGather.semaphores(count),
            ShardGather.semaphores(count),
            ColumnGather.semaphores(chunks),
        ],
        compiler_params=pltpu.CompilerParams(
            vmem_limit_bytes=VMEM_LIMIT, collective_id=0, has_side_effects=True
        ),
    )(condition, condition_weight, condition_bias, tokens, in_shard, out_shard, cosine, sine, cotangent, valid)


def attention_kernel(
    sizes, heads, chunks,
    qkv, bias, out_full, feed_back, up_shard, down_shard,
    attention, mixed_t, log_total, feed_back_all, up_full, down_t,
    query, key, pair_out, pair_in, far_out, far_in, kept, sems_scatter, sems_col, sems_up, sems_down,
):
    rows = feed_back.shape[0]
    length = qkv.shape[2]
    greet(doubling_peers(sizes) + col_peers())
    gather_up = ShardGather(sizes, up_shard, up_full, sems_up)
    gather_down = ShardGather(sizes, down_shard, down_t, sems_down)
    gather_col = ColumnGather(feed_back_all, chunks, sems_col)
    scatter = ColumnScatter(pair_out, pair_in, far_out, far_in, kept, 1, sems_scatter)
    me = gather_col.me
    gather_up.start(0)
    gather_down.start(0)
    feed_back_all[me] = feed_back[...]
    for j in range(chunks):
        gather_col.start(j)
    gather_up.keep()
    gather_down.keep()

    def prepare(i, _):
        here = block_at(i, rows)
        one = jnp.ones((1, rows), F32)
        for h in range(heads):
            query[h, :, here] = augment(qkv[h, :, here].astype(F32), [one]).astype(BF16)
            keys = augment(qkv[heads + h, :, here].astype(F32), [bias[:, here], one, one, one])
            key[h, here, :] = keys.T.astype(BF16)
        return 0

    lax.fori_loop(0, length // rows, prepare, 0)
    steps = len(gather_up.steps)

    def step(i, _):
        here = block_at(flip_by(me, 3 - i), rows)
        attend_block(heads, here, query, key, qkv.at[pl.ds(2 * heads, heads)], mixed_t, log_total)
        value = contract(mixed_t[:, :, here].reshape(heads * HD, rows), out_full[...], 0, 0)
        for order, give in enumerate(
            (scatter.give_diagonal, scatter.give_across, scatter.give_partner, scatter.give_own)
        ):

            @pl.when(i == order)
            def _():
                give(0, value)
                if order < 3:
                    gather_up.advance(order + 1)
                    gather_down.advance(order + 1)

        return 0

    lax.fori_loop(0, 4, step, 0)
    for k in range(4, steps + 1):
        gather_up.advance(k)
        gather_down.advance(k)
    for j in range(chunks):
        gather_col.across(j)
    for j in range(chunks):
        gather_col.partner(j)
        gather_col.diagonal(j)
    attention[...] = scatter.result(0)
    gather_up.close()
    gather_down.close()
    gather_col.close()
    scatter.close()


def attend(sizes, heads, qkv, bias, out_full, feed_back, up_shard, down_shard):
    count = sizes["dp"] * sizes["row"]
    rows, width = feed_back.shape
    length = qkv.shape[2]
    chunks = 2
    hidden = up_shard.shape[1]
    vmem = pl.BlockSpec(memory_space=pltpu.VMEM)
    return pl.pallas_call(
        functools.partial(attention_kernel, sizes, heads, chunks),
        out_shape=[
            jax.ShapeDtypeStruct((rows, width), F32),
            jax.ShapeDtypeStruct((heads, HD, length), BF16),
            jax.ShapeDtypeStruct((heads, 1, length), F32),
            jax.ShapeDtypeStruct((4, rows, width), BF16),
            jax.ShapeDtypeStruct((width, hidden), BF16),
            jax.ShapeDtypeStruct((width, hidden), BF16),
        ],
        in_specs=[vmem] * 6,
        out_specs=[vmem] * 6,
        scratch_shapes=[
            pltpu.VMEM((heads, AUG, length), BF16),
            pltpu.VMEM((heads, length, AUG), BF16),
            *ColumnScatter.scratch(rows, width, 1),
            ColumnGather.semaphores(chunks),
            ShardGather.semaphores(count),
            ShardGather.semaphores(count),
        ],
        compiler_params=pltpu.CompilerParams(
            vmem_limit_bytes=VMEM_LIMIT, collective_id=1, has_side_effects=True
        ),
    )(qkv, bias, out_full, feed_back, up_shard, down_shard)


def contract_exact(left, right, left_axis, right_axis):
    return lax.dot_general(
        left,
        right,
        (((left_axis,), (right_axis,)), ((), ())),
        precision=lax.Precision.HIGHEST,
        preferred_element_type=F32,
    )


def finish_kernel(
    sizes, heads, chunks,
    qkv, bias, log_total, mixed_t, back_t, cosine, sine, normed, in_t, up_source, down_source, out_source,
    tokens, middle_back, parts, others, down_part, up_part, condition_all, condition_weight,
    tokens_back, condition_back, condition_grad, bias_grad, up_bias, down_bias, in_grad, out_grad, up_grad, down_grad,
    turned, query, key, value, back, key_sum, value_sum, in_source,
    in_total, in_out, in_in, in_sems, up_total, up_out, up_in, up_sems,
    down_total, down_out, down_in, down_sems, out_total, out_out, out_in, out_sems,
    pair_out, pair_in, far_out, far_in, kept, col_sems,
    line_out, line_in, up_all, pieces, arrived, backs, collected, tiny_sems, line_sems,
):
    count = sizes["dp"] * sizes["row"]
    number = shard_number(sizes)
    length = qkv.shape[2]
    rows, width = tokens.shape
    half = HD // 2
    piece = condition_weight.shape[1]
    cond = condition_weight.shape[0]
    peers = other_peers(sizes)
    greet([peer for _, peer in peers] + col_peers())
    me = lax.axis_index("col")
    near, far = col_peers()
    scatter_up = ShardScatter(sizes, up_source, up_total, up_out, up_in, up_sems)
    scatter_down = ShardScatter(sizes, down_source, down_total, down_out, down_in, down_sems)
    scatter_out = ShardScatter(sizes, out_source, out_total, out_out, out_in, out_sems)
    scatter_in = ShardScatter(sizes, in_source, in_total, in_out, in_in, in_sems)
    column = ColumnScatter(pair_out, pair_in, far_out, far_in, kept, chunks, col_sems)

    def tiny(kind, i, source, target):
        return send_copy(source, target, tiny_sems.at[0, kind, i], tiny_sems.at[1, kind, i], peers[i][1])

    def up_copy(i, slot):
        return tiny(0, i, up_part, up_all.at[slot])

    def piece_copy(i, mine, slot):
        return tiny(1, i, pieces.at[mine], arrived.at[slot])

    def back_copy(i, mine, slot):
        return tiny(2, i, backs.at[mine], collected.at[slot])

    def line_copy(k):
        return send_copy(line_out.at[k], line_in.at[k], line_sems.at[0, k], line_sems.at[1, k], (near, far)[k])

    scatter_up.start(0)
    scatter_down.start(0)
    scatter_out.start(0)
    for i in range(count - 1):
        up_copy(i, number).start()
    up_all[number] = up_part[...]

    def turn_back(values, here):
        c, s = cosine[:, here], sine[:, here]
        a, b = values[:half], values[half:]
        return jnp.concatenate([a * c + b * s, b * c - a * s], axis=0)

    for h in range(heads):
        prepare_backward(heads, h, rows, length, qkv, bias, log_total, mixed_t, back_t, query, key, value, back)
    key_sum[...] = jnp.zeros_like(key_sum)
    value_sum[...] = jnp.zeros_like(value_sum)

    def step(i, _):
        here = block_at(i, rows)
        for h in range(heads):
            q, d = query[h, :, here], back[h, :, here]
            weights = jnp.exp2(contract(key[h], q, 1, 0) * UNIT)
            grads = (weights * contract(value[h], d, 1, 0)).astype(BF16)
            value_sum[h] += contract(d[:HD], weights.astype(BF16), 1, 1)
            key_sum[h] += contract(q[:HD], grads, 1, 1)
            query_back = contract(qkv[heads + h], grads, 1, 0) * SCALE
            turned[h, :, here] = turn_back(query_back, here).astype(BF16)

        @pl.when(i == 1)
        def _():
            scatter_up.advance(1)

        @pl.when(i == 2)
        def _():
            scatter_down.advance(1)
            scatter_out.advance(1)
            scatter_up.advance(2)

        return 0

    lax.fori_loop(0, 4, step, 0)

    def finish_block(i, _):
        here = block_at(i, rows)
        for h in range(heads):
            turned[heads + h, :, here] = turn_back(key_sum[h, :, here] * SCALE, here).astype(BF16)
            turned[2 * heads + h, :, here] = value_sum[h, :, here].astype(BF16)
        return 0

    lax.fori_loop(0, 4, finish_block, 0)
    scatter_down.advance(2)
    scatter_out.advance(2)
    in_source[...] = contract(
        normed[...], turned[...].reshape(3 * heads * HD, length), 0, 1
    )
    scatter_in.start(0)
    size = rows // chunks

    def part_of(slot, j):
        start_at = pl.multiple_of(slot * rows + j * size, size)
        block = turned[:, :, pl.ds(start_at, size)].reshape(3 * heads * HD, size)
        return contract(block, in_t[...], 0, 0)

    for j in range(chunks):
        column.give_diagonal(j, part_of(flips(me, (1, 2)), j))
    for j in range(chunks):
        column.give_across(j, part_of(flip(me, 2), j))
    scatter_up.advance(3)
    for j in range(chunks):
        column.give_partner(j, part_of(flip(me, 1), j))
    scatter_in.advance(1)
    for j in range(chunks):
        column.give_own(j, part_of(me, j))
    scatter_down.advance(3)
    scatter_out.advance(3)
    scatter_in.advance(2)
    shift_sum = jnp.zeros((1, width), F32)
    scale_sum = jnp.zeros((1, width), F32)
    for j in range(chunks):
        here = pl.ds(j * size, size)
        own = tokens[here, :]
        center = own - jnp.mean(own, axis=-1, keepdims=True)
        inverse = lax.rsqrt(jnp.mean(center * center, axis=-1, keepdims=True) + EPSILON)
        unit = center * inverse
        grad = column.result(j)
        scaled = grad * (1.0 + parts[1:2, :])
        inner = scaled - jnp.mean(scaled, axis=-1, keepdims=True) - unit * jnp.mean(scaled * unit, axis=-1, keepdims=True)
        tokens_back[here, :] = middle_back[here, :] + inverse * inner
        shift_sum = shift_sum + jnp.sum(grad, axis=0, keepdims=True)
        scale_sum = scale_sum + jnp.sum(grad * unit, axis=0, keepdims=True)
    line_out[0] = jnp.concatenate([shift_sum, scale_sum, others[...], down_part[...]], axis=1)
    line_copy(0).start()
    scatter_in.advance(3)
    steps = len(scatter_in.steps)
    for k in range(4, steps + 1):
        for one in (scatter_up, scatter_down, scatter_out, scatter_in):
            one.advance(k)
    line_copy(0).wait_recv()
    line_out[1] = line_out[0] + line_in[0]
    line_copy(1).start()
    up_grad[...] = scatter_up.result()
    down_grad[...] = scatter_down.result()
    out_grad[...] = scatter_out.result()
    in_grad[...] = scatter_in.result()
    for i in range(count - 1):
        up_copy(i, peers[i][0]).wait_recv()
    up_bias[...] = jnp.sum(jnp.concatenate([up_all[b] for b in range(count)], axis=0), axis=0, keepdims=True)
    line_copy(1).wait_recv()
    line = line_out[1] + line_in[1]
    split = 6 * width
    for b in range(count):
        pieces[b] = jnp.concatenate([line[:, b * piece : (b + 1) * piece], line[:, split:]], axis=1)
    for i in range(count - 1):
        piece_copy(i, peers[i][0], number).start()
    arrived[number] = pieces[number]
    for i in range(count - 1):
        piece_copy(i, number, peers[i][0]).wait_recv()
    stacked = jnp.concatenate([arrived[b] for b in range(count)], axis=0)
    mine = stacked[:, :piece]
    down_bias[...] = jnp.sum(stacked[:, piece:], axis=0, keepdims=True)
    bias_piece = jnp.sum(mine, axis=0, keepdims=True)
    back_rows = contract_exact(mine, condition_weight[...].astype(F32), 1, 1)
    for b in range(count):
        backs[b] = jnp.concatenate([back_rows[b : b + 1], bias_piece], axis=1)
    for i in range(count - 1):
        back_copy(i, peers[i][0], number).start()
    collected[number] = backs[number]
    conditions = jnp.concatenate([condition_all[b] for b in range(count)], axis=0)
    condition_grad[...] = contract_exact(conditions, mine, 0, 0)
    for i in range(count - 1):
        back_copy(i, number, peers[i][0]).wait_recv()
    gathered = [collected[b] for b in range(count)]
    bias_grad[...] = jnp.concatenate([one[:, cond:] for one in gathered], axis=1)
    condition_back[...] = jnp.sum(
        jnp.concatenate([one[:, :cond] for one in gathered], axis=0), axis=0, keepdims=True
    )
    for i in range(count - 1):
        up_copy(i, number).wait_send()
        piece_copy(i, peers[i][0], number).wait_send()
        back_copy(i, peers[i][0], number).wait_send()
    for k in range(2):
        line_copy(k).wait_send()
    for one in (scatter_up, scatter_down, scatter_out, scatter_in):
        one.close()
    column.close()


def finish(sizes, heads, qkv, bias, log_total, mixed_t, back_t, cosine, sine, normed, in_t, up_source, down_source,
           out_source, tokens, middle_back, parts, others, down_part, up_part, condition_all, condition_weight):
    count = sizes["dp"] * sizes["row"]
    length = qkv.shape[2]
    rows, width = tokens.shape
    chunks = 2
    local = heads * HD
    hidden = up_source.shape[1]
    cond, piece = condition_weight.shape
    share = width // count
    vmem = pl.BlockSpec(memory_space=pltpu.VMEM)
    return pl.pallas_call(
        functools.partial(finish_kernel, sizes, heads, chunks),
        out_shape=[
            jax.ShapeDtypeStruct((rows, width), F32),
            jax.ShapeDtypeStruct((1, cond), F32),
            jax.ShapeDtypeStruct((cond, piece), F32),
            jax.ShapeDtypeStruct((1, 6 * width), F32),
            jax.ShapeDtypeStruct((1, hidden), F32),
            jax.ShapeDtypeStruct((1, width), F32),
            jax.ShapeDtypeStruct((share, 3 * local), F32),
            jax.ShapeDtypeStruct((share, local), F32),
            jax.ShapeDtypeStruct((share, hidden), F32),
            jax.ShapeDtypeStruct((share, hidden), F32),
        ],
        in_specs=[vmem] * 20,
        out_specs=[vmem] * 10,
        scratch_shapes=[
            pltpu.VMEM((3 * heads, HD, length), BF16),
            pltpu.VMEM((heads, AUG, length), BF16),
            pltpu.VMEM((heads, length, AUG), BF16),
            pltpu.VMEM((heads, length, AUG), BF16),
            pltpu.VMEM((heads, AUG, length), BF16),
            pltpu.VMEM((heads, HD, length), F32),
            pltpu.VMEM((heads, HD, length), F32),
            pltpu.VMEM((width, 3 * local), F32),
            *ShardScatter.scratch(count, share, 3 * local),
            *ShardScatter.scratch(count, share, hidden),
            *ShardScatter.scratch(count, share, hidden),
            *ShardScatter.scratch(count, share, local),
            *ColumnScatter.scratch(rows, width, chunks),
            pltpu.VMEM((2, 1, 7 * width), F32),
            pltpu.VMEM((2, 1, 7 * width), F32),
            pltpu.VMEM((count, 1, hidden), F32),
            pltpu.VMEM((count, 1, piece + width), F32),
            pltpu.VMEM((count, 1, piece + width), F32),
            pltpu.VMEM((count, 1, cond + piece), F32),
            pltpu.VMEM((count, 1, cond + piece), F32),
            pltpu.SemaphoreType.DMA((2, 3, count - 1)),
            pltpu.SemaphoreType.DMA((2, 2)),
        ],
        compiler_params=pltpu.CompilerParams(
            vmem_limit_bytes=VMEM_LIMIT, collective_id=2, has_side_effects=True
        ),
    )(qkv, bias, log_total, mixed_t, back_t, cosine, sine, normed, in_t, up_source, down_source, out_source,
      tokens, middle_back, parts, others, down_part, up_part, condition_all, condition_weight)


def shards(
    sizes,
    tokens,
    condition,
    lengths,
    condition_weight,
    condition_bias,
    attention_in,
    attention_out,
    up_weight,
    up_bias,
    down_weight,
    down_bias,
    cotangent,
):
    columns = lax.axis_size("col")
    column_index = lax.axis_index("col")
    rows = tokens.shape[1]
    width = tokens.shape[2]
    length_all = rows * columns
    local_width = attention_in.shape[2]
    heads = local_width // HD
    in_shard = attention_in.reshape(attention_in.shape[0], 3 * local_width).astype(BF16)
    out_shard = attention_out.T.astype(BF16)
    up_shard = up_weight.astype(BF16)
    down_shard = down_weight.T.astype(BF16)
    condition_low = condition.astype(BF16)
    weight_low = condition_weight.astype(BF16)
    own_rows = tokens[0]
    length = lengths[0]
    position = column_index * rows + jnp.arange(rows)
    valid = (position < length).astype(F32)
    bias = jnp.where(jnp.arange(length_all) < length, 0.0, MASKED).astype(F32)[None]
    cosine, sine = (jnp.asarray(table) for table in rotary_tables(length_all))
    parts, normed_blocks, qkv, out_full, feed_back, down_bias_part, in_t, condition_all = start(
        sizes, heads, condition_low.astype(F32), weight_low, condition_bias[None], own_rows,
        in_shard, out_shard, cosine, sine, cotangent[0], valid[:, None],
    )
    normed_all = normed_blocks.reshape(length_all, width)
    attention, mixed_t, log_total, feed_back_blocks, up_full, down_t = attend(
        sizes, heads, qkv, bias, out_full, feed_back, up_shard, down_shard
    )
    mixed_rows = mixed_t.reshape(local_width, length_all)
    down_full = down_t.T
    feed_back_all = feed_back_blocks.reshape(length_all, width)
    middle = own_rows + parts[2] * attention
    second, second_pull = jax.vjp(norm_shift, middle, parts[3], parts[4])
    second_low = second.astype(BF16)
    hidden_cols = up_full.shape[1]
    second_all = lax.all_gather(second_low, "col", axis=0, tiled=True)
    bias_part = lax.dynamic_slice_in_dim(up_bias, column_index * hidden_cols, hidden_cols)
    before = jnp.dot(second_all, up_full, preferred_element_type=F32) + bias_part
    hidden, gelu_pull = jax.vjp(gelu_tanh, before)
    hidden_low = hidden.astype(BF16)
    feed = lax.psum_scatter(
        jnp.dot(hidden_low, down_full, preferred_element_type=F32).astype(BF16),
        "col",
        scatter_dimension=0,
        tiled=True,
    ).astype(F32)
    result = middle + parts[5] * (feed + down_bias)
    incoming = cotangent[0] * valid[:, None]
    gate_feed = jnp.sum(incoming * (feed + down_bias), axis=0)
    hidden_back = jnp.einsum("sd,fd->sf", feed_back_all, down_full, preferred_element_type=F32)
    down_grad = jnp.einsum("sd,sf->df", feed_back_all, hidden_low, preferred_element_type=F32)
    before_back = gelu_pull(hidden_back)[0].astype(BF16)
    up_grad = jnp.einsum("sd,sf->df", second_all, before_back, preferred_element_type=F32)
    up_bias_part = jnp.sum(before_back.astype(F32), axis=0)
    second_back = lax.psum_scatter(
        jnp.einsum("sf,df->sd", before_back, up_full, preferred_element_type=F32).astype(BF16),
        "col",
        scatter_dimension=0,
        tiled=True,
    ).astype(F32)
    middle_part, shift_feed, scale_feed = second_pull(second_back)
    middle_back = incoming + middle_part
    gate_attention = jnp.sum(middle_back * attention, axis=0)
    attention_back = (parts[2] * middle_back).astype(BF16)
    attention_back_all = lax.all_gather(attention_back, "col", axis=0, tiled=True)
    out_grad = jnp.einsum("sd,cs->dc", attention_back_all, mixed_rows, preferred_element_type=F32)
    mixed_back = jnp.einsum("sd,cd->cs", attention_back_all, out_full, preferred_element_type=F32)
    others = jnp.concatenate([gate_attention, shift_feed, scale_feed, gate_feed])[None]
    (
        tokens_back, condition_back, condition_grad, bias_grad, up_bias_grad, down_bias_grad,
        in_grad, out_grad, up_grad, down_grad,
    ) = finish(
        sizes, heads, qkv, bias, log_total, mixed_t, mixed_back.astype(BF16).reshape(heads, HD, length_all),
        cosine, sine, normed_all, in_t, up_grad, down_grad, out_grad, own_rows, middle_back, parts,
        others, down_bias_part, up_bias_part[None], condition_all, weight_low,
    )
    return (
        result[None],
        tokens_back[None],
        condition_back,
        condition_grad,
        bias_grad[0],
        in_grad.reshape(attention_in.shape),
        out_grad.T,
        up_grad,
        up_bias_grad[0],
        down_grad.T,
        down_bias_grad[0],
    )


def solution(mesh):
    sizes = {axis: mesh.shape[axis] for axis in ("dp", "row", "col")}
    in_specs = (
        P(("dp", "row"), "col", None),
        P(("dp", "row"), None),
        P(("dp", "row")),
        P(None, ("dp", "row")),
        P(),
        P(("dp", "row"), None, "col"),
        P("col", ("dp", "row")),
        P(("dp", "row"), "col"),
        P(),
        P("col", ("dp", "row")),
        P(),
        P(("dp", "row"), "col", None),
    )
    out_specs = (
        P(("dp", "row"), "col", None),
        P(("dp", "row"), "col", None),
        P(("dp", "row"), None),
        P(None, ("dp", "row")),
        P(),
        P(("dp", "row"), None, "col"),
        P("col", ("dp", "row")),
        P(("dp", "row"), "col"),
        P("col"),
        P("col", ("dp", "row")),
        P(),
    )
    return jax.shard_map(functools.partial(shards, sizes), mesh=mesh, in_specs=in_specs, out_specs=out_specs, check_vma=False)
```

```python
import functools
import math

import jax
import jax.numpy as jnp
import numpy as np
from jax import lax
from jax.experimental import pallas as pl
from jax.experimental.pallas import tpu as pltpu
from jax.sharding import PartitionSpec as P

HD = 64
AUG = 128
EPSILON = 1e-06
MASKED = -1e30
CUBIC = 0.044715
SLOPE = math.sqrt(2.0 / math.pi)
SCALE = 1.0 / math.sqrt(HD)
UNIT = SCALE * math.log2(math.e)
F32 = jnp.float32
BF16 = jnp.bfloat16
VMEM_LIMIT = 67043328


def layer_norm(values):
    center = values - jnp.mean(values, axis=-1, keepdims=True)
    spread = jnp.mean(center * center, axis=-1, keepdims=True)
    return center * lax.rsqrt(spread + EPSILON)


def rotary_tables(length):
    half = HD // 2
    exponent = np.arange(half, dtype=np.float32) * np.float32(2.0 / HD)
    frequency = np.exp(np.float32(-math.log(10000.0)) * exponent).astype(np.float32)
    angle = frequency[:, None] * np.arange(length, dtype=np.float32)[None, :]
    angle = angle.astype(np.float32).astype(np.float64)
    return np.cos(angle).astype(np.float32), np.sin(angle).astype(np.float32)


def contract(left, right, left_axis, right_axis):
    return lax.dot_general(
        left,
        right,
        (((left_axis,), (right_axis,)), ((), ())),
        preferred_element_type=F32,
    )


def block_at(index, size):
    return pl.ds(pl.multiple_of(index * size, size), size)


def split_three(values):
    high = values.astype(BF16)
    rest = values - high.astype(F32)
    middle = rest.astype(BF16)
    low = (rest - middle.astype(F32)).astype(BF16)
    return high.astype(F32), middle.astype(F32), low.astype(F32)


def augment(rows, extras):
    n = rows.shape[1]
    extras = [jnp.broadcast_to(e, (1, n)) for e in extras]
    pad = jnp.zeros((AUG - HD - len(extras), n), F32)
    return jnp.concatenate([rows] + extras + [pad], axis=0)


def attend_block(heads, here, query, key, value_t, mixed_t, log_total):
    scores = [contract(key[h], query[h, :, here], 1, 0) for h in range(heads)]
    for h in range(heads):
        top = jnp.max(scores[h], axis=0, keepdims=True)
        weights = jnp.exp2((scores[h] - top) * UNIT)
        total = jnp.sum(weights, axis=0, keepdims=True)
        out = contract(value_t[h], weights.astype(BF16), 1, 0) * (1.0 / total)
        mixed_t[h, :, here] = out.astype(BF16)
        log_total[h, :, here] = top * UNIT + jnp.log2(total)


def prepare_backward(heads, h, size, length, qkv, bias, log_total, mixed_t, back_t, query, key, value, back):
    def step(i, _):
        here = block_at(i, size)
        one = jnp.ones((1, size), F32)
        zero = jnp.zeros((1, size), F32)
        logs = split_three(log_total[h, :, here] * (-1.0 / UNIT))
        query[h, :, here] = augment(qkv[h, :, here].astype(F32), [one, *logs]).astype(BF16)
        keys = augment(qkv[heads + h, :, here].astype(F32), [bias[:, here], one, one, one])
        key[h, here, :] = keys.T.astype(BF16)
        values = augment(qkv[2 * heads + h, :, here].astype(F32), [zero, one, one, one])
        value[h, here, :] = values.T.astype(BF16)
        grad = back_t[h, :, here].astype(F32)
        center = jnp.sum(grad * mixed_t[h, :, here].astype(F32), axis=0, keepdims=True)
        back[h, :, here] = augment(grad, [zero, *split_three(-center)]).astype(BF16)
        return 0

    lax.fori_loop(0, length // size, step, 0)


MESH = pl.DeviceIdType.MESH


def flip(index, bit):
    return index + bit - 2 * bit * lax.rem(lax.div(index, bit), 2)


def flips(index, bits):
    for bit in bits:
        index = flip(index, bit)
    return index


def doubling(sizes):
    steps = []
    for axis, stride in (("dp", sizes["row"]), ("row", 1)):
        bit = sizes[axis] // 2
        while bit:
            steps.append((axis, bit, bit * stride))
            bit //= 2
    return steps


def subsets(bits):
    out = [()]
    for bit in bits:
        out = out + [kept + (bit,) for kept in out]
    return out


def send_copy(source, target, send, receive, peer):
    return pltpu.make_async_remote_copy(
        src_ref=source, dst_ref=target, send_sem=send, recv_sem=receive, device_id=peer, device_id_type=MESH
    )


def greet(peers):
    barrier = pltpu.get_barrier_semaphore()
    for peer in peers:
        pl.semaphore_signal(barrier, inc=1, device_id=peer, device_id_type=MESH)
    pl.semaphore_wait(barrier, len(peers))


def shard_number(sizes):
    return lax.axis_index("dp") * sizes["row"] + lax.axis_index("row")


def doubling_peers(sizes):
    return [{axis: flip(lax.axis_index(axis), bit)} for axis, bit, _ in doubling(sizes)]


def col_peers():
    me = lax.axis_index("col")
    return [{"col": flip(me, 1)}, {"col": flip(me, 2)}]


class ShardGather:
    def __init__(self, sizes, shard, full, sems):
        self.steps = doubling(sizes)
        self.rows = shard.shape[0]
        self.shard, self.full, self.sems = shard, full, sems
        self.me = shard_number(sizes)

    def slot(self, number):
        return self.full.at[pl.ds(pl.multiple_of(number * self.rows, self.rows), self.rows), :]

    def copies(self, k, arriving):
        axis, bit, stride = self.steps[k]
        peer = {axis: flip(lax.axis_index(axis), bit)}
        out = []
        for i, kept in enumerate(subsets([s[2] for s in self.steps[:k]])):
            number = flips(self.me, kept + ((stride,) if arriving else ()))
            source = self.slot(number)
            if not arriving and not kept:
                source = self.shard
            at = 2**k - 1 + i
            out.append(send_copy(source, self.slot(number), self.sems.at[0, at], self.sems.at[1, at], peer))
        return out

    def keep(self):
        self.slot(self.me)[...] = self.shard[...]

    def start(self, k):
        for copy in self.copies(k, False):
            copy.start()

    def arrived(self, k):
        for copy in self.copies(k, True):
            copy.wait_recv()

    def advance(self, k):
        if 0 < k <= len(self.steps):
            self.arrived(k - 1)
        if k < len(self.steps):
            self.start(k)

    def close(self):
        for k in range(len(self.steps)):
            for copy in self.copies(k, False):
                copy.wait_send()

    @staticmethod
    def semaphores(count):
        return pltpu.SemaphoreType.DMA((2, count - 1))


class ShardScatter:
    def __init__(self, sizes, source, total, out_buf, in_buf, sems):
        self.steps = doubling(sizes)[::-1]
        self.rows = out_buf.shape[1]
        self.source, self.total, self.out_buf, self.in_buf, self.sems = source, total, out_buf, in_buf, sems
        self.me = shard_number(sizes)
        self.first = [0]
        for k in range(len(self.steps)):
            self.first.append(self.first[-1] + 2 ** (len(self.steps) - 1 - k))

    def part(self, number):
        return pl.ds(pl.multiple_of(number * self.rows, self.rows), self.rows)

    def rest(self, k):
        return subsets([s[2] for s in self.steps[k + 1 :]])

    def copy(self, k, i):
        axis, bit, _ = self.steps[k]
        at = self.first[k] + i
        peer = {axis: flip(lax.axis_index(axis), bit)}
        return send_copy(self.out_buf.at[at], self.in_buf.at[at], self.sems.at[0, at], self.sems.at[1, at], peer)

    def held(self, k):
        return self.source if k == 0 else self.total

    def start(self, k):
        stride = self.steps[k][2]
        for i, kept in enumerate(self.rest(k)):
            number = flips(self.me, (stride,) + kept)
            self.out_buf[self.first[k] + i] = self.held(k)[self.part(number), :].astype(BF16)
            self.copy(k, i).start()

    def arrived(self, k):
        for i, kept in enumerate(self.rest(k)):
            self.copy(k, i).wait_recv()
            here = self.part(flips(self.me, kept))
            self.total[here, :] = self.held(k)[here, :].astype(F32) + self.in_buf[self.first[k] + i].astype(F32)

    def advance(self, k):
        if 0 < k <= len(self.steps):
            self.arrived(k - 1)
        if k < len(self.steps):
            self.start(k)

    def result(self):
        return self.total[self.part(self.me), :]

    def close(self):
        for k in range(len(self.steps)):
            for i in range(len(self.rest(k))):
                self.copy(k, i).wait_send()

    @staticmethod
    def scratch(count, rows, width):
        return [
            pltpu.VMEM((count * rows, width), F32),
            pltpu.VMEM((count - 1, rows, width), BF16),
            pltpu.VMEM((count - 1, rows, width), BF16),
            pltpu.SemaphoreType.DMA((2, count - 1)),
        ]


class ColumnGather:
    def __init__(self, full, chunks, sems):
        self.full, self.chunks, self.sems = full, chunks, sems
        self.me = lax.axis_index("col")
        self.rows = full.shape[1] // chunks

    def chunk(self, slot, j):
        return self.full.at[slot, pl.ds(j * self.rows, self.rows), :]

    def copy(self, kind, j, slot):
        peer = {"col": flip(self.me, 2 if kind == 1 else 1)}
        here = self.chunk(slot, j)
        return send_copy(here, here, self.sems.at[0, kind, j], self.sems.at[1, kind, j], peer)

    def start(self, j):
        for kind in (1, 0):
            copy = self.copy(kind, j, self.me)
            copy.start()

    def partner(self, j):
        self.copy(0, j, flip(self.me, 1)).wait_recv()

    def across(self, j):
        there = flip(self.me, 2)
        self.copy(1, j, there).wait_recv()
        copy = self.copy(2, j, there)
        copy.start()

    def diagonal(self, j):
        self.copy(2, j, flips(self.me, (1, 2))).wait_recv()

    def close(self):
        for j in range(self.chunks):
            for kind in range(3):
                self.copy(kind, j, self.me).wait_send()

    @staticmethod
    def semaphores(chunks):
        return pltpu.SemaphoreType.DMA((2, 3, chunks))


class ColumnScatter:
    def __init__(self, pair_out, pair_in, far_out, far_in, kept, chunks, sems):
        self.pair_out, self.pair_in, self.far_out, self.far_in = pair_out, pair_in, far_out, far_in
        self.kept, self.chunks, self.sems = kept, chunks, sems
        self.rows = kept.shape[0] // chunks
        me = lax.axis_index("col")
        self.near, self.far = {"col": flip(me, 1)}, {"col": flip(me, 2)}

    def at(self, j):
        return pl.ds(j * self.rows, self.rows)

    def pair(self, which, j):
        return send_copy(
            self.pair_out.at[which, self.at(j), :],
            self.pair_in.at[which, self.at(j), :],
            self.sems.at[0, which, j],
            self.sems.at[1, which, j],
            self.near,
        )

    def cross(self, j):
        return send_copy(
            self.far_out.at[self.at(j), :],
            self.far_in.at[self.at(j), :],
            self.sems.at[0, 2, j],
            self.sems.at[1, 2, j],
            self.far,
        )

    def begin(self, copy):
        copy.start()

    def give_diagonal(self, j, value):
        self.pair_out[1, self.at(j), :] = value.astype(BF16)
        self.begin(self.pair(1, j))

    def give_across(self, j, value):
        self.pair(1, j).wait_recv()
        self.far_out[self.at(j), :] = (value + self.pair_in[1, self.at(j), :].astype(F32)).astype(BF16)
        if self.far_in is not None:
            self.begin(self.cross(j))

    def give_partner(self, j, value):
        self.pair_out[0, self.at(j), :] = value.astype(BF16)
        self.begin(self.pair(0, j))

    def give_own(self, j, value):
        self.kept[self.at(j), :] = value

    def settle(self, j):
        self.pair(0, j).wait_recv()
        self.kept[self.at(j), :] = self.kept[self.at(j), :] + self.pair_in[0, self.at(j), :].astype(F32)

    def result(self, j):
        self.pair(0, j).wait_recv()
        self.cross(j).wait_recv()
        near = self.kept[self.at(j), :] + self.pair_in[0, self.at(j), :].astype(F32)
        return near + self.far_in[self.at(j), :].astype(F32)

    def close(self):
        for j in range(self.chunks):
            self.pair(0, j).wait_send()
            self.pair(1, j).wait_send()
            if self.far_in is not None:
                self.cross(j).wait_send()

    @staticmethod
    def scratch(rows, width, chunks):
        return [
            pltpu.VMEM((2, rows, width), BF16),
            pltpu.VMEM((2, rows, width), BF16),
            pltpu.VMEM((rows, width), BF16),
            pltpu.VMEM((rows, width), BF16),
            pltpu.VMEM((rows, width), F32),
            pltpu.SemaphoreType.DMA((2, 3, chunks)),
        ]


def other_peers(sizes):
    number = shard_number(sizes)
    total = sizes["dp"] * sizes["row"]
    bits = [stride for _, _, stride in doubling(sizes)]
    out = []
    for kept in subsets(bits)[1:]:
        peer = {}
        for axis, bit, stride in doubling(sizes):
            if stride in kept:
                peer[axis] = flip(peer.get(axis, lax.axis_index(axis)), bit)
        out.append((flips(number, kept), peer))
    assert len(out) == total - 1
    return out


def start_kernel(
    sizes, heads, chunks,
    condition, condition_weight, condition_bias, tokens, in_shard, out_shard, cosine, sine, cotangent, valid,
    modulation, normed, qkv, out_full, feed_back, bias_part, in_t, condition_all,
    pieces, arrived, in_full, out_t, unit, sems_tiny, sems_in, sems_out, sems_col,
):
    count = sizes["dp"] * sizes["row"]
    number = shard_number(sizes)
    rows, width = tokens.shape
    others = other_peers(sizes)
    greet([peer for _, peer in others] + col_peers())
    gather_in = ShardGather(sizes, in_shard, in_full, sems_in)
    gather_out = ShardGather(sizes, out_shard, out_t, sems_out)
    gather_col = ColumnGather(normed, chunks, sems_col)

    def condition_copy(i, slot):
        return send_copy(
            condition, condition_all.at[slot], sems_tiny.at[0, i], sems_tiny.at[1, i], others[i][1]
        )

    def piece_copy(i, mine, slot):
        return send_copy(
            pieces.at[mine], arrived.at[slot], sems_tiny.at[2, i], sems_tiny.at[3, i], others[i][1]
        )

    for i in range(count - 1):
        condition_copy(i, number).start()
    gather_in.start(0)
    gather_out.start(0)
    condition_all[number] = condition[...]
    gather_in.keep()
    gather_out.keep()
    size = rows // chunks

    def normal(j, _):
        here = block_at(j, size)
        unit[here, :] = layer_norm(tokens[here, :])
        return 0

    lax.fori_loop(0, chunks, normal, 0)
    for i in range(count - 1):
        condition_copy(i, others[i][0]).wait_recv()
    stacked = jnp.concatenate([condition_all[b] for b in range(count)], axis=0)
    product = contract(stacked.astype(BF16), condition_weight[...], 1, 0)
    for b in range(count):
        pieces[b] = product[b : b + 1]
    for i in range(count - 1):
        piece_copy(i, others[i][0], number).start()
    arrived[number] = pieces[number]
    gather_in.advance(1)
    gather_out.advance(1)
    for i in range(count - 1):
        piece_copy(i, number, others[i][0]).wait_recv()
    line = jnp.concatenate([arrived[b] for b in range(count)], axis=1) + condition_bias[...]
    parts = [line[:, t * width : (t + 1) * width] for t in range(6)]
    for t in range(6):
        modulation[t : t + 1, :] = parts[t]
    for j in range(chunks):
        here = pl.ds(j * size, size)
        value = unit[here, :] * (1.0 + parts[1]) + parts[0]
        normed[gather_col.me, here, :] = value.astype(BF16)
        gather_col.start(j)
    gather_in.advance(2)
    gather_out.advance(2)
    total = jnp.zeros((1, width), F32)
    for j in range(chunks):
        here = pl.ds(j * size, size)
        value = parts[5] * (cotangent[here, :] * valid[here, :])
        feed_back[here, :] = value.astype(BF16)
        total = total + jnp.sum(value, axis=0, keepdims=True)
    bias_part[...] = total
    steps = len(gather_in.steps)
    for k in range(3, steps + 1):
        gather_in.advance(k)
        gather_out.advance(k)
    in_t[...] = in_full[...].astype(F32).T.astype(BF16)
    out_full[...] = out_t[...].astype(F32).T.astype(BF16)

    def project(slot):
        here = pl.ds(pl.multiple_of(slot * rows, rows), rows)
        both = contract(in_t[...], normed[slot], 1, 1)
        half = HD // 2
        c, s = cosine[:, here], sine[:, here]
        for h in range(heads):
            for t in range(3):
                at = (t * heads + h) * HD
                a, b = both[at : at + half], both[at + half : at + HD]
                if t < 2:
                    a, b = a * c - b * s, b * c + a * s
                qkv[t * heads + h, :, here] = jnp.concatenate([a, b], axis=0).astype(BF16)

    me = gather_col.me
    far = flip(me, 2)

    def steps_of(i, _):
        @pl.when(i == 1)
        def _():
            for j in range(chunks):
                gather_col.partner(j)

        @pl.when(i == 2)
        def _():
            for j in range(chunks):
                gather_col.across(j)

        @pl.when(i == 3)
        def _():
            for j in range(chunks):
                gather_col.diagonal(j)

        project(flip_by(me, i))
        return 0

    lax.fori_loop(0, 4, steps_of, 0)
    for i in range(count - 1):
        condition_copy(i, number).wait_send()
        piece_copy(i, others[i][0], number).wait_send()
    gather_in.close()
    gather_out.close()
    gather_col.close()


def flip_by(index, pattern):
    out = 0
    for bit in (1, 2):
        a, b = lax.rem(lax.div(index, bit), 2), lax.rem(lax.div(pattern, bit), 2)
        out = out + bit * (a + b - 2 * a * b)
    return out


def start(sizes, heads, condition, condition_weight, condition_bias, tokens, in_shard, out_shard, cosine, sine, cotangent, valid):
    count = sizes["dp"] * sizes["row"]
    rows, width = tokens.shape
    length = cosine.shape[1]
    chunks = 2
    vmem = pl.BlockSpec(memory_space=pltpu.VMEM)
    piece = condition_weight.shape[1]
    local = heads * HD
    return pl.pallas_call(
        functools.partial(start_kernel, sizes, heads, chunks),
        out_shape=[
            jax.ShapeDtypeStruct((6, width), F32),
            jax.ShapeDtypeStruct((4, rows, width), BF16),
            jax.ShapeDtypeStruct((3 * heads, HD, length), BF16),
            jax.ShapeDtypeStruct((local, width), BF16),
            jax.ShapeDtypeStruct((rows, width), BF16),
            jax.ShapeDtypeStruct((1, width), F32),
            jax.ShapeDtypeStruct((3 * local, width), BF16),
            jax.ShapeDtypeStruct((count,) + condition.shape, F32),
        ],
        in_specs=[vmem] * 10,
        out_specs=[vmem] * 8,
        scratch_shapes=[
            pltpu.VMEM((count, 1, piece), F32),
            pltpu.VMEM((count, 1, piece), F32),
            pltpu.VMEM((width, 3 * local), BF16),
            pltpu.VMEM((width, local), BF16),
            pltpu.VMEM((rows, width), F32),
            pltpu.SemaphoreType.DMA((4, count - 1)),
            ShardGather.semaphores(count),
            ShardGather.semaphores(count),
            ColumnGather.semaphores(chunks),
        ],
        compiler_params=pltpu.CompilerParams(
            vmem_limit_bytes=VMEM_LIMIT, collective_id=0, has_side_effects=True
        ),
    )(condition, condition_weight, condition_bias, tokens, in_shard, out_shard, cosine, sine, cotangent, valid)


def attention_kernel(
    sizes, heads, chunks,
    qkv, bias, out_full, feed_back, up_shard, down_shard,
    attention, mixed_t, log_total, feed_back_all, up_full, down_t,
    query, key, pair_out, pair_in, far_out, far_in, kept, sems_scatter, sems_col, sems_up, sems_down,
):
    rows = feed_back.shape[0]
    length = qkv.shape[2]
    greet(doubling_peers(sizes) + col_peers())
    gather_up = ShardGather(sizes, up_shard, up_full, sems_up)
    gather_down = ShardGather(sizes, down_shard, down_t, sems_down)
    gather_col = ColumnGather(feed_back_all, chunks, sems_col)
    scatter = ColumnScatter(pair_out, pair_in, far_out, far_in, kept, 1, sems_scatter)
    me = gather_col.me
    gather_up.start(0)
    gather_down.start(0)
    feed_back_all[me] = feed_back[...]
    for j in range(chunks):
        gather_col.start(j)
    gather_up.keep()
    gather_down.keep()

    def prepare(i, _):
        here = block_at(i, rows)
        one = jnp.ones((1, rows), F32)
        for h in range(heads):
            query[h, :, here] = augment(qkv[h, :, here].astype(F32), [one]).astype(BF16)
            keys = augment(qkv[heads + h, :, here].astype(F32), [bias[:, here], one, one, one])
            key[h, here, :] = keys.T.astype(BF16)
        return 0

    lax.fori_loop(0, length // rows, prepare, 0)
    steps = len(gather_up.steps)

    def step(i, _):
        here = block_at(flip_by(me, 3 - i), rows)
        attend_block(heads, here, query, key, qkv.at[pl.ds(2 * heads, heads)], mixed_t, log_total)
        value = contract(mixed_t[:, :, here].reshape(heads * HD, rows), out_full[...], 0, 0)
        for order, give in enumerate(
            (scatter.give_diagonal, scatter.give_across, scatter.give_partner, scatter.give_own)
        ):

            @pl.when(i == order)
            def _():
                give(0, value)
                if order < 3:
                    gather_up.advance(order + 1)
                    gather_down.advance(order + 1)

        return 0

    lax.fori_loop(0, 4, step, 0)
    for k in range(4, steps + 1):
        gather_up.advance(k)
        gather_down.advance(k)
    for j in range(chunks):
        gather_col.across(j)
    for j in range(chunks):
        gather_col.partner(j)
        gather_col.diagonal(j)
    attention[...] = scatter.result(0)
    gather_up.close()
    gather_down.close()
    gather_col.close()
    scatter.close()


def attend(sizes, heads, qkv, bias, out_full, feed_back, up_shard, down_shard):
    count = sizes["dp"] * sizes["row"]
    rows, width = feed_back.shape
    length = qkv.shape[2]
    chunks = 2
    hidden = up_shard.shape[1]
    vmem = pl.BlockSpec(memory_space=pltpu.VMEM)
    return pl.pallas_call(
        functools.partial(attention_kernel, sizes, heads, chunks),
        out_shape=[
            jax.ShapeDtypeStruct((rows, width), F32),
            jax.ShapeDtypeStruct((heads, HD, length), BF16),
            jax.ShapeDtypeStruct((heads, 1, length), F32),
            jax.ShapeDtypeStruct((4, rows, width), BF16),
            jax.ShapeDtypeStruct((width, hidden), BF16),
            jax.ShapeDtypeStruct((width, hidden), BF16),
        ],
        in_specs=[vmem] * 6,
        out_specs=[vmem] * 6,
        scratch_shapes=[
            pltpu.VMEM((heads, AUG, length), BF16),
            pltpu.VMEM((heads, length, AUG), BF16),
            *ColumnScatter.scratch(rows, width, 1),
            ColumnGather.semaphores(chunks),
            ShardGather.semaphores(count),
            ShardGather.semaphores(count),
        ],
        compiler_params=pltpu.CompilerParams(
            vmem_limit_bytes=VMEM_LIMIT, collective_id=1, has_side_effects=True
        ),
    )(qkv, bias, out_full, feed_back, up_shard, down_shard)


def feed_kernel(
    sizes, heads, chunks,
    tokens, attention, parts, up_full, down_t, up_bias, feed_back_all, cotangent, valid, mixed_t, out_full,
    middle, middle_back, mixed_back, up_grad, down_grad, out_grad, up_part, sums, feed_far, feed_kept,
    second_all, hidden_all, before_all, back_all, second_sems, back_sems,
    pair_out, pair_in, far_out, far_in, kept, scatter_sems, feed_pair_out, feed_pair_in, feed_sems,
):
    rows, width = tokens.shape
    size = rows // chunks
    length = 4 * rows
    greet(col_peers())
    gather = ColumnGather(second_all, chunks, second_sems)
    gather_back = ColumnGather(back_all, chunks, back_sems)
    scatter = ColumnScatter(pair_out, pair_in, far_out, far_in, kept, chunks, scatter_sems)
    feed = ColumnScatter(feed_pair_out, feed_pair_in, feed_far, None, feed_kept, chunks, feed_sems)
    me = gather.me
    for j in range(chunks):
        here = pl.ds(j * size, size)
        value = tokens[here, :] + parts[2:3, :] * attention[here, :]
        middle[here, :] = value
        second_all[me, here, :] = (layer_norm(value) * (1.0 + parts[4:5, :]) + parts[3:4, :]).astype(BF16)
        gather.start(j)
    up_part[...] = jnp.zeros_like(up_part)

    def block(i, _):
        late = lax.div(i, 4)
        pattern = (1 - late) * lax.div(i, 2) + late * (3 - lax.rem(i, 2))
        j = (1 - late) * lax.rem(i, 2) + late * (lax.div(i, 2) - 2)
        slot = flip_by(me, pattern)
        here = pl.ds(pl.multiple_of(j * size, size), size)

        @pl.when(i == 2)
        def _():
            for c in range(chunks):
                gather.partner(c)

        @pl.when(i == 3)
        def _():
            gather.across(0)

        @pl.when(i == 4)
        def _():
            gather.diagonal(0)

        @pl.when(i == 6)
        def _():
            gather.diagonal(1)

        before = contract(second_all[slot, here, :], up_full[...], 1, 0) + up_bias[...]
        bend = jnp.tanh(SLOPE * (before + CUBIC * before * before * before))
        hidden = (0.5 * before * (1.0 + bend)).astype(BF16)
        slope = 0.5 * (1.0 + bend) + 0.5 * before * (1.0 - bend * bend) * (SLOPE * (1.0 + 3.0 * CUBIC * before * before))
        hidden_back = contract(feed_back_all[slot, here, :], down_t[...], 1, 0)
        before_back = (hidden_back * slope).astype(BF16)
        hidden_all[slot, here, :] = hidden
        before_all[slot, here, :] = before_back
        up_part[...] += jnp.sum(before_back.astype(F32), axis=0, keepdims=True)
        back_value = contract(before_back, up_full[...], 1, 1)
        feed_value = contract(hidden, down_t[...], 1, 1)
        for at, (name, c) in enumerate(
            (("own", 0), ("own", 1), ("partner", 0), ("partner", 1), ("diagonal", 0), ("across", 0), ("diagonal", 1), ("across", 1))
        ):

            @pl.when(i == at)
            def _():
                getattr(scatter, "give_" + name)(c, back_value)
                getattr(feed, "give_" + name)(c, feed_value)
                if at == 5:
                    gather.across(1)

        return 0

    lax.fori_loop(0, 8, block, 0)
    gate_sum = jnp.zeros((1, width), F32)
    shift_sum = jnp.zeros((1, width), F32)
    scale_sum = jnp.zeros((1, width), F32)
    for j in range(chunks):
        here = pl.ds(j * size, size)
        own = middle[here, :]
        center = own - jnp.mean(own, axis=-1, keepdims=True)
        inverse = lax.rsqrt(jnp.mean(center * center, axis=-1, keepdims=True) + EPSILON)
        unit = center * inverse
        grad = scatter.result(j)
        scaled = grad * (1.0 + parts[4:5, :])
        inner = scaled - jnp.mean(scaled, axis=-1, keepdims=True) - unit * jnp.mean(scaled * unit, axis=-1, keepdims=True)
        total = cotangent[here, :] * valid[here, :] + inverse * inner
        middle_back[here, :] = total
        back_all[me, here, :] = (parts[2:3, :] * total).astype(BF16)
        gather_back.start(j)
        gate_sum = gate_sum + jnp.sum(total * attention[here, :], axis=0, keepdims=True)
        shift_sum = shift_sum + jnp.sum(grad, axis=0, keepdims=True)
        scale_sum = scale_sum + jnp.sum(grad * unit, axis=0, keepdims=True)
        if j == 0:
            up_grad[...] = contract(second_all[...].reshape(length, width), before_all[...].reshape(length, -1), 0, 0).astype(BF16)
        if j == 1:
            down_grad[...] = contract(feed_back_all[...].reshape(length, width), hidden_all[...].reshape(length, -1), 0, 0).astype(BF16)
    sums[...] = jnp.concatenate([gate_sum, shift_sum, scale_sum], axis=1)
    for j in range(chunks):
        feed.settle(j)
    gather_back.across(0)

    def mix(i, _):
        @pl.when(i == 1)
        def _():
            for c in range(chunks):
                gather_back.partner(c)

        @pl.when(i == 2)
        def _():
            gather_back.across(1)

        @pl.when(i == 3)
        def _():
            for c in range(chunks):
                gather_back.diagonal(c)

        slot = flip_by(me, i)
        here = block_at(slot, rows)
        value = contract(out_full[...], back_all[slot], 1, 1).astype(BF16)
        for h in range(heads):
            mixed_back[h, :, here] = value[h * HD : (h + 1) * HD]
        return 0

    lax.fori_loop(0, 4, mix, 0)
    out_grad[...] = contract(
        back_all[...].reshape(length, width), mixed_t[...].reshape(heads * HD, length), 0, 1
    ).astype(BF16)
    gather.close()
    gather_back.close()
    scatter.close()
    feed.close()


def feed_forward(
    sizes, heads, tokens, attention, parts, up_full, down_t, up_bias, feed_back_all, cotangent, valid, mixed_t, out_full
):
    rows, width = tokens.shape
    hidden = up_full.shape[1]
    length = 4 * rows
    local = heads * HD
    chunks = 2
    vmem = pl.BlockSpec(memory_space=pltpu.VMEM)
    own = jax.ShapeDtypeStruct((rows, width), F32)
    return pl.pallas_call(
        functools.partial(feed_kernel, sizes, heads, chunks),
        out_shape=[
            own,
            own,
            jax.ShapeDtypeStruct((heads, HD, length), BF16),
            jax.ShapeDtypeStruct((width, hidden), BF16),
            jax.ShapeDtypeStruct((width, hidden), BF16),
            jax.ShapeDtypeStruct((width, local), BF16),
            jax.ShapeDtypeStruct((1, hidden), F32),
            jax.ShapeDtypeStruct((1, 3 * width), F32),
            jax.ShapeDtypeStruct((rows, width), BF16),
            own,
        ],
        in_specs=[vmem] * 11,
        out_specs=[vmem] * 10,
        scratch_shapes=[
            pltpu.VMEM((4, rows, width), BF16),
            pltpu.VMEM((4, rows, hidden), BF16),
            pltpu.VMEM((4, rows, hidden), BF16),
            pltpu.VMEM((4, rows, width), BF16),
            ColumnGather.semaphores(chunks),
            ColumnGather.semaphores(chunks),
            *ColumnScatter.scratch(rows, width, chunks),
            pltpu.VMEM((2, rows, width), BF16),
            pltpu.VMEM((2, rows, width), BF16),
            pltpu.SemaphoreType.DMA((2, 3, chunks)),
        ],
        compiler_params=pltpu.CompilerParams(
            vmem_limit_bytes=VMEM_LIMIT, collective_id=3, has_side_effects=True
        ),
    )(tokens, attention, parts, up_full, down_t, up_bias, feed_back_all, cotangent, valid, mixed_t, out_full)


def contract_exact(left, right, left_axis, right_axis):
    return lax.dot_general(
        left,
        right,
        (((left_axis,), (right_axis,)), ((), ())),
        precision=lax.Precision.HIGHEST,
        preferred_element_type=F32,
    )


def finish_kernel(
    sizes, heads, chunks,
    qkv, bias, log_total, mixed_t, back_t, cosine, sine, normed, in_t, up_source, down_source, out_source,
    tokens, middle_back, parts, others, down_part, up_part, condition_all, condition_weight,
    middle, feed_far, feed_kept, cotangent, valid, down_bias_in,
    output, tokens_back, condition_back, condition_grad, bias_grad, up_bias, down_bias, in_grad, out_grad, up_grad, down_grad,
    turned, query, key, value, back, key_sum, value_sum, in_source,
    in_total, in_out, in_in, in_sems, up_total, up_out, up_in, up_sems,
    down_total, down_out, down_in, down_sems, out_total, out_out, out_in, out_sems,
    pair_out, pair_in, far_out, far_in, kept, col_sems,
    line_out, line_in, up_all, pieces, arrived, backs, collected, tiny_sems, line_sems, feed_in, feed_sems,
):
    count = sizes["dp"] * sizes["row"]
    number = shard_number(sizes)
    length = qkv.shape[2]
    rows, width = tokens.shape
    half = HD // 2
    piece = condition_weight.shape[1]
    cond = condition_weight.shape[0]
    peers = other_peers(sizes)
    greet([peer for _, peer in peers] + col_peers())
    me = lax.axis_index("col")
    near, far = col_peers()
    scatter_up = ShardScatter(sizes, up_source, up_total, up_out, up_in, up_sems)
    scatter_down = ShardScatter(sizes, down_source, down_total, down_out, down_in, down_sems)
    scatter_out = ShardScatter(sizes, out_source, out_total, out_out, out_in, out_sems)
    scatter_in = ShardScatter(sizes, in_source, in_total, in_out, in_in, in_sems)
    column = ColumnScatter(pair_out, pair_in, far_out, far_in, kept, chunks, col_sems)

    def tiny(kind, i, source, target):
        return send_copy(source, target, tiny_sems.at[0, kind, i], tiny_sems.at[1, kind, i], peers[i][1])

    def up_copy(i, slot):
        return tiny(0, i, up_part, up_all.at[slot])

    def piece_copy(i, mine, slot):
        return tiny(1, i, pieces.at[mine], arrived.at[slot])

    def back_copy(i, mine, slot):
        return tiny(2, i, backs.at[mine], collected.at[slot])

    def line_copy(k):
        return send_copy(line_out.at[k], line_in.at[k], line_sems.at[0, k], line_sems.at[1, k], (near, far)[k])

    feed_copy = send_copy(feed_far, feed_in, feed_sems.at[0], feed_sems.at[1], far)
    feed_copy.start()
    scatter_up.start(0)
    scatter_down.start(0)
    scatter_out.start(0)
    for i in range(count - 1):
        up_copy(i, number).start()
    up_all[number] = up_part[...]

    def turn_back(values, here):
        c, s = cosine[:, here], sine[:, here]
        a, b = values[:half], values[half:]
        return jnp.concatenate([a * c + b * s, b * c - a * s], axis=0)

    for h in range(heads):
        prepare_backward(heads, h, rows, length, qkv, bias, log_total, mixed_t, back_t, query, key, value, back)
    key_sum[...] = jnp.zeros_like(key_sum)
    value_sum[...] = jnp.zeros_like(value_sum)

    def step(i, _):
        here = block_at(i, rows)
        for h in range(heads):
            q, d = query[h, :, here], back[h, :, here]
            weights = jnp.exp2(contract(key[h], q, 1, 0) * UNIT)
            grads = (weights * contract(value[h], d, 1, 0)).astype(BF16)
            value_sum[h] += contract(d[:HD], weights.astype(BF16), 1, 1)
            key_sum[h] += contract(q[:HD], grads, 1, 1)
            query_back = contract(qkv[heads + h], grads, 1, 0) * SCALE
            turned[h, :, here] = turn_back(query_back, here).astype(BF16)

        @pl.when(i == 1)
        def _():
            scatter_up.advance(1)

        @pl.when(i == 2)
        def _():
            scatter_down.advance(1)
            scatter_out.advance(1)
            scatter_up.advance(2)

        return 0

    lax.fori_loop(0, 4, step, 0)

    def finish_block(i, _):
        here = block_at(i, rows)
        for h in range(heads):
            turned[heads + h, :, here] = turn_back(key_sum[h, :, here] * SCALE, here).astype(BF16)
            turned[2 * heads + h, :, here] = value_sum[h, :, here].astype(BF16)
        return 0

    lax.fori_loop(0, 4, finish_block, 0)
    scatter_down.advance(2)
    scatter_out.advance(2)
    in_source[...] = contract(
        normed[...], turned[...].reshape(3 * heads * HD, length), 0, 1
    ).astype(BF16)
    scatter_in.start(0)
    size = rows // chunks

    def part_of(slot, j):
        start_at = pl.multiple_of(slot * rows + j * size, size)
        block = turned[:, :, pl.ds(start_at, size)].reshape(3 * heads * HD, size)
        return contract(block, in_t[...], 0, 0)

    for j in range(chunks):
        column.give_diagonal(j, part_of(flips(me, (1, 2)), j))
    for j in range(chunks):
        column.give_across(j, part_of(flip(me, 2), j))
    scatter_up.advance(3)
    for j in range(chunks):
        column.give_partner(j, part_of(flip(me, 1), j))
    scatter_in.advance(1)
    for j in range(chunks):
        column.give_own(j, part_of(me, j))
    scatter_down.advance(3)
    scatter_out.advance(3)
    scatter_in.advance(2)
    shift_sum = jnp.zeros((1, width), F32)
    scale_sum = jnp.zeros((1, width), F32)
    gate_sum = jnp.zeros((1, width), F32)
    feed_copy.wait_recv()
    for j in range(chunks):
        here = pl.ds(j * size, size)
        feed = feed_kept[here, :] + feed_in[here, :].astype(F32) + down_bias_in[...]
        output[here, :] = middle[here, :] + parts[5:6, :] * feed
        gate_sum = gate_sum + jnp.sum(cotangent[here, :] * valid[here, :] * feed, axis=0, keepdims=True)
    for j in range(chunks):
        here = pl.ds(j * size, size)
        own = tokens[here, :]
        center = own - jnp.mean(own, axis=-1, keepdims=True)
        inverse = lax.rsqrt(jnp.mean(center * center, axis=-1, keepdims=True) + EPSILON)
        unit = center * inverse
        grad = column.result(j)
        scaled = grad * (1.0 + parts[1:2, :])
        inner = scaled - jnp.mean(scaled, axis=-1, keepdims=True) - unit * jnp.mean(scaled * unit, axis=-1, keepdims=True)
        tokens_back[here, :] = middle_back[here, :] + inverse * inner
        shift_sum = shift_sum + jnp.sum(grad, axis=0, keepdims=True)
        scale_sum = scale_sum + jnp.sum(grad * unit, axis=0, keepdims=True)
    line_out[0] = jnp.concatenate([shift_sum, scale_sum, others[...], gate_sum, down_part[...]], axis=1)
    line_copy(0).start()
    scatter_in.advance(3)
    steps = len(scatter_in.steps)
    for k in range(4, steps + 1):
        for one in (scatter_up, scatter_down, scatter_out, scatter_in):
            one.advance(k)
    line_copy(0).wait_recv()
    line_out[1] = line_out[0] + line_in[0]
    line_copy(1).start()
    up_grad[...] = scatter_up.result()
    down_grad[...] = scatter_down.result()
    out_grad[...] = scatter_out.result()
    in_grad[...] = scatter_in.result()
    for i in range(count - 1):
        up_copy(i, peers[i][0]).wait_recv()
    up_bias[...] = jnp.sum(jnp.concatenate([up_all[b] for b in range(count)], axis=0), axis=0, keepdims=True)
    line_copy(1).wait_recv()
    line = line_out[1] + line_in[1]
    split = 6 * width
    for b in range(count):
        pieces[b] = jnp.concatenate([line[:, b * piece : (b + 1) * piece], line[:, split:]], axis=1)
    for i in range(count - 1):
        piece_copy(i, peers[i][0], number).start()
    arrived[number] = pieces[number]
    for i in range(count - 1):
        piece_copy(i, number, peers[i][0]).wait_recv()
    stacked = jnp.concatenate([arrived[b] for b in range(count)], axis=0)
    mine = stacked[:, :piece]
    down_bias[...] = jnp.sum(stacked[:, piece:], axis=0, keepdims=True)
    bias_piece = jnp.sum(mine, axis=0, keepdims=True)
    back_rows = contract_exact(mine, condition_weight[...].astype(F32), 1, 1)
    for b in range(count):
        backs[b] = jnp.concatenate([back_rows[b : b + 1], bias_piece], axis=1)
    for i in range(count - 1):
        back_copy(i, peers[i][0], number).start()
    collected[number] = backs[number]
    conditions = jnp.concatenate([condition_all[b] for b in range(count)], axis=0)
    condition_grad[...] = contract_exact(conditions, mine, 0, 0)
    for i in range(count - 1):
        back_copy(i, number, peers[i][0]).wait_recv()
    gathered = [collected[b] for b in range(count)]
    bias_grad[...] = jnp.concatenate([one[:, cond:] for one in gathered], axis=1)
    condition_back[...] = jnp.sum(
        jnp.concatenate([one[:, :cond] for one in gathered], axis=0), axis=0, keepdims=True
    )
    for i in range(count - 1):
        up_copy(i, number).wait_send()
        piece_copy(i, peers[i][0], number).wait_send()
        back_copy(i, peers[i][0], number).wait_send()
    for k in range(2):
        line_copy(k).wait_send()
    feed_copy.wait_send()
    for one in (scatter_up, scatter_down, scatter_out, scatter_in):
        one.close()
    column.close()


def finish(sizes, heads, qkv, bias, log_total, mixed_t, back_t, cosine, sine, normed, in_t, up_source, down_source,
           out_source, tokens, middle_back, parts, others, down_part, up_part, condition_all, condition_weight,
           middle, feed_far, feed_kept, cotangent, valid, down_bias):
    count = sizes["dp"] * sizes["row"]
    length = qkv.shape[2]
    rows, width = tokens.shape
    chunks = 2
    local = heads * HD
    hidden = up_source.shape[1]
    cond, piece = condition_weight.shape
    share = width // count
    vmem = pl.BlockSpec(memory_space=pltpu.VMEM)
    return pl.pallas_call(
        functools.partial(finish_kernel, sizes, heads, chunks),
        out_shape=[
            jax.ShapeDtypeStruct((rows, width), F32),
            jax.ShapeDtypeStruct((rows, width), F32),
            jax.ShapeDtypeStruct((1, cond), F32),
            jax.ShapeDtypeStruct((cond, piece), F32),
            jax.ShapeDtypeStruct((1, 6 * width), F32),
            jax.ShapeDtypeStruct((1, hidden), F32),
            jax.ShapeDtypeStruct((1, width), F32),
            jax.ShapeDtypeStruct((share, 3 * local), F32),
            jax.ShapeDtypeStruct((share, local), F32),
            jax.ShapeDtypeStruct((share, hidden), F32),
            jax.ShapeDtypeStruct((share, hidden), F32),
        ],
        in_specs=[vmem] * 26,
        out_specs=[vmem] * 11,
        scratch_shapes=[
            pltpu.VMEM((3 * heads, HD, length), BF16),
            pltpu.VMEM((heads, AUG, length), BF16),
            pltpu.VMEM((heads, length, AUG), BF16),
            pltpu.VMEM((heads, length, AUG), BF16),
            pltpu.VMEM((heads, AUG, length), BF16),
            pltpu.VMEM((heads, HD, length), F32),
            pltpu.VMEM((heads, HD, length), F32),
            pltpu.VMEM((width, 3 * local), BF16),
            *ShardScatter.scratch(count, share, 3 * local),
            *ShardScatter.scratch(count, share, hidden),
            *ShardScatter.scratch(count, share, hidden),
            *ShardScatter.scratch(count, share, local),
            *ColumnScatter.scratch(rows, width, chunks),
            pltpu.VMEM((2, 1, 7 * width), F32),
            pltpu.VMEM((2, 1, 7 * width), F32),
            pltpu.VMEM((count, 1, hidden), F32),
            pltpu.VMEM((count, 1, piece + width), F32),
            pltpu.VMEM((count, 1, piece + width), F32),
            pltpu.VMEM((count, 1, cond + piece), F32),
            pltpu.VMEM((count, 1, cond + piece), F32),
            pltpu.SemaphoreType.DMA((2, 3, count - 1)),
            pltpu.SemaphoreType.DMA((2, 2)),
            pltpu.VMEM((rows, width), BF16),
            pltpu.SemaphoreType.DMA((2,)),
        ],
        compiler_params=pltpu.CompilerParams(
            vmem_limit_bytes=VMEM_LIMIT, collective_id=2, has_side_effects=True
        ),
    )(qkv, bias, log_total, mixed_t, back_t, cosine, sine, normed, in_t, up_source, down_source, out_source,
      tokens, middle_back, parts, others, down_part, up_part, condition_all, condition_weight,
      middle, feed_far, feed_kept, cotangent, valid, down_bias)


def shards(
    sizes,
    tokens,
    condition,
    lengths,
    condition_weight,
    condition_bias,
    attention_in,
    attention_out,
    up_weight,
    up_bias,
    down_weight,
    down_bias,
    cotangent,
):
    columns = lax.axis_size("col")
    column_index = lax.axis_index("col")
    rows = tokens.shape[1]
    width = tokens.shape[2]
    length_all = rows * columns
    local_width = attention_in.shape[2]
    heads = local_width // HD
    in_shard = attention_in.reshape(attention_in.shape[0], 3 * local_width).astype(BF16)
    out_shard = attention_out.T.astype(BF16)
    up_shard = up_weight.astype(BF16)
    down_shard = down_weight.T.astype(BF16)
    condition_low = condition.astype(BF16)
    weight_low = condition_weight.astype(BF16)
    own_rows = tokens[0]
    length = lengths[0]
    position = column_index * rows + jnp.arange(rows)
    valid = (position < length).astype(F32)
    bias = jnp.where(jnp.arange(length_all) < length, 0.0, MASKED).astype(F32)[None]
    cosine, sine = (jnp.asarray(table) for table in rotary_tables(length_all))
    parts, normed_blocks, qkv, out_full, feed_back, down_bias_part, in_t, condition_all = start(
        sizes, heads, condition_low.astype(F32), weight_low, condition_bias[None], own_rows,
        in_shard, out_shard, cosine, sine, cotangent[0], valid[:, None],
    )
    normed_all = normed_blocks.reshape(length_all, width)
    attention, mixed_t, log_total, feed_back_blocks, up_full, down_t = attend(
        sizes, heads, qkv, bias, out_full, feed_back, up_shard, down_shard
    )
    hidden_cols = up_full.shape[1]
    bias_part = lax.dynamic_slice_in_dim(up_bias, column_index * hidden_cols, hidden_cols)
    (
        middle, middle_back, mixed_back, up_grad, down_grad, out_grad, up_bias_part, others, feed_far, feed_kept
    ) = feed_forward(
        sizes, heads, own_rows, attention, parts, up_full, down_t, bias_part[None], feed_back_blocks,
        cotangent[0], valid[:, None], mixed_t, out_full,
    )
    (
        result, tokens_back, condition_back, condition_grad, bias_grad, up_bias_grad, down_bias_grad,
        in_grad, out_grad, up_grad, down_grad,
    ) = finish(
        sizes, heads, qkv, bias, log_total, mixed_t, mixed_back,
        cosine, sine, normed_all, in_t, up_grad, down_grad, out_grad, own_rows, middle_back, parts,
        others, down_bias_part, up_bias_part, condition_all, weight_low,
        middle, feed_far, feed_kept, cotangent[0], valid[:, None], down_bias[None],
    )
    return (
        result[None],
        tokens_back[None],
        condition_back,
        condition_grad,
        bias_grad[0],
        in_grad.reshape(attention_in.shape),
        out_grad.T,
        up_grad,
        up_bias_grad[0],
        down_grad.T,
        down_bias_grad[0],
    )


def solution(mesh):
    sizes = {axis: mesh.shape[axis] for axis in ("dp", "row", "col")}
    in_specs = (
        P(("dp", "row"), "col", None),
        P(("dp", "row"), None),
        P(("dp", "row")),
        P(None, ("dp", "row")),
        P(),
        P(("dp", "row"), None, "col"),
        P("col", ("dp", "row")),
        P(("dp", "row"), "col"),
        P(),
        P("col", ("dp", "row")),
        P(),
        P(("dp", "row"), "col", None),
    )
    out_specs = (
        P(("dp", "row"), "col", None),
        P(("dp", "row"), "col", None),
        P(("dp", "row"), None),
        P(None, ("dp", "row")),
        P(),
        P(("dp", "row"), None, "col"),
        P("col", ("dp", "row")),
        P(("dp", "row"), "col"),
        P("col"),
        P("col", ("dp", "row")),
        P(),
    )
    return jax.shard_map(functools.partial(shards, sizes), mesh=mesh, in_specs=in_specs, out_specs=out_specs, check_vma=False)
```

```python
import functools
import math

import jax
import jax.numpy as jnp
import numpy as np
from jax import lax
from jax.experimental import pallas as pl
from jax.experimental.pallas import tpu as pltpu
from jax.sharding import PartitionSpec as P

HD = 64
AUG = 128
EPSILON = 1e-06
MASKED = -1e30
CUBIC = 0.044715
SLOPE = math.sqrt(2.0 / math.pi)
SCALE = 1.0 / math.sqrt(HD)
UNIT = SCALE * math.log2(math.e)
F32 = jnp.float32
BF16 = jnp.bfloat16
VMEM_LIMIT = 67043328


def layer_norm(values):
    center = values - jnp.mean(values, axis=-1, keepdims=True)
    spread = jnp.mean(center * center, axis=-1, keepdims=True)
    return center * lax.rsqrt(spread + EPSILON)


def rotary_tables(length):
    half = HD // 2
    exponent = np.arange(half, dtype=np.float32) * np.float32(2.0 / HD)
    frequency = np.exp(np.float32(-math.log(10000.0)) * exponent).astype(np.float32)
    angle = frequency[:, None] * np.arange(length, dtype=np.float32)[None, :]
    angle = angle.astype(np.float32).astype(np.float64)
    return np.cos(angle).astype(np.float32), np.sin(angle).astype(np.float32)


def contract(left, right, left_axis, right_axis):
    return lax.dot_general(
        left,
        right,
        (((left_axis,), (right_axis,)), ((), ())),
        preferred_element_type=F32,
    )


def block_at(index, size):
    return pl.ds(pl.multiple_of(index * size, size), size)


def split_three(values):
    high = values.astype(BF16)
    rest = values - high.astype(F32)
    middle = rest.astype(BF16)
    low = (rest - middle.astype(F32)).astype(BF16)
    return high.astype(F32), middle.astype(F32), low.astype(F32)


def augment(rows, extras):
    n = rows.shape[1]
    extras = [jnp.broadcast_to(e, (1, n)) for e in extras]
    pad = jnp.zeros((AUG - HD - len(extras), n), F32)
    return jnp.concatenate([rows] + extras + [pad], axis=0)


def attend_block(heads, here, query, key, value_t, mixed_t, log_total):
    scores = [contract(key[h], query[h, :, here], 1, 0) for h in range(heads)]
    for h in range(heads):
        top = jnp.max(scores[h], axis=0, keepdims=True)
        weights = jnp.exp2((scores[h] - top) * UNIT)
        total = jnp.sum(weights, axis=0, keepdims=True)
        out = contract(value_t[h], weights.astype(BF16), 1, 0) * (1.0 / total)
        mixed_t[h, :, here] = out.astype(BF16)
        log_total[h, :, here] = top * UNIT + jnp.log2(total)


def prepare_backward(heads, h, size, length, qkv, bias, log_total, mixed_t, back_t, query, key, value, back):
    def step(i, _):
        here = block_at(i, size)
        one = jnp.ones((1, size), F32)
        zero = jnp.zeros((1, size), F32)
        logs = split_three(log_total[h, :, here] * (-1.0 / UNIT))
        query[h, :, here] = augment(qkv[h, :, here].astype(F32), [one, *logs]).astype(BF16)
        keys = augment(qkv[heads + h, :, here].astype(F32), [bias[:, here], one, one, one])
        key[h, here, :] = keys.T.astype(BF16)
        values = augment(qkv[2 * heads + h, :, here].astype(F32), [zero, one, one, one])
        value[h, here, :] = values.T.astype(BF16)
        grad = back_t[h, :, here].astype(F32)
        center = jnp.sum(grad * mixed_t[h, :, here].astype(F32), axis=0, keepdims=True)
        back[h, :, here] = augment(grad, [zero, *split_three(-center)]).astype(BF16)
        return 0

    lax.fori_loop(0, length // size, step, 0)


MESH = pl.DeviceIdType.MESH


def flip(index, bit):
    return index + bit - 2 * bit * lax.rem(lax.div(index, bit), 2)


def flips(index, bits):
    for bit in bits:
        index = flip(index, bit)
    return index


def doubling(sizes):
    steps = []
    for axis, stride in (("dp", sizes["row"]), ("row", 1)):
        bit = sizes[axis] // 2
        while bit:
            steps.append((axis, bit, bit * stride))
            bit //= 2
    return steps


def subsets(bits):
    out = [()]
    for bit in bits:
        out = out + [kept + (bit,) for kept in out]
    return out


def send_copy(source, target, send, receive, peer):
    return pltpu.make_async_remote_copy(
        src_ref=source, dst_ref=target, send_sem=send, recv_sem=receive, device_id=peer, device_id_type=MESH
    )


def greet(peers):
    barrier = pltpu.get_barrier_semaphore()
    for peer in peers:
        pl.semaphore_signal(barrier, inc=1, device_id=peer, device_id_type=MESH)
    pl.semaphore_wait(barrier, len(peers))


def shard_number(sizes):
    return lax.axis_index("dp") * sizes["row"] + lax.axis_index("row")


def doubling_peers(sizes):
    return [{axis: flip(lax.axis_index(axis), bit)} for axis, bit, _ in doubling(sizes)]


def neighbour_peers(sizes):
    z = lax.axis_index("dp")
    n, m = sizes["dp"], sizes["row"]
    peers = [{"dp": lax.rem(z + 1, n)}, {"dp": lax.rem(z + n - 1, n)}]
    bit = m // 2
    while bit:
        peers.append({"row": flip(lax.axis_index("row"), bit)})
        bit //= 2
    return peers


def col_peers():
    me = lax.axis_index("col")
    return [{"col": flip(me, 1)}, {"col": flip(me, 2)}]


class ShardGather:
    def __init__(self, sizes, shard, full, sems):
        self.n, self.m = sizes["dp"], sizes["row"]
        self.rows = shard.shape[0]
        self.shard, self.full, self.sems = shard, full, sems
        self.z, self.y = lax.axis_index("dp"), lax.axis_index("row")

    def slot(self, z, y):
        return self.full.at[pl.ds(pl.multiple_of((z * self.m + y) * self.rows, self.rows), self.rows), :]

    def held(self, side, h):
        z = self.z - side * h
        return z, (z >= 0) if side > 0 else (z < self.n)

    def onward(self, side):
        return (self.z + 1 < self.n) if side > 0 else (self.z > 0)

    def stream(self, side, h, arriving):
        z, _ = self.held(side, h if arriving else h - 1)
        at = (h - 1) + (self.n - 1 if side < 0 else 0)
        source = self.slot(z, self.y) if arriving or h > 1 else self.shard
        peer = {"dp": self.z + (side if not arriving else -side)}
        return send_copy(source, self.slot(z, self.y), self.sems.at[0, at], self.sems.at[1, at], peer)

    def over(self, side, h, arriving):
        z, _ = self.held(side, h)
        bit = self.m // 2
        at = 2 * (self.n - 1) + h + (self.n - 1 if side < 0 and h else 0)
        there = self.slot(z, flip(self.y, bit) if arriving else self.y)
        source = self.shard if h == 0 and not arriving else there
        return send_copy(source, there, self.sems.at[0, at], self.sems.at[1, at], {"row": flip(self.y, bit)})

    def keep(self):
        self.slot(self.z, self.y)[...] = self.shard[...]

    def start(self):
        for side in (1, -1):

            @pl.when(self.onward(side))
            def _():
                self.stream(side, 1, False).start()

        self.over(1, 0, False).start()

    def advance(self, h):
        if h >= self.n:
            return
        for side in (1, -1):
            _, here = self.held(side, h)

            @pl.when(here)
            def _():
                self.stream(side, h, True).wait_recv()

            if h + 1 < self.n:

                @pl.when(jnp.logical_and(here, self.onward(side)))
                def _():
                    self.stream(side, h + 1, False).start()

            @pl.when(here)
            def _():
                self.over(side, h, False).start()

    def others(self):
        out, held, at = [], (self.m // 2,), 4 * self.n - 3
        bit = self.m // 4
        while bit:
            kept = subsets(held)
            out.append((bit, kept, at))
            at += self.n * len(kept)
            held = held + (bit,)
            bit //= 2
        return out

    def spread(self, bit, kept, at, arriving):
        peer = {"row": flip(self.y, bit)}
        for z in range(self.n):
            for i, bits in enumerate(kept):
                there = self.slot(z, flips(self.y, bits + ((bit,) if arriving else ())))
                k = at + z * len(kept) + i
                yield send_copy(there, there, self.sems.at[0, k], self.sems.at[1, k], peer)

    def finish(self):
        self.over(1, 0, True).wait_recv()
        for side in (1, -1):
            for h in range(1, self.n):

                @pl.when(self.held(side, h)[1])
                def _():
                    self.over(side, h, True).wait_recv()

        for step in self.others():
            for copy in self.spread(*step, False):
                copy.start()
            for copy in self.spread(*step, True):
                copy.wait_recv()

    def close(self):
        self.over(1, 0, False).wait_send()
        for side in (1, -1):
            for h in range(1, self.n):
                _, here = self.held(side, h)

                @pl.when(jnp.logical_and(self.held(side, h - 1)[1], self.onward(side)))
                def _():
                    self.stream(side, h, False).wait_send()

                @pl.when(here)
                def _():
                    self.over(side, h, False).wait_send()

        for step in self.others():
            for copy in self.spread(*step, False):
                copy.wait_send()

    @staticmethod
    def semaphores(sizes):
        n, m = sizes["dp"], sizes["row"]
        return pltpu.SemaphoreType.DMA((2, 4 * n - 3 + n * max(m - 2, 0)))


class ShardScatter:
    def __init__(self, sizes, source, total, out_buf, in_buf, sems):
        self.steps = doubling(sizes)[::-1]
        self.rows = out_buf.shape[1]
        self.source, self.total, self.out_buf, self.in_buf, self.sems = source, total, out_buf, in_buf, sems
        self.me = shard_number(sizes)
        self.first = [0]
        for k in range(len(self.steps)):
            self.first.append(self.first[-1] + 2 ** (len(self.steps) - 1 - k))

    def part(self, number):
        return pl.ds(pl.multiple_of(number * self.rows, self.rows), self.rows)

    def rest(self, k):
        return subsets([s[2] for s in self.steps[k + 1 :]])

    def copy(self, k, i):
        axis, bit, _ = self.steps[k]
        at = self.first[k] + i
        peer = {axis: flip(lax.axis_index(axis), bit)}
        return send_copy(self.out_buf.at[at], self.in_buf.at[at], self.sems.at[0, at], self.sems.at[1, at], peer)

    def held(self, k):
        return self.source if k == 0 else self.total

    def start(self, k):
        stride = self.steps[k][2]
        for i, kept in enumerate(self.rest(k)):
            number = flips(self.me, (stride,) + kept)
            self.out_buf[self.first[k] + i] = self.held(k)[self.part(number), :].astype(BF16)
            self.copy(k, i).start()

    def arrived(self, k):
        for i, kept in enumerate(self.rest(k)):
            self.copy(k, i).wait_recv()
            here = self.part(flips(self.me, kept))
            self.total[here, :] = self.held(k)[here, :].astype(F32) + self.in_buf[self.first[k] + i].astype(F32)

    def advance(self, k):
        if 0 < k <= len(self.steps):
            self.arrived(k - 1)
        if k < len(self.steps):
            self.start(k)

    def result(self):
        return self.total[self.part(self.me), :]

    def close(self):
        for k in range(len(self.steps)):
            for i in range(len(self.rest(k))):
                self.copy(k, i).wait_send()

    @staticmethod
    def scratch(count, rows, width):
        return [
            pltpu.VMEM((count * rows, width), F32),
            pltpu.VMEM((count - 1, rows, width), BF16),
            pltpu.VMEM((count - 1, rows, width), BF16),
            pltpu.SemaphoreType.DMA((2, count - 1)),
        ]


class ColumnGather:
    def __init__(self, full, chunks, sems):
        self.full, self.chunks, self.sems = full, chunks, sems
        self.me = lax.axis_index("col")
        self.rows = full.shape[1] // chunks

    def chunk(self, slot, j):
        return self.full.at[slot, pl.ds(j * self.rows, self.rows), :]

    def copy(self, kind, j, slot):
        peer = {"col": flip(self.me, 2 if kind == 1 else 1)}
        here = self.chunk(slot, j)
        return send_copy(here, here, self.sems.at[0, kind, j], self.sems.at[1, kind, j], peer)

    def start(self, j):
        for kind in (1, 0):
            copy = self.copy(kind, j, self.me)
            copy.start()

    def partner(self, j):
        self.copy(0, j, flip(self.me, 1)).wait_recv()

    def across(self, j):
        there = flip(self.me, 2)
        self.copy(1, j, there).wait_recv()
        copy = self.copy(2, j, there)
        copy.start()

    def diagonal(self, j):
        self.copy(2, j, flips(self.me, (1, 2))).wait_recv()

    def close(self):
        for j in range(self.chunks):
            for kind in range(3):
                self.copy(kind, j, self.me).wait_send()

    @staticmethod
    def semaphores(chunks):
        return pltpu.SemaphoreType.DMA((2, 3, chunks))


class ColumnScatter:
    def __init__(self, pair_out, pair_in, far_out, far_in, kept, chunks, sems):
        self.pair_out, self.pair_in, self.far_out, self.far_in = pair_out, pair_in, far_out, far_in
        self.kept, self.chunks, self.sems = kept, chunks, sems
        self.rows = kept.shape[0] // chunks
        me = lax.axis_index("col")
        self.near, self.far = {"col": flip(me, 1)}, {"col": flip(me, 2)}

    def at(self, j):
        return pl.ds(j * self.rows, self.rows)

    def pair(self, which, j):
        return send_copy(
            self.pair_out.at[which, self.at(j), :],
            self.pair_in.at[which, self.at(j), :],
            self.sems.at[0, which, j],
            self.sems.at[1, which, j],
            self.near,
        )

    def cross(self, j):
        return send_copy(
            self.far_out.at[self.at(j), :],
            self.far_in.at[self.at(j), :],
            self.sems.at[0, 2, j],
            self.sems.at[1, 2, j],
            self.far,
        )

    def begin(self, copy):
        copy.start()

    def give_diagonal(self, j, value):
        self.pair_out[1, self.at(j), :] = value.astype(BF16)
        self.begin(self.pair(1, j))

    def give_across(self, j, value):
        self.pair(1, j).wait_recv()
        self.far_out[self.at(j), :] = (value + self.pair_in[1, self.at(j), :].astype(F32)).astype(BF16)
        if self.far_in is not None:
            self.begin(self.cross(j))

    def give_partner(self, j, value):
        self.pair_out[0, self.at(j), :] = value.astype(BF16)
        self.begin(self.pair(0, j))

    def give_own(self, j, value):
        self.kept[self.at(j), :] = value

    def settle(self, j):
        self.pair(0, j).wait_recv()
        self.kept[self.at(j), :] = self.kept[self.at(j), :] + self.pair_in[0, self.at(j), :].astype(F32)

    def result(self, j):
        self.pair(0, j).wait_recv()
        self.cross(j).wait_recv()
        near = self.kept[self.at(j), :] + self.pair_in[0, self.at(j), :].astype(F32)
        return near + self.far_in[self.at(j), :].astype(F32)

    def close(self):
        for j in range(self.chunks):
            self.pair(0, j).wait_send()
            self.pair(1, j).wait_send()
            if self.far_in is not None:
                self.cross(j).wait_send()

    @staticmethod
    def scratch(rows, width, chunks):
        return [
            pltpu.VMEM((2, rows, width), BF16),
            pltpu.VMEM((2, rows, width), BF16),
            pltpu.VMEM((rows, width), BF16),
            pltpu.VMEM((rows, width), BF16),
            pltpu.VMEM((rows, width), F32),
            pltpu.SemaphoreType.DMA((2, 3, chunks)),
        ]


def other_peers(sizes):
    number = shard_number(sizes)
    total = sizes["dp"] * sizes["row"]
    bits = [stride for _, _, stride in doubling(sizes)]
    out = []
    for kept in subsets(bits)[1:]:
        peer = {}
        for axis, bit, stride in doubling(sizes):
            if stride in kept:
                peer[axis] = flip(peer.get(axis, lax.axis_index(axis)), bit)
        out.append((flips(number, kept), peer))
    assert len(out) == total - 1
    return out


def start_kernel(
    sizes, heads, chunks,
    condition, condition_weight, condition_bias, tokens, in_shard, out_shard, cosine, sine, cotangent, valid,
    modulation, normed, qkv, out_full, feed_back, bias_part, in_t, condition_all,
    pieces, arrived, in_full, out_t, unit, sems_tiny, sems_in, sems_out, sems_col,
):
    count = sizes["dp"] * sizes["row"]
    number = shard_number(sizes)
    rows, width = tokens.shape
    others = other_peers(sizes)
    greet([peer for _, peer in others] + col_peers())
    gather_in = ShardGather(sizes, in_shard, in_full, sems_in)
    gather_out = ShardGather(sizes, out_shard, out_t, sems_out)
    gather_col = ColumnGather(normed, chunks, sems_col)

    def condition_copy(i, slot):
        return send_copy(
            condition, condition_all.at[slot], sems_tiny.at[0, i], sems_tiny.at[1, i], others[i][1]
        )

    def piece_copy(i, mine, slot):
        return send_copy(
            pieces.at[mine], arrived.at[slot], sems_tiny.at[2, i], sems_tiny.at[3, i], others[i][1]
        )

    for i in range(count - 1):
        condition_copy(i, number).start()
    gather_in.start()
    gather_out.start()
    condition_all[number] = condition[...]
    gather_in.keep()
    gather_out.keep()
    size = rows // chunks

    def normal(j, _):
        here = block_at(j, size)
        unit[here, :] = layer_norm(tokens[here, :])
        return 0

    lax.fori_loop(0, chunks, normal, 0)
    for i in range(count - 1):
        condition_copy(i, others[i][0]).wait_recv()
    stacked = jnp.concatenate([condition_all[b] for b in range(count)], axis=0)
    product = contract(stacked.astype(BF16), condition_weight[...], 1, 0)
    for b in range(count):
        pieces[b] = product[b : b + 1]
    for i in range(count - 1):
        piece_copy(i, others[i][0], number).start()
    arrived[number] = pieces[number]
    gather_in.advance(1)
    gather_out.advance(1)
    for i in range(count - 1):
        piece_copy(i, number, others[i][0]).wait_recv()
    line = jnp.concatenate([arrived[b] for b in range(count)], axis=1) + condition_bias[...]
    parts = [line[:, t * width : (t + 1) * width] for t in range(6)]
    for t in range(6):
        modulation[t : t + 1, :] = parts[t]
    for j in range(chunks):
        here = pl.ds(j * size, size)
        value = unit[here, :] * (1.0 + parts[1]) + parts[0]
        normed[gather_col.me, here, :] = value.astype(BF16)
        gather_col.start(j)
    gather_in.advance(2)
    gather_out.advance(2)
    gather_in.advance(3)
    gather_out.advance(3)
    total = jnp.zeros((1, width), F32)
    for j in range(chunks):
        here = pl.ds(j * size, size)
        value = parts[5] * (cotangent[here, :] * valid[here, :])
        feed_back[here, :] = value.astype(BF16)
        total = total + jnp.sum(value, axis=0, keepdims=True)
    bias_part[...] = total
    for k in range(4, sizes["dp"]):
        gather_in.advance(k)
        gather_out.advance(k)
    gather_in.finish()
    gather_out.finish()
    in_t[...] = in_full[...].astype(F32).T.astype(BF16)
    out_full[...] = out_t[...].astype(F32).T.astype(BF16)

    def project(slot):
        here = pl.ds(pl.multiple_of(slot * rows, rows), rows)
        both = contract(in_t[...], normed[slot], 1, 1)
        half = HD // 2
        c, s = cosine[:, here], sine[:, here]
        for h in range(heads):
            for t in range(3):
                at = (t * heads + h) * HD
                a, b = both[at : at + half], both[at + half : at + HD]
                if t < 2:
                    a, b = a * c - b * s, b * c + a * s
                qkv[t * heads + h, :, here] = jnp.concatenate([a, b], axis=0).astype(BF16)

    me = gather_col.me
    far = flip(me, 2)

    def steps_of(i, _):
        @pl.when(i == 1)
        def _():
            for j in range(chunks):
                gather_col.partner(j)

        @pl.when(i == 2)
        def _():
            for j in range(chunks):
                gather_col.across(j)

        @pl.when(i == 3)
        def _():
            for j in range(chunks):
                gather_col.diagonal(j)

        project(flip_by(me, i))
        return 0

    lax.fori_loop(0, 4, steps_of, 0)
    for i in range(count - 1):
        condition_copy(i, number).wait_send()
        piece_copy(i, others[i][0], number).wait_send()
    gather_in.close()
    gather_out.close()
    gather_col.close()


def flip_by(index, pattern):
    out = 0
    for bit in (1, 2):
        a, b = lax.rem(lax.div(index, bit), 2), lax.rem(lax.div(pattern, bit), 2)
        out = out + bit * (a + b - 2 * a * b)
    return out


def start(sizes, heads, condition, condition_weight, condition_bias, tokens, in_shard, out_shard, cosine, sine, cotangent, valid):
    count = sizes["dp"] * sizes["row"]
    rows, width = tokens.shape
    length = cosine.shape[1]
    chunks = 2
    vmem = pl.BlockSpec(memory_space=pltpu.VMEM)
    piece = condition_weight.shape[1]
    local = heads * HD
    return pl.pallas_call(
        functools.partial(start_kernel, sizes, heads, chunks),
        out_shape=[
            jax.ShapeDtypeStruct((6, width), F32),
            jax.ShapeDtypeStruct((4, rows, width), BF16),
            jax.ShapeDtypeStruct((3 * heads, HD, length), BF16),
            jax.ShapeDtypeStruct((local, width), BF16),
            jax.ShapeDtypeStruct((rows, width), BF16),
            jax.ShapeDtypeStruct((1, width), F32),
            jax.ShapeDtypeStruct((3 * local, width), BF16),
            jax.ShapeDtypeStruct((count,) + condition.shape, F32),
        ],
        in_specs=[vmem] * 10,
        out_specs=[vmem] * 8,
        scratch_shapes=[
            pltpu.VMEM((count, 1, piece), F32),
            pltpu.VMEM((count, 1, piece), F32),
            pltpu.VMEM((width, 3 * local), BF16),
            pltpu.VMEM((width, local), BF16),
            pltpu.VMEM((rows, width), F32),
            pltpu.SemaphoreType.DMA((4, count - 1)),
            ShardGather.semaphores(sizes),
            ShardGather.semaphores(sizes),
            ColumnGather.semaphores(chunks),
        ],
        compiler_params=pltpu.CompilerParams(
            vmem_limit_bytes=VMEM_LIMIT, collective_id=0, has_side_effects=True
        ),
    )(condition, condition_weight, condition_bias, tokens, in_shard, out_shard, cosine, sine, cotangent, valid)


def attention_kernel(
    sizes, heads, chunks,
    qkv, bias, out_full, feed_back, up_shard, down_shard,
    attention, mixed_t, log_total, feed_back_all, up_full, down_t,
    query, key, up_low, down_low,
    pair_out, pair_in, far_out, far_in, kept, sems_scatter, sems_col, sems_up, sems_down,
):
    rows = feed_back.shape[0]
    length = qkv.shape[2]
    up_low[...] = up_shard[...].astype(BF16)
    down_low[...] = down_shard[...].T.astype(BF16)
    greet(neighbour_peers(sizes) + col_peers())
    gather_up = ShardGather(sizes, up_low, up_full, sems_up)
    gather_down = ShardGather(sizes, down_low, down_t, sems_down)
    gather_col = ColumnGather(feed_back_all, chunks, sems_col)
    scatter = ColumnScatter(pair_out, pair_in, far_out, far_in, kept, 1, sems_scatter)
    me = gather_col.me
    gather_up.start()
    gather_down.start()
    feed_back_all[me] = feed_back[...]
    for j in range(chunks):
        gather_col.start(j)
    gather_up.keep()
    gather_down.keep()

    def prepare(i, _):
        here = block_at(i, rows)
        one = jnp.ones((1, rows), F32)
        for h in range(heads):
            query[h, :, here] = augment(qkv[h, :, here].astype(F32), [one]).astype(BF16)
            keys = augment(qkv[heads + h, :, here].astype(F32), [bias[:, here], one, one, one])
            key[h, here, :] = keys.T.astype(BF16)
        return 0

    lax.fori_loop(0, length // rows, prepare, 0)

    def step(i, _):
        here = block_at(flip_by(me, 3 - i), rows)
        attend_block(heads, here, query, key, qkv.at[pl.ds(2 * heads, heads)], mixed_t, log_total)
        value = contract(mixed_t[:, :, here].reshape(heads * HD, rows), out_full[...], 0, 0)
        for order, give in enumerate(
            (scatter.give_diagonal, scatter.give_across, scatter.give_partner, scatter.give_own)
        ):

            @pl.when(i == order)
            def _():
                give(0, value)
                if order < 3:
                    gather_up.advance(order + 1)
                    gather_down.advance(order + 1)
                if order == 2:
                    for j in range(chunks):
                        gather_col.across(j)

        return 0

    lax.fori_loop(0, 4, step, 0)
    for k in range(4, sizes["dp"]):
        gather_up.advance(k)
        gather_down.advance(k)
    for j in range(chunks):
        gather_col.partner(j)
        gather_col.diagonal(j)
    gather_up.finish()
    gather_down.finish()
    attention[...] = scatter.result(0)
    gather_up.close()
    gather_down.close()
    gather_col.close()
    scatter.close()


def attend(sizes, heads, qkv, bias, out_full, feed_back, up_shard, down_shard):
    count = sizes["dp"] * sizes["row"]
    rows, width = feed_back.shape
    length = qkv.shape[2]
    chunks = 2
    hidden = up_shard.shape[1]
    vmem = pl.BlockSpec(memory_space=pltpu.VMEM)
    return pl.pallas_call(
        functools.partial(attention_kernel, sizes, heads, chunks),
        out_shape=[
            jax.ShapeDtypeStruct((rows, width), F32),
            jax.ShapeDtypeStruct((heads, HD, length), BF16),
            jax.ShapeDtypeStruct((heads, 1, length), F32),
            jax.ShapeDtypeStruct((4, rows, width), BF16),
            jax.ShapeDtypeStruct((width, hidden), BF16),
            jax.ShapeDtypeStruct((width, hidden), BF16),
        ],
        in_specs=[vmem] * 6,
        out_specs=[vmem] * 6,
        scratch_shapes=[
            pltpu.VMEM((heads, AUG, length), BF16),
            pltpu.VMEM((heads, length, AUG), BF16),
            pltpu.VMEM((width // count, hidden), BF16),
            pltpu.VMEM((width // count, hidden), BF16),
            *ColumnScatter.scratch(rows, width, 1),
            ColumnGather.semaphores(chunks),
            ShardGather.semaphores(sizes),
            ShardGather.semaphores(sizes),
        ],
        compiler_params=pltpu.CompilerParams(
            vmem_limit_bytes=VMEM_LIMIT, collective_id=1, has_side_effects=True
        ),
    )(qkv, bias, out_full, feed_back, up_shard, down_shard)


def feed_kernel(
    sizes, heads, chunks,
    tokens, attention, parts, up_full, down_t, up_bias, feed_back_all, cotangent, valid, mixed_t, out_full,
    middle, middle_back, mixed_back, up_grad, down_grad, out_grad, up_part, sums, feed_far, feed_kept,
    second_all, hidden_all, before_all, back_all, second_sems, back_sems,
    pair_out, pair_in, far_out, far_in, kept, scatter_sems, feed_pair_out, feed_pair_in, feed_sems,
):
    rows, width = tokens.shape
    size = rows // chunks
    length = 4 * rows
    greet(col_peers())
    gather = ColumnGather(second_all, chunks, second_sems)
    gather_back = ColumnGather(back_all, chunks, back_sems)
    scatter = ColumnScatter(pair_out, pair_in, far_out, far_in, kept, chunks, scatter_sems)
    feed = ColumnScatter(feed_pair_out, feed_pair_in, feed_far, None, feed_kept, chunks, feed_sems)
    me = gather.me
    for j in range(chunks):
        here = pl.ds(j * size, size)
        value = tokens[here, :] + parts[2:3, :] * attention[here, :]
        middle[here, :] = value
        second_all[me, here, :] = (layer_norm(value) * (1.0 + parts[4:5, :]) + parts[3:4, :]).astype(BF16)
        gather.start(j)
    up_part[...] = jnp.zeros_like(up_part)

    def block(i, _):
        late = lax.div(i, 4)
        pattern = (1 - late) * lax.div(i, 2) + late * (3 - lax.rem(i, 2))
        j = (1 - late) * lax.rem(i, 2) + late * (lax.div(i, 2) - 2)
        slot = flip_by(me, pattern)
        here = pl.ds(pl.multiple_of(j * size, size), size)

        @pl.when(i == 2)
        def _():
            for c in range(chunks):
                gather.partner(c)

        @pl.when(i == 3)
        def _():
            gather.across(0)

        @pl.when(i == 4)
        def _():
            gather.diagonal(0)

        @pl.when(i == 6)
        def _():
            gather.diagonal(1)

        before = contract(second_all[slot, here, :], up_full[...], 1, 0) + up_bias[...]
        bend = jnp.tanh(SLOPE * (before + CUBIC * before * before * before))
        hidden = (0.5 * before * (1.0 + bend)).astype(BF16)
        slope = 0.5 * (1.0 + bend) + 0.5 * before * (1.0 - bend * bend) * (SLOPE * (1.0 + 3.0 * CUBIC * before * before))
        hidden_back = contract(feed_back_all[slot, here, :], down_t[...], 1, 0)
        before_back = (hidden_back * slope).astype(BF16)
        hidden_all[slot, here, :] = hidden
        before_all[slot, here, :] = before_back
        up_part[...] += jnp.sum(before_back.astype(F32), axis=0, keepdims=True)
        back_value = contract(before_back, up_full[...], 1, 1)
        feed_value = contract(hidden, down_t[...], 1, 1)
        for at, (name, c) in enumerate(
            (("own", 0), ("own", 1), ("partner", 0), ("partner", 1), ("diagonal", 0), ("across", 0), ("diagonal", 1), ("across", 1))
        ):

            @pl.when(i == at)
            def _():
                getattr(scatter, "give_" + name)(c, back_value)
                getattr(feed, "give_" + name)(c, feed_value)
                if at == 5:
                    gather.across(1)

        return 0

    lax.fori_loop(0, 8, block, 0)
    gate_sum = jnp.zeros((1, width), F32)
    shift_sum = jnp.zeros((1, width), F32)
    scale_sum = jnp.zeros((1, width), F32)
    for j in range(chunks):
        here = pl.ds(j * size, size)
        own = middle[here, :]
        center = own - jnp.mean(own, axis=-1, keepdims=True)
        inverse = lax.rsqrt(jnp.mean(center * center, axis=-1, keepdims=True) + EPSILON)
        unit = center * inverse
        grad = scatter.result(j)
        scaled = grad * (1.0 + parts[4:5, :])
        inner = scaled - jnp.mean(scaled, axis=-1, keepdims=True) - unit * jnp.mean(scaled * unit, axis=-1, keepdims=True)
        total = cotangent[here, :] * valid[here, :] + inverse * inner
        middle_back[here, :] = total
        back_all[me, here, :] = (parts[2:3, :] * total).astype(BF16)
        gather_back.start(j)
        gate_sum = gate_sum + jnp.sum(total * attention[here, :], axis=0, keepdims=True)
        shift_sum = shift_sum + jnp.sum(grad, axis=0, keepdims=True)
        scale_sum = scale_sum + jnp.sum(grad * unit, axis=0, keepdims=True)
        if j == 0:
            up_grad[...] = contract(second_all[...].reshape(length, width), before_all[...].reshape(length, -1), 0, 0).astype(BF16)
        if j == 1:
            down_grad[...] = contract(feed_back_all[...].reshape(length, width), hidden_all[...].reshape(length, -1), 0, 0).astype(BF16)
    sums[...] = jnp.concatenate([gate_sum, shift_sum, scale_sum], axis=1)
    for j in range(chunks):
        feed.settle(j)
    gather_back.across(0)

    def mix(i, _):
        @pl.when(i == 1)
        def _():
            for c in range(chunks):
                gather_back.partner(c)

        @pl.when(i == 2)
        def _():
            gather_back.across(1)

        @pl.when(i == 3)
        def _():
            for c in range(chunks):
                gather_back.diagonal(c)

        slot = flip_by(me, i)
        here = block_at(slot, rows)
        value = contract(out_full[...], back_all[slot], 1, 1).astype(BF16)
        for h in range(heads):
            mixed_back[h, :, here] = value[h * HD : (h + 1) * HD]
        return 0

    lax.fori_loop(0, 4, mix, 0)
    out_grad[...] = contract(
        back_all[...].reshape(length, width), mixed_t[...].reshape(heads * HD, length), 0, 1
    ).astype(BF16)
    gather.close()
    gather_back.close()
    scatter.close()
    feed.close()


def feed_forward(
    sizes, heads, tokens, attention, parts, up_full, down_t, up_bias, feed_back_all, cotangent, valid, mixed_t, out_full
):
    rows, width = tokens.shape
    hidden = up_full.shape[1]
    length = 4 * rows
    local = heads * HD
    chunks = 2
    vmem = pl.BlockSpec(memory_space=pltpu.VMEM)
    own = jax.ShapeDtypeStruct((rows, width), F32)
    return pl.pallas_call(
        functools.partial(feed_kernel, sizes, heads, chunks),
        out_shape=[
            own,
            own,
            jax.ShapeDtypeStruct((heads, HD, length), BF16),
            jax.ShapeDtypeStruct((width, hidden), BF16),
            jax.ShapeDtypeStruct((width, hidden), BF16),
            jax.ShapeDtypeStruct((width, local), BF16),
            jax.ShapeDtypeStruct((1, hidden), F32),
            jax.ShapeDtypeStruct((1, 3 * width), F32),
            jax.ShapeDtypeStruct((rows, width), BF16),
            own,
        ],
        in_specs=[vmem] * 11,
        out_specs=[vmem] * 10,
        scratch_shapes=[
            pltpu.VMEM((4, rows, width), BF16),
            pltpu.VMEM((4, rows, hidden), BF16),
            pltpu.VMEM((4, rows, hidden), BF16),
            pltpu.VMEM((4, rows, width), BF16),
            ColumnGather.semaphores(chunks),
            ColumnGather.semaphores(chunks),
            *ColumnScatter.scratch(rows, width, chunks),
            pltpu.VMEM((2, rows, width), BF16),
            pltpu.VMEM((2, rows, width), BF16),
            pltpu.SemaphoreType.DMA((2, 3, chunks)),
        ],
        compiler_params=pltpu.CompilerParams(
            vmem_limit_bytes=VMEM_LIMIT, collective_id=3, has_side_effects=True
        ),
    )(tokens, attention, parts, up_full, down_t, up_bias, feed_back_all, cotangent, valid, mixed_t, out_full)


def contract_exact(left, right, left_axis, right_axis):
    return lax.dot_general(
        left,
        right,
        (((left_axis,), (right_axis,)), ((), ())),
        precision=lax.Precision.HIGHEST,
        preferred_element_type=F32,
    )


def finish_kernel(
    sizes, heads, chunks,
    qkv, bias, log_total, mixed_t, back_t, cosine, sine, normed, in_t, up_source, down_source, out_source,
    tokens, middle_back, parts, others, down_part, up_part, condition_all, condition_weight,
    middle, feed_far, feed_kept, cotangent, valid, down_bias_in,
    output, tokens_back, condition_back, condition_grad, bias_grad, up_bias, down_bias, in_grad, out_grad, up_grad, down_grad,
    turned, query, key, value, back, key_sum, value_sum, in_source,
    in_total, in_out, in_in, in_sems, up_total, up_out, up_in, up_sems,
    down_total, down_out, down_in, down_sems, out_total, out_out, out_in, out_sems,
    pair_out, pair_in, far_out, far_in, kept, col_sems,
    line_out, line_in, up_all, pieces, arrived, backs, collected, tiny_sems, line_sems, feed_in, feed_sems,
):
    count = sizes["dp"] * sizes["row"]
    number = shard_number(sizes)
    length = qkv.shape[2]
    rows, width = tokens.shape
    half = HD // 2
    piece = condition_weight.shape[1]
    cond = condition_weight.shape[0]
    peers = other_peers(sizes)
    greet([peer for _, peer in peers] + col_peers())
    me = lax.axis_index("col")
    near, far = col_peers()
    scatter_up = ShardScatter(sizes, up_source, up_total, up_out, up_in, up_sems)
    scatter_down = ShardScatter(sizes, down_source, down_total, down_out, down_in, down_sems)
    scatter_out = ShardScatter(sizes, out_source, out_total, out_out, out_in, out_sems)
    scatter_in = ShardScatter(sizes, in_source, in_total, in_out, in_in, in_sems)
    column = ColumnScatter(pair_out, pair_in, far_out, far_in, kept, chunks, col_sems)

    def tiny(kind, i, source, target):
        return send_copy(source, target, tiny_sems.at[0, kind, i], tiny_sems.at[1, kind, i], peers[i][1])

    def up_copy(i, slot):
        return tiny(0, i, up_part, up_all.at[slot])

    def piece_copy(i, mine, slot):
        return tiny(1, i, pieces.at[mine], arrived.at[slot])

    def back_copy(i, mine, slot):
        return tiny(2, i, backs.at[mine], collected.at[slot])

    def line_copy(k):
        return send_copy(line_out.at[k], line_in.at[k], line_sems.at[0, k], line_sems.at[1, k], (near, far)[k])

    feed_copy = send_copy(feed_far, feed_in, feed_sems.at[0], feed_sems.at[1], far)
    feed_copy.start()
    scatter_up.start(0)
    scatter_down.start(0)
    scatter_out.start(0)
    for i in range(count - 1):
        up_copy(i, number).start()
    up_all[number] = up_part[...]

    def turn_back(values, here):
        c, s = cosine[:, here], sine[:, here]
        a, b = values[:half], values[half:]
        return jnp.concatenate([a * c + b * s, b * c - a * s], axis=0)

    for h in range(heads):
        prepare_backward(heads, h, rows, length, qkv, bias, log_total, mixed_t, back_t, query, key, value, back)
    key_sum[...] = jnp.zeros_like(key_sum)
    value_sum[...] = jnp.zeros_like(value_sum)

    def step(i, _):
        here = block_at(i, rows)
        for h in range(heads):
            q, d = query[h, :, here], back[h, :, here]
            weights = jnp.exp2(contract(key[h], q, 1, 0) * UNIT)
            grads = (weights * contract(value[h], d, 1, 0)).astype(BF16)
            value_sum[h] += contract(d[:HD], weights.astype(BF16), 1, 1)
            key_sum[h] += contract(q[:HD], grads, 1, 1)
            query_back = contract(qkv[heads + h], grads, 1, 0) * SCALE
            turned[h, :, here] = turn_back(query_back, here).astype(BF16)

        @pl.when(i == 1)
        def _():
            scatter_up.advance(1)

        @pl.when(i == 2)
        def _():
            scatter_down.advance(1)
            scatter_out.advance(1)
            scatter_up.advance(2)

        return 0

    lax.fori_loop(0, 4, step, 0)

    def finish_block(i, _):
        here = block_at(i, rows)
        for h in range(heads):
            turned[heads + h, :, here] = turn_back(key_sum[h, :, here] * SCALE, here).astype(BF16)
            turned[2 * heads + h, :, here] = value_sum[h, :, here].astype(BF16)
        return 0

    lax.fori_loop(0, 4, finish_block, 0)
    scatter_down.advance(2)
    scatter_out.advance(2)
    size = rows // chunks

    def part_of(slot, j):
        start_at = pl.multiple_of(slot * rows + j * size, size)
        block = turned[:, :, pl.ds(start_at, size)].reshape(3 * heads * HD, size)
        return contract(block, in_t[...], 0, 0)

    for j in range(chunks):
        column.give_diagonal(j, part_of(flips(me, (1, 2)), j))
    for j in range(chunks):
        column.give_across(j, part_of(flip(me, 2), j))
    in_source[...] = contract(
        normed[...], turned[...].reshape(3 * heads * HD, length), 0, 1
    ).astype(BF16)
    scatter_in.start(0)
    scatter_up.advance(3)
    for j in range(chunks):
        column.give_partner(j, part_of(flip(me, 1), j))
    for j in range(chunks):
        column.give_own(j, part_of(me, j))
    scatter_down.advance(3)
    scatter_out.advance(3)
    shift_sum = jnp.zeros((1, width), F32)
    scale_sum = jnp.zeros((1, width), F32)
    gate_sum = jnp.zeros((1, width), F32)
    feed_copy.wait_recv()
    for j in range(chunks):
        here = pl.ds(j * size, size)
        feed = feed_kept[here, :] + feed_in[here, :].astype(F32) + down_bias_in[...]
        output[here, :] = middle[here, :] + parts[5:6, :] * feed
        gate_sum = gate_sum + jnp.sum(cotangent[here, :] * valid[here, :] * feed, axis=0, keepdims=True)
    scatter_in.advance(1)
    for j in range(chunks):
        here = pl.ds(j * size, size)
        own = tokens[here, :]
        center = own - jnp.mean(own, axis=-1, keepdims=True)
        inverse = lax.rsqrt(jnp.mean(center * center, axis=-1, keepdims=True) + EPSILON)
        unit = center * inverse
        grad = column.result(j)
        scaled = grad * (1.0 + parts[1:2, :])
        inner = scaled - jnp.mean(scaled, axis=-1, keepdims=True) - unit * jnp.mean(scaled * unit, axis=-1, keepdims=True)
        tokens_back[here, :] = middle_back[here, :] + inverse * inner
        shift_sum = shift_sum + jnp.sum(grad, axis=0, keepdims=True)
        scale_sum = scale_sum + jnp.sum(grad * unit, axis=0, keepdims=True)
    line_out[0] = jnp.concatenate([shift_sum, scale_sum, others[...], gate_sum, down_part[...]], axis=1)
    line_copy(0).start()
    scatter_in.advance(2)
    steps = len(scatter_in.steps)
    for k in range(4, steps + 1):
        for one in (scatter_up, scatter_down, scatter_out):
            one.advance(k)
    line_copy(0).wait_recv()
    line_out[1] = line_out[0] + line_in[0]
    line_copy(1).start()
    up_grad[...] = scatter_up.result()
    down_grad[...] = scatter_down.result()
    out_grad[...] = scatter_out.result()
    for i in range(count - 1):
        up_copy(i, peers[i][0]).wait_recv()
    up_bias[...] = jnp.sum(jnp.concatenate([up_all[b] for b in range(count)], axis=0), axis=0, keepdims=True)
    line_copy(1).wait_recv()
    line = line_out[1] + line_in[1]
    split = 6 * width
    for b in range(count):
        pieces[b] = jnp.concatenate([line[:, b * piece : (b + 1) * piece], line[:, split:]], axis=1)
    for i in range(count - 1):
        piece_copy(i, peers[i][0], number).start()
    arrived[number] = pieces[number]
    for i in range(count - 1):
        piece_copy(i, number, peers[i][0]).wait_recv()
    stacked = jnp.concatenate([arrived[b] for b in range(count)], axis=0)
    mine = stacked[:, :piece]
    down_bias[...] = jnp.sum(stacked[:, piece:], axis=0, keepdims=True)
    bias_piece = jnp.sum(mine, axis=0, keepdims=True)
    back_rows = contract_exact(mine, condition_weight[...].astype(F32), 1, 1)
    for b in range(count):
        backs[b] = jnp.concatenate([back_rows[b : b + 1], bias_piece], axis=1)
    for i in range(count - 1):
        back_copy(i, peers[i][0], number).start()
    collected[number] = backs[number]
    for k in range(3, steps + 1):
        scatter_in.advance(k)
    in_grad[...] = scatter_in.result()
    conditions = jnp.concatenate([condition_all[b] for b in range(count)], axis=0)
    condition_grad[...] = contract_exact(conditions, mine, 0, 0)
    for i in range(count - 1):
        back_copy(i, number, peers[i][0]).wait_recv()
    gathered = [collected[b] for b in range(count)]
    bias_grad[...] = jnp.concatenate([one[:, cond:] for one in gathered], axis=1)
    condition_back[...] = jnp.sum(
        jnp.concatenate([one[:, :cond] for one in gathered], axis=0), axis=0, keepdims=True
    )
    for i in range(count - 1):
        up_copy(i, number).wait_send()
        piece_copy(i, peers[i][0], number).wait_send()
        back_copy(i, peers[i][0], number).wait_send()
    for k in range(2):
        line_copy(k).wait_send()
    feed_copy.wait_send()
    for one in (scatter_up, scatter_down, scatter_out, scatter_in):
        one.close()
    column.close()


def finish(sizes, heads, qkv, bias, log_total, mixed_t, back_t, cosine, sine, normed, in_t, up_source, down_source,
           out_source, tokens, middle_back, parts, others, down_part, up_part, condition_all, condition_weight,
           middle, feed_far, feed_kept, cotangent, valid, down_bias):
    count = sizes["dp"] * sizes["row"]
    length = qkv.shape[2]
    rows, width = tokens.shape
    chunks = 2
    local = heads * HD
    hidden = up_source.shape[1]
    cond, piece = condition_weight.shape
    share = width // count
    vmem = pl.BlockSpec(memory_space=pltpu.VMEM)
    return pl.pallas_call(
        functools.partial(finish_kernel, sizes, heads, chunks),
        out_shape=[
            jax.ShapeDtypeStruct((rows, width), F32),
            jax.ShapeDtypeStruct((rows, width), F32),
            jax.ShapeDtypeStruct((1, cond), F32),
            jax.ShapeDtypeStruct((cond, piece), F32),
            jax.ShapeDtypeStruct((1, 6 * width), F32),
            jax.ShapeDtypeStruct((1, hidden), F32),
            jax.ShapeDtypeStruct((1, width), F32),
            jax.ShapeDtypeStruct((share, 3 * local), F32),
            jax.ShapeDtypeStruct((share, local), F32),
            jax.ShapeDtypeStruct((share, hidden), F32),
            jax.ShapeDtypeStruct((share, hidden), F32),
        ],
        in_specs=[vmem] * 26,
        out_specs=[vmem] * 11,
        scratch_shapes=[
            pltpu.VMEM((3 * heads, HD, length), BF16),
            pltpu.VMEM((heads, AUG, length), BF16),
            pltpu.VMEM((heads, length, AUG), BF16),
            pltpu.VMEM((heads, length, AUG), BF16),
            pltpu.VMEM((heads, AUG, length), BF16),
            pltpu.VMEM((heads, HD, length), F32),
            pltpu.VMEM((heads, HD, length), F32),
            pltpu.VMEM((width, 3 * local), BF16),
            *ShardScatter.scratch(count, share, 3 * local),
            *ShardScatter.scratch(count, share, hidden),
            *ShardScatter.scratch(count, share, hidden),
            *ShardScatter.scratch(count, share, local),
            *ColumnScatter.scratch(rows, width, chunks),
            pltpu.VMEM((2, 1, 7 * width), F32),
            pltpu.VMEM((2, 1, 7 * width), F32),
            pltpu.VMEM((count, 1, hidden), F32),
            pltpu.VMEM((count, 1, piece + width), F32),
            pltpu.VMEM((count, 1, piece + width), F32),
            pltpu.VMEM((count, 1, cond + piece), F32),
            pltpu.VMEM((count, 1, cond + piece), F32),
            pltpu.SemaphoreType.DMA((2, 3, count - 1)),
            pltpu.SemaphoreType.DMA((2, 2)),
            pltpu.VMEM((rows, width), BF16),
            pltpu.SemaphoreType.DMA((2,)),
        ],
        compiler_params=pltpu.CompilerParams(
            vmem_limit_bytes=VMEM_LIMIT, collective_id=2, has_side_effects=True
        ),
    )(qkv, bias, log_total, mixed_t, back_t, cosine, sine, normed, in_t, up_source, down_source, out_source,
      tokens, middle_back, parts, others, down_part, up_part, condition_all, condition_weight,
      middle, feed_far, feed_kept, cotangent, valid, down_bias)


def shards(
    sizes,
    tokens,
    condition,
    lengths,
    condition_weight,
    condition_bias,
    attention_in,
    attention_out,
    up_weight,
    up_bias,
    down_weight,
    down_bias,
    cotangent,
):
    columns = lax.axis_size("col")
    column_index = lax.axis_index("col")
    rows = tokens.shape[1]
    width = tokens.shape[2]
    length_all = rows * columns
    local_width = attention_in.shape[2]
    heads = local_width // HD
    in_shard = attention_in.reshape(attention_in.shape[0], 3 * local_width).astype(BF16)
    out_shard = attention_out.T.astype(BF16)
    condition_low = condition.astype(BF16)
    weight_low = condition_weight.astype(BF16)
    own_rows = tokens[0]
    length = lengths[0]
    position = column_index * rows + jnp.arange(rows)
    valid = (position < length).astype(F32)
    bias = jnp.where(jnp.arange(length_all) < length, 0.0, MASKED).astype(F32)[None]
    cosine, sine = (jnp.asarray(table) for table in rotary_tables(length_all))
    parts, normed_blocks, qkv, out_full, feed_back, down_bias_part, in_t, condition_all = start(
        sizes, heads, condition_low.astype(F32), weight_low, condition_bias[None], own_rows,
        in_shard, out_shard, cosine, sine, cotangent[0], valid[:, None],
    )
    normed_all = normed_blocks.reshape(length_all, width)
    attention, mixed_t, log_total, feed_back_blocks, up_full, down_t = attend(
        sizes, heads, qkv, bias, out_full, feed_back, up_weight, down_weight
    )
    hidden_cols = up_full.shape[1]
    bias_part = lax.dynamic_slice_in_dim(up_bias, column_index * hidden_cols, hidden_cols)
    (
        middle, middle_back, mixed_back, up_grad, down_grad, out_grad, up_bias_part, others, feed_far, feed_kept
    ) = feed_forward(
        sizes, heads, own_rows, attention, parts, up_full, down_t, bias_part[None], feed_back_blocks,
        cotangent[0], valid[:, None], mixed_t, out_full,
    )
    (
        result, tokens_back, condition_back, condition_grad, bias_grad, up_bias_grad, down_bias_grad,
        in_grad, out_grad, up_grad, down_grad,
    ) = finish(
        sizes, heads, qkv, bias, log_total, mixed_t, mixed_back,
        cosine, sine, normed_all, in_t, up_grad, down_grad, out_grad, own_rows, middle_back, parts,
        others, down_bias_part, up_bias_part, condition_all, weight_low,
        middle, feed_far, feed_kept, cotangent[0], valid[:, None], down_bias[None],
    )
    return (
        result[None],
        tokens_back[None],
        condition_back,
        condition_grad,
        bias_grad[0],
        in_grad.reshape(attention_in.shape),
        out_grad.T,
        up_grad,
        up_bias_grad[0],
        down_grad.T,
        down_bias_grad[0],
    )


def solution(mesh):
    sizes = {axis: mesh.shape[axis] for axis in ("dp", "row", "col")}
    in_specs = (
        P(("dp", "row"), "col", None),
        P(("dp", "row"), None),
        P(("dp", "row")),
        P(None, ("dp", "row")),
        P(),
        P(("dp", "row"), None, "col"),
        P("col", ("dp", "row")),
        P(("dp", "row"), "col"),
        P(),
        P("col", ("dp", "row")),
        P(),
        P(("dp", "row"), "col", None),
    )
    out_specs = (
        P(("dp", "row"), "col", None),
        P(("dp", "row"), "col", None),
        P(("dp", "row"), None),
        P(None, ("dp", "row")),
        P(),
        P(("dp", "row"), None, "col"),
        P("col", ("dp", "row")),
        P(("dp", "row"), "col"),
        P("col"),
        P("col", ("dp", "row")),
        P(),
    )
    return jax.shard_map(functools.partial(shards, sizes), mesh=mesh, in_specs=in_specs, out_specs=out_specs, check_vma=False)
```

```python
import functools
import math

import jax
import jax.numpy as jnp
import numpy as np
from jax import lax
from jax.experimental import pallas as pl
from jax.experimental.pallas import tpu as pltpu
from jax.sharding import PartitionSpec as P

HD = 64
AUG = 128
EPSILON = 1e-06
MASKED = -1e30
CUBIC = 0.044715
SLOPE = math.sqrt(2.0 / math.pi)
SCALE = 1.0 / math.sqrt(HD)
UNIT = SCALE * math.log2(math.e)
F32 = jnp.float32
BF16 = jnp.bfloat16
VMEM_LIMIT = 67043328


def layer_norm(values):
    center = values - jnp.mean(values, axis=-1, keepdims=True)
    spread = jnp.mean(center * center, axis=-1, keepdims=True)
    return center * lax.rsqrt(spread + EPSILON)


def rotary_tables(length):
    half = HD // 2
    exponent = np.arange(half, dtype=np.float32) * np.float32(2.0 / HD)
    frequency = np.exp(np.float32(-math.log(10000.0)) * exponent).astype(np.float32)
    angle = frequency[:, None] * np.arange(length, dtype=np.float32)[None, :]
    angle = angle.astype(np.float32).astype(np.float64)
    return np.cos(angle).astype(np.float32), np.sin(angle).astype(np.float32)


def contract(left, right, left_axis, right_axis):
    return lax.dot_general(
        left,
        right,
        (((left_axis,), (right_axis,)), ((), ())),
        preferred_element_type=F32,
    )


def block_at(index, size):
    return pl.ds(pl.multiple_of(index * size, size), size)


def split_three(values):
    high = values.astype(BF16)
    rest = values - high.astype(F32)
    middle = rest.astype(BF16)
    low = (rest - middle.astype(F32)).astype(BF16)
    return high.astype(F32), middle.astype(F32), low.astype(F32)


def augment(rows, extras):
    n = rows.shape[1]
    extras = [jnp.broadcast_to(e, (1, n)) for e in extras]
    pad = jnp.zeros((AUG - HD - len(extras), n), F32)
    return jnp.concatenate([rows] + extras + [pad], axis=0)


def attend_block(heads, here, query, key, value_t, mixed_t, log_total):
    scores = [contract(key[h], query[h, :, here], 1, 0) for h in range(heads)]
    for h in range(heads):
        top = jnp.max(scores[h], axis=0, keepdims=True)
        weights = jnp.exp2((scores[h] - top) * UNIT)
        total = jnp.sum(weights, axis=0, keepdims=True)
        out = contract(value_t[h], weights.astype(BF16), 1, 0) * (1.0 / total)
        mixed_t[h, :, here] = out.astype(BF16)
        log_total[h, :, here] = top * UNIT + jnp.log2(total)


def prepare_backward(heads, h, size, length, qkv, bias, log_total, mixed_t, back_t, query, key, value, back):
    def step(i, _):
        here = block_at(i, size)
        one = jnp.ones((1, size), F32)
        zero = jnp.zeros((1, size), F32)
        logs = split_three(log_total[h, :, here] * (-1.0 / UNIT))
        query[h, :, here] = augment(qkv[h, :, here].astype(F32), [one, *logs]).astype(BF16)
        keys = augment(qkv[heads + h, :, here].astype(F32), [bias[:, here], one, one, one])
        key[h, here, :] = keys.T.astype(BF16)
        values = augment(qkv[2 * heads + h, :, here].astype(F32), [zero, one, one, one])
        value[h, here, :] = values.T.astype(BF16)
        grad = back_t[h, :, here].astype(F32)
        center = jnp.sum(grad * mixed_t[h, :, here].astype(F32), axis=0, keepdims=True)
        back[h, :, here] = augment(grad, [zero, *split_three(-center)]).astype(BF16)
        return 0

    lax.fori_loop(0, length // size, step, 0)


MESH = pl.DeviceIdType.MESH


def local_copies(sources, targets, sems):
    return [pltpu.make_async_copy(a, b, sems.at[i]) for i, (a, b) in enumerate(zip(sources, targets))]


def flip(index, bit):
    return index + bit - 2 * bit * lax.rem(lax.div(index, bit), 2)


def flips(index, bits):
    for bit in bits:
        index = flip(index, bit)
    return index


def doubling(sizes):
    steps = []
    for axis, stride in (("dp", sizes["row"]), ("row", 1)):
        bit = sizes[axis] // 2
        while bit:
            steps.append((axis, bit, bit * stride))
            bit //= 2
    return steps


def subsets(bits):
    out = [()]
    for bit in bits:
        out = out + [kept + (bit,) for kept in out]
    return out


def send_copy(source, target, send, receive, peer):
    return pltpu.make_async_remote_copy(
        src_ref=source, dst_ref=target, send_sem=send, recv_sem=receive, device_id=peer, device_id_type=MESH
    )


def greet(peers):
    barrier = pltpu.get_barrier_semaphore()
    for peer in peers:
        pl.semaphore_signal(barrier, inc=1, device_id=peer, device_id_type=MESH)
    pl.semaphore_wait(barrier, len(peers))


def shard_number(sizes):
    return lax.axis_index("dp") * sizes["row"] + lax.axis_index("row")


def doubling_peers(sizes):
    return [{axis: flip(lax.axis_index(axis), bit)} for axis, bit, _ in doubling(sizes)]


def neighbour_peers(sizes):
    z = lax.axis_index("dp")
    n, m = sizes["dp"], sizes["row"]
    peers = [{"dp": lax.rem(z + 1, n)}, {"dp": lax.rem(z + n - 1, n)}]
    bit = m // 2
    while bit:
        peers.append({"row": flip(lax.axis_index("row"), bit)})
        bit //= 2
    return peers


def col_peers():
    me = lax.axis_index("col")
    return [{"col": flip(me, 1)}, {"col": flip(me, 2)}]


class ShardGather:
    def __init__(self, sizes, shard, full, sems):
        self.n, self.m = sizes["dp"], sizes["row"]
        self.rows = shard.shape[0]
        self.shard, self.full, self.sems = shard, full, sems
        self.z, self.y = lax.axis_index("dp"), lax.axis_index("row")

    def slot(self, z, y):
        return self.full.at[pl.ds(pl.multiple_of((z * self.m + y) * self.rows, self.rows), self.rows), :]

    def held(self, side, h):
        z = self.z - side * h
        return z, (z >= 0) if side > 0 else (z < self.n)

    def onward(self, side):
        return (self.z + 1 < self.n) if side > 0 else (self.z > 0)

    def stream(self, side, h, arriving):
        z, _ = self.held(side, h if arriving else h - 1)
        at = (h - 1) + (self.n - 1 if side < 0 else 0)
        source = self.slot(z, self.y) if arriving or h > 1 else self.shard
        peer = {"dp": self.z + (side if not arriving else -side)}
        return send_copy(source, self.slot(z, self.y), self.sems.at[0, at], self.sems.at[1, at], peer)

    def over(self, side, h, arriving):
        z, _ = self.held(side, h)
        bit = self.m // 2
        at = 2 * (self.n - 1) + h + (self.n - 1 if side < 0 and h else 0)
        there = self.slot(z, flip(self.y, bit) if arriving else self.y)
        source = self.shard if h == 0 and not arriving else there
        return send_copy(source, there, self.sems.at[0, at], self.sems.at[1, at], {"row": flip(self.y, bit)})

    def keep(self):
        self.slot(self.z, self.y)[...] = self.shard[...]

    def start(self):
        for side in (1, -1):

            @pl.when(self.onward(side))
            def _():
                self.stream(side, 1, False).start()

        self.over(1, 0, False).start()

    def advance(self, h):
        if h >= self.n:
            return
        for side in (1, -1):
            _, here = self.held(side, h)

            @pl.when(here)
            def _():
                self.stream(side, h, True).wait_recv()

            if h + 1 < self.n:

                @pl.when(jnp.logical_and(here, self.onward(side)))
                def _():
                    self.stream(side, h + 1, False).start()

            @pl.when(here)
            def _():
                self.over(side, h, False).start()

    def others(self):
        out, held, at = [], (self.m // 2,), 4 * self.n - 3
        bit = self.m // 4
        while bit:
            kept = subsets(held)
            out.append((bit, kept, at))
            at += self.n * len(kept)
            held = held + (bit,)
            bit //= 2
        return out

    def spread(self, bit, kept, at, arriving):
        peer = {"row": flip(self.y, bit)}
        for z in range(self.n):
            for i, bits in enumerate(kept):
                there = self.slot(z, flips(self.y, bits + ((bit,) if arriving else ())))
                k = at + z * len(kept) + i
                yield send_copy(there, there, self.sems.at[0, k], self.sems.at[1, k], peer)

    def finish(self):
        self.over(1, 0, True).wait_recv()
        for side in (1, -1):
            for h in range(1, self.n):

                @pl.when(self.held(side, h)[1])
                def _():
                    self.over(side, h, True).wait_recv()

        for step in self.others():
            for copy in self.spread(*step, False):
                copy.start()
            for copy in self.spread(*step, True):
                copy.wait_recv()

    def close(self):
        self.over(1, 0, False).wait_send()
        for side in (1, -1):
            for h in range(1, self.n):
                _, here = self.held(side, h)

                @pl.when(jnp.logical_and(self.held(side, h - 1)[1], self.onward(side)))
                def _():
                    self.stream(side, h, False).wait_send()

                @pl.when(here)
                def _():
                    self.over(side, h, False).wait_send()

        for step in self.others():
            for copy in self.spread(*step, False):
                copy.wait_send()

    @staticmethod
    def semaphores(sizes):
        n, m = sizes["dp"], sizes["row"]
        return pltpu.SemaphoreType.DMA((2, 4 * n - 3 + n * max(m - 2, 0)))


class ShardScatter:
    def __init__(self, sizes, source, total, out_buf, in_buf, sems):
        self.steps = doubling(sizes)[::-1]
        self.rows = out_buf.shape[1]
        self.source, self.total, self.out_buf, self.in_buf, self.sems = source, total, out_buf, in_buf, sems
        self.me = shard_number(sizes)
        self.first = [0]
        for k in range(len(self.steps)):
            self.first.append(self.first[-1] + 2 ** (len(self.steps) - 1 - k))

    def part(self, number):
        return pl.ds(pl.multiple_of(number * self.rows, self.rows), self.rows)

    def rest(self, k):
        return subsets([s[2] for s in self.steps[k + 1 :]])

    def copy(self, k, i):
        axis, bit, _ = self.steps[k]
        at = self.first[k] + i
        peer = {axis: flip(lax.axis_index(axis), bit)}
        return send_copy(self.out_buf.at[at], self.in_buf.at[at], self.sems.at[0, at], self.sems.at[1, at], peer)

    def held(self, k):
        return self.source if k == 0 else self.total

    def start(self, k):
        stride = self.steps[k][2]
        for i, kept in enumerate(self.rest(k)):
            number = flips(self.me, (stride,) + kept)
            self.out_buf[self.first[k] + i] = self.held(k)[self.part(number), :].astype(BF16)
            self.copy(k, i).start()

    def arrived(self, k):
        for i, kept in enumerate(self.rest(k)):
            self.copy(k, i).wait_recv()
            here = self.part(flips(self.me, kept))
            self.total[here, :] = self.held(k)[here, :].astype(F32) + self.in_buf[self.first[k] + i].astype(F32)

    def advance(self, k):
        if 0 < k <= len(self.steps):
            self.arrived(k - 1)
        if k < len(self.steps):
            self.start(k)

    def result(self):
        return self.total[self.part(self.me), :]

    def close(self):
        for k in range(len(self.steps)):
            for i in range(len(self.rest(k))):
                self.copy(k, i).wait_send()

    @staticmethod
    def scratch(count, rows, width):
        return [
            pltpu.VMEM((count * rows, width), F32),
            pltpu.VMEM((count - 1, rows, width), BF16),
            pltpu.VMEM((count - 1, rows, width), BF16),
            pltpu.SemaphoreType.DMA((2, count - 1)),
        ]


class ColumnGather:
    def __init__(self, full, chunks, sems):
        self.full, self.chunks, self.sems = full, chunks, sems
        self.me = lax.axis_index("col")
        self.rows = full.shape[1] // chunks

    def chunk(self, slot, j):
        return self.full.at[slot, pl.ds(j * self.rows, self.rows), :]

    def copy(self, kind, j, slot):
        peer = {"col": flip(self.me, 2 if kind == 1 else 1)}
        here = self.chunk(slot, j)
        return send_copy(here, here, self.sems.at[0, kind, j], self.sems.at[1, kind, j], peer)

    def start(self, j):
        for kind in (1, 0):
            copy = self.copy(kind, j, self.me)
            copy.start()

    def partner(self, j):
        self.copy(0, j, flip(self.me, 1)).wait_recv()

    def across(self, j):
        there = flip(self.me, 2)
        self.copy(1, j, there).wait_recv()
        copy = self.copy(2, j, there)
        copy.start()

    def diagonal(self, j):
        self.copy(2, j, flips(self.me, (1, 2))).wait_recv()

    def close(self):
        for j in range(self.chunks):
            for kind in range(3):
                self.copy(kind, j, self.me).wait_send()

    @staticmethod
    def semaphores(chunks):
        return pltpu.SemaphoreType.DMA((2, 3, chunks))


class ColumnScatter:
    def __init__(self, pair_out, pair_in, far_out, far_in, kept, chunks, sems):
        self.pair_out, self.pair_in, self.far_out, self.far_in = pair_out, pair_in, far_out, far_in
        self.kept, self.chunks, self.sems = kept, chunks, sems
        self.rows = kept.shape[0] // chunks
        me = lax.axis_index("col")
        self.near, self.far = {"col": flip(me, 1)}, {"col": flip(me, 2)}

    def at(self, j):
        return pl.ds(j * self.rows, self.rows)

    def pair(self, which, j):
        return send_copy(
            self.pair_out.at[which, self.at(j), :],
            self.pair_in.at[which, self.at(j), :],
            self.sems.at[0, which, j],
            self.sems.at[1, which, j],
            self.near,
        )

    def cross(self, j):
        return send_copy(
            self.far_out.at[self.at(j), :],
            self.far_in.at[self.at(j), :],
            self.sems.at[0, 2, j],
            self.sems.at[1, 2, j],
            self.far,
        )

    def begin(self, copy):
        copy.start()

    def give_diagonal(self, j, value):
        self.pair_out[1, self.at(j), :] = value.astype(BF16)
        self.begin(self.pair(1, j))

    def give_across(self, j, value):
        self.pair(1, j).wait_recv()
        self.far_out[self.at(j), :] = (value + self.pair_in[1, self.at(j), :].astype(F32)).astype(BF16)
        if self.far_in is not None:
            self.begin(self.cross(j))

    def give_partner(self, j, value):
        self.pair_out[0, self.at(j), :] = value.astype(BF16)
        self.begin(self.pair(0, j))

    def give_own(self, j, value):
        self.kept[self.at(j), :] = value

    def settle(self, j):
        self.pair(0, j).wait_recv()
        self.kept[self.at(j), :] = self.kept[self.at(j), :] + self.pair_in[0, self.at(j), :].astype(F32)

    def result(self, j):
        self.pair(0, j).wait_recv()
        self.cross(j).wait_recv()
        near = self.kept[self.at(j), :] + self.pair_in[0, self.at(j), :].astype(F32)
        return near + self.far_in[self.at(j), :].astype(F32)

    def close(self):
        for j in range(self.chunks):
            self.pair(0, j).wait_send()
            self.pair(1, j).wait_send()
            if self.far_in is not None:
                self.cross(j).wait_send()

    @staticmethod
    def scratch(rows, width, chunks):
        return [
            pltpu.VMEM((2, rows, width), BF16),
            pltpu.VMEM((2, rows, width), BF16),
            pltpu.VMEM((rows, width), BF16),
            pltpu.VMEM((rows, width), BF16),
            pltpu.VMEM((rows, width), F32),
            pltpu.SemaphoreType.DMA((2, 3, chunks)),
        ]


def other_peers(sizes):
    number = shard_number(sizes)
    total = sizes["dp"] * sizes["row"]
    bits = [stride for _, _, stride in doubling(sizes)]
    out = []
    for kept in subsets(bits)[1:]:
        peer = {}
        for axis, bit, stride in doubling(sizes):
            if stride in kept:
                peer[axis] = flip(peer.get(axis, lax.axis_index(axis)), bit)
        out.append((flips(number, kept), peer))
    assert len(out) == total - 1
    return out


def start_kernel(
    sizes, heads, chunks,
    condition, condition_weight, vectors, tokens, in_weight, out_weight, cosine, sine, cotangent, valid,
    modulation, normed, qkv, out_full, feed_back, bias_part, in_t, condition_all,
    in_shard, out_shard, pieces, arrived, in_full, out_t, unit, sems_tiny, sems_in, sems_out, sems_col,
):
    count = sizes["dp"] * sizes["row"]
    number = shard_number(sizes)
    rows, width = tokens.shape
    others = other_peers(sizes)
    in_shard[...] = jnp.concatenate([in_weight[t] for t in range(3)], axis=1).astype(BF16)
    out_shard[...] = out_weight[...].T.astype(BF16)
    greet([peer for _, peer in others] + col_peers())
    gather_in = ShardGather(sizes, in_shard, in_full, sems_in)
    gather_out = ShardGather(sizes, out_shard, out_t, sems_out)
    gather_col = ColumnGather(normed, chunks, sems_col)

    def condition_copy(i, slot):
        return send_copy(
            condition, condition_all.at[slot], sems_tiny.at[0, i], sems_tiny.at[1, i], others[i][1]
        )

    def piece_copy(i, mine, slot):
        return send_copy(
            pieces.at[mine], arrived.at[slot], sems_tiny.at[2, i], sems_tiny.at[3, i], others[i][1]
        )

    for i in range(count - 1):
        condition_copy(i, number).start()
    gather_in.start()
    gather_out.start()
    condition_all[number] = condition[...]
    gather_in.keep()
    gather_out.keep()
    size = rows // chunks

    def normal(j, _):
        here = block_at(j, size)
        unit[here, :] = layer_norm(tokens[here, :])
        return 0

    lax.fori_loop(0, chunks, normal, 0)
    for i in range(count - 1):
        condition_copy(i, others[i][0]).wait_recv()
    stacked = jnp.concatenate([condition_all[b] for b in range(count)], axis=0)
    product = contract(stacked.astype(BF16), condition_weight[...].astype(BF16), 1, 1)
    for b in range(count):
        pieces[b] = product[b : b + 1]
    for i in range(count - 1):
        piece_copy(i, others[i][0], number).start()
    arrived[number] = pieces[number]
    gather_in.advance(1)
    gather_out.advance(1)
    for i in range(count - 1):
        piece_copy(i, number, others[i][0]).wait_recv()
    line = jnp.concatenate([arrived[b] for b in range(count)], axis=1) + vectors[:, : 6 * width]
    parts = [line[:, t * width : (t + 1) * width] for t in range(6)]
    for t in range(6):
        modulation[t : t + 1, :] = parts[t]
    for j in range(chunks):
        here = pl.ds(j * size, size)
        value = unit[here, :] * (1.0 + parts[1]) + parts[0]
        normed[gather_col.me, here, :] = value.astype(BF16)
        gather_col.start(j)
    gather_in.advance(2)
    gather_out.advance(2)
    gather_in.advance(3)
    gather_out.advance(3)
    total = jnp.zeros((1, width), F32)
    for j in range(chunks):
        here = pl.ds(j * size, size)
        value = parts[5] * (cotangent[here, :] * valid[here, :])
        feed_back[here, :] = value.astype(BF16)
        total = total + jnp.sum(value, axis=0, keepdims=True)
    bias_part[...] = total
    for k in range(4, sizes["dp"]):
        gather_in.advance(k)
        gather_out.advance(k)
    gather_in.finish()
    gather_out.finish()
    in_t[...] = in_full[...].astype(F32).T.astype(BF16)
    out_full[...] = out_t[...].astype(F32).T.astype(BF16)

    def project(slot):
        here = pl.ds(pl.multiple_of(slot * rows, rows), rows)
        both = contract(in_t[...], normed[slot], 1, 1)
        half = HD // 2
        c, s = cosine[:, here], sine[:, here]
        for h in range(heads):
            for t in range(3):
                at = (t * heads + h) * HD
                a, b = both[at : at + half], both[at + half : at + HD]
                if t < 2:
                    a, b = a * c - b * s, b * c + a * s
                qkv[t * heads + h, :, here] = jnp.concatenate([a, b], axis=0).astype(BF16)

    me = gather_col.me
    far = flip(me, 2)

    def steps_of(i, _):
        @pl.when(i == 1)
        def _():
            for j in range(chunks):
                gather_col.partner(j)

        @pl.when(i == 2)
        def _():
            for j in range(chunks):
                gather_col.across(j)

        @pl.when(i == 3)
        def _():
            for j in range(chunks):
                gather_col.diagonal(j)

        project(flip_by(me, i))
        return 0

    lax.fori_loop(0, 4, steps_of, 0)
    for i in range(count - 1):
        condition_copy(i, number).wait_send()
        piece_copy(i, others[i][0], number).wait_send()
    gather_in.close()
    gather_out.close()
    gather_col.close()


def flip_by(index, pattern):
    out = 0
    for bit in (1, 2):
        a, b = lax.rem(lax.div(index, bit), 2), lax.rem(lax.div(pattern, bit), 2)
        out = out + bit * (a + b - 2 * a * b)
    return out


def start(sizes, heads, condition, condition_weight, vectors, tokens, in_weight, out_weight, cosine, sine, cotangent, valid):
    count = sizes["dp"] * sizes["row"]
    rows, width = tokens.shape
    length = cosine.shape[1]
    chunks = 2
    vmem = pl.BlockSpec(memory_space=pltpu.VMEM)
    piece = condition_weight.shape[0]
    local = heads * HD
    return pl.pallas_call(
        functools.partial(start_kernel, sizes, heads, chunks),
        out_shape=[
            jax.ShapeDtypeStruct((6, width), F32),
            jax.ShapeDtypeStruct((4, rows, width), BF16),
            jax.ShapeDtypeStruct((3 * heads, HD, length), BF16),
            jax.ShapeDtypeStruct((local, width), BF16),
            jax.ShapeDtypeStruct((rows, width), BF16),
            jax.ShapeDtypeStruct((1, width), F32),
            jax.ShapeDtypeStruct((3 * local, width), BF16),
            jax.ShapeDtypeStruct((count,) + condition.shape, F32),
        ],
        in_specs=[vmem] * 10,
        out_specs=[vmem] * 8,
        scratch_shapes=[
            pltpu.VMEM((width // count, 3 * local), BF16),
            pltpu.VMEM((width // count, local), BF16),
            pltpu.VMEM((count, 1, piece), F32),
            pltpu.VMEM((count, 1, piece), F32),
            pltpu.VMEM((width, 3 * local), BF16),
            pltpu.VMEM((width, local), BF16),
            pltpu.VMEM((rows, width), F32),
            pltpu.SemaphoreType.DMA((4, count - 1)),
            ShardGather.semaphores(sizes),
            ShardGather.semaphores(sizes),
            ColumnGather.semaphores(chunks),
        ],
        compiler_params=pltpu.CompilerParams(
            vmem_limit_bytes=VMEM_LIMIT, collective_id=0, has_side_effects=True
        ),
    )(condition, condition_weight, vectors, tokens, in_weight, out_weight, cosine, sine, cotangent, valid)


def attention_kernel(
    sizes, heads, chunks,
    qkv, bias, out_full, feed_back, up_shard, down_shard,
    attention, mixed_t, log_total, feed_back_all, up_full, down_t,
    query, key, up_low, down_low,
    pair_out, pair_in, far_out, far_in, kept, sems_scatter, sems_col, sems_up, sems_down,
):
    rows = feed_back.shape[0]
    length = qkv.shape[2]
    up_low[...] = up_shard[...].astype(BF16)
    down_low[...] = down_shard[...].astype(BF16)
    greet(neighbour_peers(sizes) + col_peers())
    gather_up = ShardGather(sizes, up_low, up_full, sems_up)
    gather_down = ShardGather(sizes, down_low, down_t, sems_down)
    gather_col = ColumnGather(feed_back_all, chunks, sems_col)
    scatter = ColumnScatter(pair_out, pair_in, far_out, far_in, kept, 1, sems_scatter)
    me = gather_col.me
    gather_up.start()
    gather_down.start()
    feed_back_all[me] = feed_back[...]
    for j in range(chunks):
        gather_col.start(j)
    gather_up.keep()
    gather_down.keep()

    def prepare(i, _):
        here = block_at(i, rows)
        one = jnp.ones((1, rows), F32)
        for h in range(heads):
            query[h, :, here] = augment(qkv[h, :, here].astype(F32), [one]).astype(BF16)
            keys = augment(qkv[heads + h, :, here].astype(F32), [bias[:, here], one, one, one])
            key[h, here, :] = keys.T.astype(BF16)
        return 0

    lax.fori_loop(0, length // rows, prepare, 0)

    def step(i, _):
        here = block_at(flip_by(me, 3 - i), rows)
        attend_block(heads, here, query, key, qkv.at[pl.ds(2 * heads, heads)], mixed_t, log_total)
        value = contract(mixed_t[:, :, here].reshape(heads * HD, rows), out_full[...], 0, 0)
        for order, give in enumerate(
            (scatter.give_diagonal, scatter.give_across, scatter.give_partner, scatter.give_own)
        ):

            @pl.when(i == order)
            def _():
                give(0, value)
                if order < 3:
                    gather_up.advance(order + 1)
                    gather_down.advance(order + 1)
                if order == 2:
                    for j in range(chunks):
                        gather_col.across(j)

        return 0

    lax.fori_loop(0, 4, step, 0)
    for k in range(4, sizes["dp"]):
        gather_up.advance(k)
        gather_down.advance(k)
    for j in range(chunks):
        gather_col.partner(j)
        gather_col.diagonal(j)
    gather_up.finish()
    gather_down.finish()
    attention[...] = scatter.result(0)
    gather_up.close()
    gather_down.close()
    gather_col.close()
    scatter.close()


def attend(sizes, heads, qkv, bias, out_full, feed_back, up_shard, down_shard):
    count = sizes["dp"] * sizes["row"]
    rows, width = feed_back.shape
    length = qkv.shape[2]
    chunks = 2
    hidden = up_shard.shape[1]
    vmem = pl.BlockSpec(memory_space=pltpu.VMEM)
    return pl.pallas_call(
        functools.partial(attention_kernel, sizes, heads, chunks),
        out_shape=[
            jax.ShapeDtypeStruct((rows, width), F32),
            jax.ShapeDtypeStruct((heads, HD, length), BF16),
            jax.ShapeDtypeStruct((heads, 1, length), F32),
            jax.ShapeDtypeStruct((4, rows, width), BF16),
            jax.ShapeDtypeStruct((width, hidden), BF16),
            jax.ShapeDtypeStruct((width, hidden), BF16),
        ],
        in_specs=[vmem] * 6,
        out_specs=[vmem] * 6,
        scratch_shapes=[
            pltpu.VMEM((heads, AUG, length), BF16),
            pltpu.VMEM((heads, length, AUG), BF16),
            pltpu.VMEM((width // count, hidden), BF16),
            pltpu.VMEM((width // count, hidden), BF16),
            *ColumnScatter.scratch(rows, width, 1),
            ColumnGather.semaphores(chunks),
            ShardGather.semaphores(sizes),
            ShardGather.semaphores(sizes),
        ],
        compiler_params=pltpu.CompilerParams(
            vmem_limit_bytes=VMEM_LIMIT, collective_id=1, has_side_effects=True
        ),
    )(qkv, bias, out_full, feed_back, up_shard, down_shard)


def feed_kernel(
    sizes, heads, chunks,
    tokens, attention, parts, vectors, valid, up_far, down_far, feed_back_far, cotangent_far, mixed_far, out_far,
    mixed_back, out_grad, up_part, sums, middle_to, middle_back_to, up_to, down_to, feed_far_to, feed_kept_to,
    second_all, hidden_all, before_all, back_all, second_sems, back_sems,
    pair_out, pair_in, far_out, far_in, kept, scatter_sems, feed_pair_out, feed_pair_in, feed_sems,
    up_full, down_t, feed_back_all, cotangent, mixed_t, out_full,
    middle, middle_back, up_grad, down_grad, feed_far, feed_kept, load_sems, store_sems,
):
    rows, width = tokens.shape
    size = rows // chunks
    loads = local_copies(
        (up_far, down_far, feed_back_far, cotangent_far, mixed_far, out_far),
        (up_full, down_t, feed_back_all, cotangent, mixed_t, out_full),
        load_sems,
    )
    stores = local_copies(
        (middle, feed_far, middle_back, up_grad, down_grad, feed_kept),
        (middle_to, feed_far_to, middle_back_to, up_to, down_to, feed_kept_to),
        store_sems,
    )
    for copy in loads:
        copy.start()
    length = 4 * rows
    greet(col_peers())
    gather = ColumnGather(second_all, chunks, second_sems)
    gather_back = ColumnGather(back_all, chunks, back_sems)
    scatter = ColumnScatter(pair_out, pair_in, far_out, far_in, kept, chunks, scatter_sems)
    feed = ColumnScatter(feed_pair_out, feed_pair_in, feed_far, None, feed_kept, chunks, feed_sems)
    me = gather.me
    for j in range(chunks):
        here = pl.ds(j * size, size)
        value = tokens[here, :] + parts[2:3, :] * attention[here, :]
        middle[here, :] = value
        second_all[me, here, :] = (layer_norm(value) * (1.0 + parts[4:5, :]) + parts[3:4, :]).astype(BF16)
        gather.start(j)
    up_part[...] = jnp.zeros_like(up_part)
    for copy in loads:
        copy.wait()

    def block(i, _):
        late = lax.div(i, 4)
        pattern = (1 - late) * lax.div(i, 2) + late * (3 - lax.rem(i, 2))
        j = (1 - late) * lax.rem(i, 2) + late * (lax.div(i, 2) - 2)
        slot = flip_by(me, pattern)
        here = pl.ds(pl.multiple_of(j * size, size), size)

        @pl.when(i == 2)
        def _():
            for c in range(chunks):
                gather.partner(c)

        @pl.when(i == 3)
        def _():
            gather.across(0)

        @pl.when(i == 4)
        def _():
            gather.diagonal(0)

        @pl.when(i == 6)
        def _():
            gather.diagonal(1)

        before = contract(second_all[slot, here, :], up_full[...], 1, 0) + vectors[:, 6 * width : 6 * width + up_part.shape[1]]
        bend = jnp.tanh(SLOPE * (before + CUBIC * before * before * before))
        hidden = (0.5 * before * (1.0 + bend)).astype(BF16)
        slope = 0.5 * (1.0 + bend) + 0.5 * before * (1.0 - bend * bend) * (SLOPE * (1.0 + 3.0 * CUBIC * before * before))
        hidden_back = contract(feed_back_all[slot, here, :], down_t[...], 1, 0)
        before_back = (hidden_back * slope).astype(BF16)
        hidden_all[slot, here, :] = hidden
        before_all[slot, here, :] = before_back
        up_part[...] += jnp.sum(before_back.astype(F32), axis=0, keepdims=True)
        back_value = contract(before_back, up_full[...], 1, 1)
        feed_value = contract(hidden, down_t[...], 1, 1)
        for at, (name, c) in enumerate(
            (("own", 0), ("own", 1), ("partner", 0), ("partner", 1), ("diagonal", 0), ("across", 0), ("diagonal", 1), ("across", 1))
        ):

            @pl.when(i == at)
            def _():
                getattr(scatter, "give_" + name)(c, back_value)
                getattr(feed, "give_" + name)(c, feed_value)
                if at == 5:
                    gather.across(1)

        return 0

    lax.fori_loop(0, 8, block, 0)
    stores[0].start()
    stores[1].start()
    gate_sum = jnp.zeros((1, width), F32)
    shift_sum = jnp.zeros((1, width), F32)
    scale_sum = jnp.zeros((1, width), F32)
    for j in range(chunks):
        here = pl.ds(j * size, size)
        own = middle[here, :]
        center = own - jnp.mean(own, axis=-1, keepdims=True)
        inverse = lax.rsqrt(jnp.mean(center * center, axis=-1, keepdims=True) + EPSILON)
        unit = center * inverse
        grad = scatter.result(j)
        scaled = grad * (1.0 + parts[4:5, :])
        inner = scaled - jnp.mean(scaled, axis=-1, keepdims=True) - unit * jnp.mean(scaled * unit, axis=-1, keepdims=True)
        total = cotangent[here, :] * valid[here, :] + inverse * inner
        middle_back[here, :] = total
        back_all[me, here, :] = (parts[2:3, :] * total).astype(BF16)
        gather_back.start(j)
        gate_sum = gate_sum + jnp.sum(total * attention[here, :], axis=0, keepdims=True)
        shift_sum = shift_sum + jnp.sum(grad, axis=0, keepdims=True)
        scale_sum = scale_sum + jnp.sum(grad * unit, axis=0, keepdims=True)
        if j == 0:
            up_grad[...] = contract(second_all[...].reshape(length, width), before_all[...].reshape(length, -1), 0, 0).astype(BF16)
        if j == 1:
            down_grad[...] = contract(feed_back_all[...].reshape(length, width), hidden_all[...].reshape(length, -1), 0, 0).astype(BF16)
    sums[...] = jnp.concatenate([gate_sum, shift_sum, scale_sum], axis=1)
    for j in range(chunks):
        feed.settle(j)
    gather_back.across(0)
    for copy in stores[2:5]:
        copy.start()

    def mix(i, _):
        @pl.when(i == 1)
        def _():
            for c in range(chunks):
                gather_back.partner(c)

        @pl.when(i == 2)
        def _():
            stores[5].start()
            gather_back.across(1)

        @pl.when(i == 3)
        def _():
            for c in range(chunks):
                gather_back.diagonal(c)

        slot = flip_by(me, i)
        here = block_at(slot, rows)
        value = contract(out_full[...], back_all[slot], 1, 1).astype(BF16)
        for h in range(heads):
            mixed_back[h, :, here] = value[h * HD : (h + 1) * HD]
        return 0

    lax.fori_loop(0, 4, mix, 0)
    out_grad[...] = contract(
        back_all[...].reshape(length, width), mixed_t[...].reshape(heads * HD, length), 0, 1
    ).astype(BF16)
    for copy in stores:
        copy.wait()
    gather.close()
    gather_back.close()
    scatter.close()
    feed.close()


def feed_forward(
    sizes, heads, tokens, attention, parts, up_full, down_t, vectors, feed_back_all, cotangent, valid, mixed_t, out_full
):
    rows, width = tokens.shape
    hidden = up_full.shape[1]
    length = 4 * rows
    local = heads * HD
    chunks = 2
    vmem = pl.BlockSpec(memory_space=pltpu.VMEM)
    far = pl.BlockSpec(memory_space=pl.ANY)
    own = jax.ShapeDtypeStruct((rows, width), F32)
    late = (up_full, down_t, feed_back_all, cotangent, mixed_t, out_full)
    return pl.pallas_call(
        functools.partial(feed_kernel, sizes, heads, chunks),
        out_shape=[
            jax.ShapeDtypeStruct((heads, HD, length), BF16),
            jax.ShapeDtypeStruct((width, local), BF16),
            jax.ShapeDtypeStruct((1, hidden), F32),
            jax.ShapeDtypeStruct((1, 3 * width), F32),
            own,
            own,
            jax.ShapeDtypeStruct((width, hidden), BF16),
            jax.ShapeDtypeStruct((width, hidden), BF16),
            jax.ShapeDtypeStruct((rows, width), BF16),
            own,
        ],
        in_specs=[vmem] * 5 + [far] * 6,
        out_specs=[vmem] * 4 + [far] * 6,
        scratch_shapes=[
            pltpu.VMEM((4, rows, width), BF16),
            pltpu.VMEM((4, rows, hidden), BF16),
            pltpu.VMEM((4, rows, hidden), BF16),
            pltpu.VMEM((4, rows, width), BF16),
            ColumnGather.semaphores(chunks),
            ColumnGather.semaphores(chunks),
            *ColumnScatter.scratch(rows, width, chunks),
            pltpu.VMEM((2, rows, width), BF16),
            pltpu.VMEM((2, rows, width), BF16),
            pltpu.SemaphoreType.DMA((2, 3, chunks)),
            *[pltpu.VMEM(one.shape, one.dtype) for one in late],
            pltpu.VMEM((rows, width), F32),
            pltpu.VMEM((rows, width), F32),
            pltpu.VMEM((width, hidden), BF16),
            pltpu.VMEM((width, hidden), BF16),
            pltpu.VMEM((rows, width), BF16),
            pltpu.VMEM((rows, width), F32),
            pltpu.SemaphoreType.DMA((6,)),
            pltpu.SemaphoreType.DMA((6,)),
        ],
        compiler_params=pltpu.CompilerParams(
            vmem_limit_bytes=VMEM_LIMIT, collective_id=3, has_side_effects=True
        ),
    )(tokens, attention, parts, vectors, valid, *late)


def contract_exact(left, right, left_axis, right_axis):
    return lax.dot_general(
        left,
        right,
        (((left_axis,), (right_axis,)), ((), ())),
        precision=lax.Precision.HIGHEST,
        preferred_element_type=F32,
    )


def finish_kernel(
    sizes, heads, chunks,
    qkv, bias, log_total, mixed_t, back_t, cosine, sine, up_source, down_source, out_source,
    parts, others, down_part, up_part, condition_all, condition_weight, feed_far, valid, vectors,
    normed_far, in_far, tokens_far, middle_back_far, middle_far, feed_kept_far, cotangent_far,
    output_to, tokens_back_to, condition_back, condition_grad, bias_grad, up_bias, down_bias, in_grad, out_grad, up_grad, down_grad,
    turned, query, key, value, back, key_sum, value_sum, in_source,
    in_total, in_out, in_in, in_sems, up_total, up_out, up_in, up_sems,
    down_total, down_out, down_in, down_sems, out_total, out_out, out_in, out_sems,
    pair_out, pair_in, far_out, far_in, kept, col_sems,
    line_out, line_in, up_all, pieces, arrived, backs, collected, tiny_sems, line_sems, feed_in, feed_sems,
    normed, in_t, tokens, middle_back, middle, feed_kept, cotangent, output, tokens_back, load_sems, store_sems,
    condition_low, weight_low,
):
    count = sizes["dp"] * sizes["row"]
    number = shard_number(sizes)
    length = qkv.shape[2]
    rows, width = tokens.shape
    half = HD // 2
    piece, cond = condition_weight.shape
    peers = other_peers(sizes)
    me = lax.axis_index("col")
    near, far = col_peers()
    greet([peer for _, peer in peers] + [near, far, {"col": flips(me, (1, 2))}])
    loads = local_copies(
        (normed_far, in_far, tokens_far, middle_back_far, middle_far, feed_kept_far, cotangent_far),
        (normed, in_t, tokens, middle_back, middle, feed_kept, cotangent),
        load_sems,
    )
    stores = local_copies((output, tokens_back), (output_to, tokens_back_to), store_sems)
    for copy in loads:
        copy.start()
    scatter_up = ShardScatter(sizes, up_source, up_total, up_out, up_in, up_sems)
    scatter_down = ShardScatter(sizes, down_source, down_total, down_out, down_in, down_sems)
    scatter_out = ShardScatter(sizes, out_source, out_total, out_out, out_in, out_sems)
    scatter_in = ShardScatter(sizes, in_source, in_total, in_out, in_in, in_sems)
    column = ColumnScatter(pair_out, pair_in, far_out, far_in, kept, chunks, col_sems)

    def tiny(kind, i, source, target):
        return send_copy(source, target, tiny_sems.at[0, kind, i], tiny_sems.at[1, kind, i], peers[i][1])

    def up_copy(i, slot):
        return tiny(0, i, up_part, up_all.at[slot])

    def piece_copy(i, mine, slot):
        return tiny(1, i, pieces.at[mine], arrived.at[slot])

    def back_copy(i, mine, slot):
        return tiny(2, i, backs.at[mine], collected.at[slot])

    def line_copy(k, arriving):
        other = flips(me, [bit for bit in (1, 2) if k & bit])
        slot = other if arriving else me
        return send_copy(
            line_out, line_in.at[slot], line_sems.at[0, k - 1], line_sems.at[1, k - 1], {"col": other}
        )

    feed_copy = send_copy(feed_far, feed_in, feed_sems.at[0], feed_sems.at[1], far)
    feed_copy.start()
    scatter_up.start(0)
    scatter_down.start(0)
    scatter_out.start(0)
    for i in range(count - 1):
        up_copy(i, number).start()
    up_all[number] = up_part[...]

    def turn_back(values, here):
        c, s = cosine[:, here], sine[:, here]
        a, b = values[:half], values[half:]
        return jnp.concatenate([a * c + b * s, b * c - a * s], axis=0)

    for h in range(heads):
        prepare_backward(heads, h, rows, length, qkv, bias, log_total, mixed_t, back_t, query, key, value, back)
    condition_low[...] = jnp.concatenate([condition_all[b] for b in range(count)], axis=0).astype(BF16)
    weight_low[...] = condition_weight[...].astype(BF16)
    key_sum[...] = jnp.zeros_like(key_sum)
    value_sum[...] = jnp.zeros_like(value_sum)

    def step(i, _):
        here = block_at(i, rows)
        for h in range(heads):
            q, d = query[h, :, here], back[h, :, here]
            weights = jnp.exp2(contract(key[h], q, 1, 0) * UNIT)
            grads = (weights * contract(value[h], d, 1, 0)).astype(BF16)
            value_sum[h] += contract(d[:HD], weights.astype(BF16), 1, 1)
            key_sum[h] += contract(q[:HD], grads, 1, 1)
            query_back = contract(qkv[heads + h], grads, 1, 0) * SCALE
            turned[h, :, here] = turn_back(query_back, here).astype(BF16)

        @pl.when(i == 1)
        def _():
            scatter_up.advance(1)

        @pl.when(i == 2)
        def _():
            scatter_down.advance(1)
            scatter_out.advance(1)
            scatter_up.advance(2)

        return 0

    lax.fori_loop(0, 4, step, 0)

    def finish_block(i, _):
        here = block_at(i, rows)
        for h in range(heads):
            turned[heads + h, :, here] = turn_back(key_sum[h, :, here] * SCALE, here).astype(BF16)
            turned[2 * heads + h, :, here] = value_sum[h, :, here].astype(BF16)
        return 0

    lax.fori_loop(0, 4, finish_block, 0)
    for copy in loads:
        copy.wait()
    scatter_down.advance(2)
    scatter_out.advance(2)
    size = rows // chunks

    def part_of(slot, j):
        start_at = pl.multiple_of(slot * rows + j * size, size)
        block = turned[:, :, pl.ds(start_at, size)].reshape(3 * heads * HD, size)
        return contract(block, in_t[...], 0, 0)

    for j in range(chunks):
        column.give_diagonal(j, part_of(flips(me, (1, 2)), j))
    for j in range(chunks):
        column.give_across(j, part_of(flip(me, 2), j))
    in_source[...] = contract(
        normed[...], turned[...].reshape(3 * heads * HD, length), 0, 1
    ).astype(BF16)
    scatter_in.start(0)
    scatter_up.advance(3)
    for j in range(chunks):
        column.give_partner(j, part_of(flip(me, 1), j))
    for j in range(chunks):
        column.give_own(j, part_of(me, j))
    scatter_down.advance(3)
    scatter_out.advance(3)
    shift_sum = jnp.zeros((1, width), F32)
    scale_sum = jnp.zeros((1, width), F32)
    gate_sum = jnp.zeros((1, width), F32)
    feed_copy.wait_recv()
    for j in range(chunks):
        here = pl.ds(j * size, size)
        feed = feed_kept[here, :] + feed_in[here, :].astype(F32) + vectors[:, vectors.shape[1] - width :]
        output[here, :] = middle[here, :] + parts[5:6, :] * feed
        gate_sum = gate_sum + jnp.sum(cotangent[here, :] * valid[here, :] * feed, axis=0, keepdims=True)
    scatter_in.advance(1)
    for j in range(chunks):
        here = pl.ds(j * size, size)
        own = tokens[here, :]
        center = own - jnp.mean(own, axis=-1, keepdims=True)
        inverse = lax.rsqrt(jnp.mean(center * center, axis=-1, keepdims=True) + EPSILON)
        unit = center * inverse
        grad = column.result(j)
        scaled = grad * (1.0 + parts[1:2, :])
        inner = scaled - jnp.mean(scaled, axis=-1, keepdims=True) - unit * jnp.mean(scaled * unit, axis=-1, keepdims=True)
        tokens_back[here, :] = middle_back[here, :] + inverse * inner
        shift_sum = shift_sum + jnp.sum(grad, axis=0, keepdims=True)
        scale_sum = scale_sum + jnp.sum(grad * unit, axis=0, keepdims=True)
    line_out[...] = jnp.concatenate([shift_sum, scale_sum, others[...], gate_sum, down_part[...]], axis=1)
    for k in (2, 3, 1):
        line_copy(k, False).start()
    line_in[me] = line_out[...]
    scatter_in.advance(2)
    for copy in stores:
        copy.start()
    steps = len(scatter_in.steps)
    for k in range(4, steps + 1):
        for one in (scatter_up, scatter_down, scatter_out):
            one.advance(k)
    up_grad[...] = scatter_up.result()
    down_grad[...] = scatter_down.result()
    out_grad[...] = scatter_out.result()
    for i in range(count - 1):
        up_copy(i, peers[i][0]).wait_recv()
    up_bias[...] = jnp.sum(jnp.concatenate([up_all[b] for b in range(count)], axis=0), axis=0, keepdims=True)
    for k in (1, 2, 3):
        line_copy(k, True).wait_recv()
    line = (line_in[0] + line_in[1]) + (line_in[2] + line_in[3])
    split = 6 * width
    for b in range(count):
        pieces[b] = jnp.concatenate([line[:, b * piece : (b + 1) * piece], line[:, split:]], axis=1)
    for i in range(count - 1):
        piece_copy(i, peers[i][0], number).start()
    arrived[number] = pieces[number]
    for i in range(count - 1):
        piece_copy(i, number, peers[i][0]).wait_recv()
    stacked = jnp.concatenate([arrived[b] for b in range(count)], axis=0)
    mine = stacked[:, :piece]
    down_bias[...] = jnp.sum(stacked[:, piece:], axis=0, keepdims=True)
    bias_piece = jnp.sum(mine, axis=0, keepdims=True)
    back_rows = contract_exact(mine, weight_low[...].astype(F32), 1, 0)
    for b in range(count):
        backs[b] = jnp.concatenate([back_rows[b : b + 1], bias_piece], axis=1)
    for i in range(count - 1):
        back_copy(i, peers[i][0], number).start()
    collected[number] = backs[number]
    for k in range(3, steps + 1):
        scatter_in.advance(k)
    in_grad[...] = scatter_in.result()
    condition_grad[...] = contract_exact(condition_low[...].astype(F32), mine, 0, 0).T
    for i in range(count - 1):
        back_copy(i, number, peers[i][0]).wait_recv()
    gathered = [collected[b] for b in range(count)]
    bias_grad[...] = jnp.concatenate([one[:, cond:] for one in gathered], axis=1)
    condition_back[...] = jnp.sum(
        jnp.concatenate([one[:, :cond] for one in gathered], axis=0), axis=0, keepdims=True
    )
    for i in range(count - 1):
        up_copy(i, number).wait_send()
        piece_copy(i, peers[i][0], number).wait_send()
        back_copy(i, peers[i][0], number).wait_send()
    for k in (1, 2, 3):
        line_copy(k, False).wait_send()
    for copy in stores:
        copy.wait()
    feed_copy.wait_send()
    for one in (scatter_up, scatter_down, scatter_out, scatter_in):
        one.close()
    column.close()


def finish(sizes, heads, qkv, bias, log_total, mixed_t, back_t, cosine, sine, normed, in_t, up_source, down_source,
           out_source, tokens, middle_back, parts, others, down_part, up_part, condition_all, condition_weight,
           middle, feed_far, feed_kept, cotangent, valid, vectors):
    count = sizes["dp"] * sizes["row"]
    length = qkv.shape[2]
    rows, width = tokens.shape
    chunks = 2
    local = heads * HD
    hidden = up_source.shape[1]
    piece, cond = condition_weight.shape
    share = width // count
    late = (normed, in_t, tokens, middle_back, middle, feed_kept, cotangent)
    far = pl.BlockSpec(memory_space=pl.ANY)
    vmem = pl.BlockSpec(memory_space=pltpu.VMEM)
    return pl.pallas_call(
        functools.partial(finish_kernel, sizes, heads, chunks),
        out_shape=[
            jax.ShapeDtypeStruct((rows, width), F32),
            jax.ShapeDtypeStruct((rows, width), F32),
            jax.ShapeDtypeStruct((1, cond), F32),
            jax.ShapeDtypeStruct((piece, cond), F32),
            jax.ShapeDtypeStruct((1, 6 * width), F32),
            jax.ShapeDtypeStruct((1, hidden), F32),
            jax.ShapeDtypeStruct((1, width), F32),
            jax.ShapeDtypeStruct((share, 3 * local), F32),
            jax.ShapeDtypeStruct((share, local), F32),
            jax.ShapeDtypeStruct((share, hidden), F32),
            jax.ShapeDtypeStruct((share, hidden), F32),
        ],
        in_specs=[vmem] * 16 + [far] + [vmem] * 2 + [far] * len(late),
        out_specs=[far] * 2 + [vmem] * 9,
        scratch_shapes=[
            pltpu.VMEM((3 * heads, HD, length), BF16),
            pltpu.VMEM((heads, AUG, length), BF16),
            pltpu.VMEM((heads, length, AUG), BF16),
            pltpu.VMEM((heads, length, AUG), BF16),
            pltpu.VMEM((heads, AUG, length), BF16),
            pltpu.VMEM((heads, HD, length), F32),
            pltpu.VMEM((heads, HD, length), F32),
            pltpu.VMEM((width, 3 * local), BF16),
            *ShardScatter.scratch(count, share, 3 * local),
            *ShardScatter.scratch(count, share, hidden),
            *ShardScatter.scratch(count, share, hidden),
            *ShardScatter.scratch(count, share, local),
            *ColumnScatter.scratch(rows, width, chunks),
            pltpu.VMEM((1, 7 * width), F32),
            pltpu.VMEM((4, 1, 7 * width), F32),
            pltpu.VMEM((count, 1, hidden), F32),
            pltpu.VMEM((count, 1, piece + width), F32),
            pltpu.VMEM((count, 1, piece + width), F32),
            pltpu.VMEM((count, 1, cond + piece), F32),
            pltpu.VMEM((count, 1, cond + piece), F32),
            pltpu.SemaphoreType.DMA((2, 3, count - 1)),
            pltpu.SemaphoreType.DMA((2, 3)),
            pltpu.VMEM((rows, width), BF16),
            pltpu.SemaphoreType.DMA((2,)),
            *[pltpu.VMEM(one.shape, one.dtype) for one in late],
            pltpu.VMEM((rows, width), F32),
            pltpu.VMEM((rows, width), F32),
            pltpu.SemaphoreType.DMA((len(late),)),
            pltpu.SemaphoreType.DMA((2,)),
            pltpu.VMEM((count, cond), BF16),
            pltpu.VMEM((piece, cond), BF16),
        ],
        compiler_params=pltpu.CompilerParams(
            vmem_limit_bytes=VMEM_LIMIT, collective_id=2, has_side_effects=True
        ),
    )(qkv, bias, log_total, mixed_t, back_t, cosine, sine, up_source, down_source, out_source,
      parts, others, down_part, up_part, condition_all, condition_weight, feed_far, valid, vectors, *late)


def emit_kernel(heads, output, tokens_back, condition_grad, in_grad, out_grad, up_grad, down_grad, *rest):
    output_to, tokens_to, condition_to, in_to, out_to, up_to, down_to = rest[4:11]
    for one, to in zip(rest[:3], rest[11:14]):
        to[...] = one[...].reshape(to.shape)
    rest[14][...] = rest[3][...]
    output_to[...] = output[...]
    tokens_to[...] = tokens_back[...]
    condition_to[...] = condition_grad[...]
    local = heads * HD
    for t in range(3):
        in_to[t] = in_grad[:, t * local : (t + 1) * local]
    out_to[...] = out_grad[...].T
    up_to[...] = up_grad[...]
    down_to[...] = down_grad[...]


def emit(heads, *arrays):
    output, tokens_back, condition_grad, in_grad, out_grad, up_grad, down_grad = arrays[:7]
    share, local = out_grad.shape
    vmem = pl.BlockSpec(memory_space=pltpu.VMEM)
    shapes = [
        output.shape, tokens_back.shape, condition_grad.shape, (3, share, local), (local, share),
        up_grad.shape, down_grad.shape, *[one.shape[1:] for one in arrays[7:10]], arrays[10].shape,
    ]
    return pl.pallas_call(
        functools.partial(emit_kernel, heads),
        out_shape=[jax.ShapeDtypeStruct(one, F32) for one in shapes],
        in_specs=[vmem] * 11,
        out_specs=[vmem] * 11,
    )(*arrays)


def shards(
    sizes,
    tokens,
    condition,
    lengths,
    condition_weight,
    condition_bias,
    attention_in,
    attention_out,
    up_weight,
    up_bias,
    down_weight,
    down_bias,
    cotangent,
):
    columns = lax.axis_size("col")
    column_index = lax.axis_index("col")
    rows = tokens.shape[1]
    width = tokens.shape[2]
    length_all = rows * columns
    local_width = attention_in.shape[2]
    heads = local_width // HD
    own_rows = tokens[0]
    length = lengths[0]
    position = column_index * rows + jnp.arange(rows)
    valid = (position < length).astype(F32)
    bias = jnp.where(jnp.arange(length_all) < length, 0.0, MASKED).astype(F32)[None]
    cosine, sine = (jnp.asarray(table) for table in rotary_tables(length_all))
    hidden_cols = up_weight.shape[1]
    bias_part = lax.dynamic_slice_in_dim(up_bias, column_index * hidden_cols, hidden_cols)
    vectors = jnp.concatenate([condition_bias, bias_part, down_bias])[None]
    parts, normed_blocks, qkv, out_full, feed_back, down_bias_part, in_t, condition_all = start(
        sizes, heads, condition, condition_weight.T, vectors, own_rows,
        jnp.transpose(attention_in, (1, 0, 2)), attention_out, cosine, sine, cotangent[0], valid[:, None],
    )
    normed_all = normed_blocks.reshape(length_all, width)
    attention, mixed_t, log_total, feed_back_blocks, up_full, down_t = attend(
        sizes, heads, qkv, bias, out_full, feed_back, up_weight, down_weight.T
    )
    (
        mixed_back, out_grad, up_bias_part, others, middle, middle_back, up_grad, down_grad, feed_far, feed_kept
    ) = feed_forward(
        sizes, heads, own_rows, attention, parts, up_full, down_t, vectors, feed_back_blocks,
        cotangent[0], valid[:, None], mixed_t, out_full,
    )
    (
        result, tokens_back, condition_back, condition_grad, bias_grad, up_bias_grad, down_bias_grad,
        in_grad, out_grad, up_grad, down_grad,
    ) = finish(
        sizes, heads, qkv, bias, log_total, mixed_t, mixed_back,
        cosine, sine, normed_all, in_t, up_grad, down_grad, out_grad, own_rows, middle_back, parts,
        others, down_bias_part, up_bias_part, condition_all, condition_weight.T,
        middle, feed_far, feed_kept, cotangent[0], valid[:, None], vectors,
    )
    (
        result, tokens_back, condition_grad, in_grad, out_grad, up_grad, down_grad,
        bias_grad, up_bias_grad, down_bias_grad, condition_back,
    ) = emit(
        heads, result, tokens_back, condition_grad, in_grad, out_grad, up_grad, down_grad,
        bias_grad, up_bias_grad, down_bias_grad, condition_back,
    )
    return (
        result[None],
        tokens_back[None],
        condition_back,
        condition_grad.T,
        bias_grad,
        jnp.transpose(in_grad, (1, 0, 2)),
        out_grad,
        up_grad,
        up_bias_grad,
        down_grad.T,
        down_bias_grad,
    )


def solution(mesh):
    sizes = {axis: mesh.shape[axis] for axis in ("dp", "row", "col")}
    in_specs = (
        P(("dp", "row"), "col", None),
        P(("dp", "row"), None),
        P(("dp", "row")),
        P(None, ("dp", "row")),
        P(),
        P(("dp", "row"), None, "col"),
        P("col", ("dp", "row")),
        P(("dp", "row"), "col"),
        P(),
        P("col", ("dp", "row")),
        P(),
        P(("dp", "row"), "col", None),
    )
    out_specs = (
        P(("dp", "row"), "col", None),
        P(("dp", "row"), "col", None),
        P(("dp", "row"), None),
        P(None, ("dp", "row")),
        P(),
        P(("dp", "row"), None, "col"),
        P("col", ("dp", "row")),
        P(("dp", "row"), "col"),
        P("col"),
        P("col", ("dp", "row")),
        P(),
    )
    return jax.shard_map(functools.partial(shards, sizes), mesh=mesh, in_specs=in_specs, out_specs=out_specs, check_vma=False)
```

```python
import functools
import math

import jax
import jax.numpy as jnp
import numpy as np
from jax import lax
from jax.experimental import pallas as pl
from jax.experimental.pallas import tpu as pltpu
from jax.sharding import PartitionSpec as P

HD = 64
AUG = 128
EPSILON = 1e-06
MASKED = -1e30
CUBIC = 0.044715
SLOPE = math.sqrt(2.0 / math.pi)
SCALE = 1.0 / math.sqrt(HD)
UNIT = SCALE * math.log2(math.e)
F32 = jnp.float32
BF16 = jnp.bfloat16
VMEM_LIMIT = 67043328


def layer_norm(values):
    center = values - jnp.mean(values, axis=-1, keepdims=True)
    spread = jnp.mean(center * center, axis=-1, keepdims=True)
    return center * lax.rsqrt(spread + EPSILON)


def rotary_tables(length):
    half = HD // 2
    exponent = np.arange(half, dtype=np.float32) * np.float32(2.0 / HD)
    frequency = np.exp(np.float32(-math.log(10000.0)) * exponent).astype(np.float32)
    angle = frequency[:, None] * np.arange(length, dtype=np.float32)[None, :]
    angle = angle.astype(np.float32).astype(np.float64)
    return np.cos(angle).astype(np.float32), np.sin(angle).astype(np.float32)


def contract(left, right, left_axis, right_axis):
    return lax.dot_general(
        left,
        right,
        (((left_axis,), (right_axis,)), ((), ())),
        preferred_element_type=F32,
    )


def block_at(index, size):
    return pl.ds(pl.multiple_of(index * size, size), size)


def split_three(values):
    high = values.astype(BF16)
    rest = values - high.astype(F32)
    middle = rest.astype(BF16)
    low = (rest - middle.astype(F32)).astype(BF16)
    return high.astype(F32), middle.astype(F32), low.astype(F32)


def augment(rows, extras):
    n = rows.shape[1]
    extras = [jnp.broadcast_to(e, (1, n)) for e in extras]
    pad = jnp.zeros((AUG - HD - len(extras), n), F32)
    return jnp.concatenate([rows] + extras + [pad], axis=0)


def attend_block(heads, here, query, key, value_t, mixed_t, log_total):
    scores = [contract(key[h], query[h, :, here], 1, 0) for h in range(heads)]
    for h in range(heads):
        top = jnp.max(scores[h], axis=0, keepdims=True)
        weights = jnp.exp2((scores[h] - top) * UNIT)
        total = jnp.sum(weights, axis=0, keepdims=True)
        out = contract(value_t[h], weights.astype(BF16), 1, 0) * (1.0 / total)
        mixed_t[h, :, here] = out.astype(BF16)
        log_total[h, :, here] = top * UNIT + jnp.log2(total)


def prepare_backward(heads, h, size, length, qkv, bias, log_total, mixed_t, back_t, query, key, value, back):
    def step(i, _):
        here = block_at(i, size)
        one = jnp.ones((1, size), F32)
        zero = jnp.zeros((1, size), F32)
        logs = split_three(log_total[h, :, here] * (-1.0 / UNIT))
        query[h, :, here] = augment(qkv[h, :, here].astype(F32), [one, *logs]).astype(BF16)
        keys = augment(qkv[heads + h, :, here].astype(F32), [bias[:, here], one, one, one])
        key[h, here, :] = keys.T.astype(BF16)
        values = augment(qkv[2 * heads + h, :, here].astype(F32), [zero, one, one, one])
        value[h, here, :] = values.T.astype(BF16)
        grad = back_t[h, :, here].astype(F32)
        center = jnp.sum(grad * mixed_t[h, :, here].astype(F32), axis=0, keepdims=True)
        back[h, :, here] = augment(grad, [zero, *split_three(-center)]).astype(BF16)
        return 0

    lax.fori_loop(0, length // size, step, 0)


MESH = pl.DeviceIdType.MESH


def local_copies(sources, targets, sems):
    return [pltpu.make_async_copy(a, b, sems.at[i]) for i, (a, b) in enumerate(zip(sources, targets))]


def flip(index, bit):
    return index + bit - 2 * bit * lax.rem(lax.div(index, bit), 2)


def flips(index, bits):
    for bit in bits:
        index = flip(index, bit)
    return index


def doubling(sizes):
    steps = []
    for axis, stride in (("dp", sizes["row"]), ("row", 1)):
        bit = sizes[axis] // 2
        while bit:
            steps.append((axis, bit, bit * stride))
            bit //= 2
    return steps


def subsets(bits):
    out = [()]
    for bit in bits:
        out = out + [kept + (bit,) for kept in out]
    return out


def send_copy(source, target, send, receive, peer):
    return pltpu.make_async_remote_copy(
        src_ref=source, dst_ref=target, send_sem=send, recv_sem=receive, device_id=peer, device_id_type=MESH
    )


def greet(peers):
    barrier = pltpu.get_barrier_semaphore()
    for peer in peers:
        pl.semaphore_signal(barrier, inc=1, device_id=peer, device_id_type=MESH)
    pl.semaphore_wait(barrier, len(peers))


def shard_number(sizes):
    return lax.axis_index("dp") * sizes["row"] + lax.axis_index("row")


def doubling_peers(sizes):
    return [{axis: flip(lax.axis_index(axis), bit)} for axis, bit, _ in doubling(sizes)]


def neighbour_peers(sizes):
    z = lax.axis_index("dp")
    n, m = sizes["dp"], sizes["row"]
    peers = [{"dp": lax.rem(z + 1, n)}, {"dp": lax.rem(z + n - 1, n)}]
    bit = m // 2
    while bit:
        peers.append({"row": flip(lax.axis_index("row"), bit)})
        bit //= 2
    return peers


def col_peers():
    me = lax.axis_index("col")
    return [{"col": flip(me, 1)}, {"col": flip(me, 2)}]


class ShardGather:
    def __init__(self, sizes, shard, full, sems):
        self.n, self.m = sizes["dp"], sizes["row"]
        self.rows = shard.shape[0]
        self.shard, self.full, self.sems = shard, full, sems
        self.z, self.y = lax.axis_index("dp"), lax.axis_index("row")

    def slot(self, z, y):
        return self.full.at[pl.ds(pl.multiple_of((z * self.m + y) * self.rows, self.rows), self.rows), :]

    def held(self, side, h):
        z = self.z - side * h
        return z, (z >= 0) if side > 0 else (z < self.n)

    def onward(self, side):
        return (self.z + 1 < self.n) if side > 0 else (self.z > 0)

    def stream(self, side, h, arriving):
        z, _ = self.held(side, h if arriving else h - 1)
        at = (h - 1) + (self.n - 1 if side < 0 else 0)
        source = self.slot(z, self.y) if arriving or h > 1 else self.shard
        peer = {"dp": self.z + (side if not arriving else -side)}
        return send_copy(source, self.slot(z, self.y), self.sems.at[0, at], self.sems.at[1, at], peer)

    def over(self, side, h, arriving):
        z, _ = self.held(side, h)
        bit = self.m // 2
        at = 2 * (self.n - 1) + h + (self.n - 1 if side < 0 and h else 0)
        there = self.slot(z, flip(self.y, bit) if arriving else self.y)
        source = self.shard if h == 0 and not arriving else there
        return send_copy(source, there, self.sems.at[0, at], self.sems.at[1, at], {"row": flip(self.y, bit)})

    def keep(self):
        self.slot(self.z, self.y)[...] = self.shard[...]

    def start(self):
        for side in (1, -1):

            @pl.when(self.onward(side))
            def _():
                self.stream(side, 1, False).start()

        self.over(1, 0, False).start()

    def advance(self, h):
        if h >= self.n:
            return
        for side in (1, -1):
            _, here = self.held(side, h)

            @pl.when(here)
            def _():
                self.stream(side, h, True).wait_recv()

            if h + 1 < self.n:

                @pl.when(jnp.logical_and(here, self.onward(side)))
                def _():
                    self.stream(side, h + 1, False).start()

            @pl.when(here)
            def _():
                self.over(side, h, False).start()

    def others(self):
        out, held, at = [], (self.m // 2,), 4 * self.n - 3
        bit = self.m // 4
        while bit:
            kept = subsets(held)
            out.append((bit, kept, at))
            at += self.n * len(kept)
            held = held + (bit,)
            bit //= 2
        return out

    def spread(self, bit, kept, at, arriving):
        peer = {"row": flip(self.y, bit)}
        for z in range(self.n):
            for i, bits in enumerate(kept):
                there = self.slot(z, flips(self.y, bits + ((bit,) if arriving else ())))
                k = at + z * len(kept) + i
                yield send_copy(there, there, self.sems.at[0, k], self.sems.at[1, k], peer)

    def finish(self):
        self.over(1, 0, True).wait_recv()
        for side in (1, -1):
            for h in range(1, self.n):

                @pl.when(self.held(side, h)[1])
                def _():
                    self.over(side, h, True).wait_recv()

        for step in self.others():
            for copy in self.spread(*step, False):
                copy.start()
            for copy in self.spread(*step, True):
                copy.wait_recv()

    def close(self):
        self.over(1, 0, False).wait_send()
        for side in (1, -1):
            for h in range(1, self.n):
                _, here = self.held(side, h)

                @pl.when(jnp.logical_and(self.held(side, h - 1)[1], self.onward(side)))
                def _():
                    self.stream(side, h, False).wait_send()

                @pl.when(here)
                def _():
                    self.over(side, h, False).wait_send()

        for step in self.others():
            for copy in self.spread(*step, False):
                copy.wait_send()

    @staticmethod
    def semaphores(sizes):
        n, m = sizes["dp"], sizes["row"]
        return pltpu.SemaphoreType.DMA((2, 4 * n - 3 + n * max(m - 2, 0)))


class ShardScatter:
    def __init__(self, sizes, source, total, out_buf, in_buf, sems):
        self.steps = doubling(sizes)[::-1]
        self.rows = out_buf.shape[1]
        self.source, self.total, self.out_buf, self.in_buf, self.sems = source, total, out_buf, in_buf, sems
        self.me = shard_number(sizes)
        self.first = [0]
        for k in range(len(self.steps)):
            self.first.append(self.first[-1] + 2 ** (len(self.steps) - 1 - k))

    def part(self, number):
        return pl.ds(pl.multiple_of(number * self.rows, self.rows), self.rows)

    def rest(self, k):
        return subsets([s[2] for s in self.steps[k + 1 :]])

    def copy(self, k, i):
        axis, bit, _ = self.steps[k]
        at = self.first[k] + i
        peer = {axis: flip(lax.axis_index(axis), bit)}
        return send_copy(self.out_buf.at[at], self.in_buf.at[at], self.sems.at[0, at], self.sems.at[1, at], peer)

    def held(self, k):
        return self.source if k == 0 else self.total

    def start(self, k):
        stride = self.steps[k][2]
        for i, kept in enumerate(self.rest(k)):
            number = flips(self.me, (stride,) + kept)
            self.out_buf[self.first[k] + i] = self.held(k)[self.part(number), :].astype(BF16)
            self.copy(k, i).start()

    def arrived(self, k):
        for i, kept in enumerate(self.rest(k)):
            self.copy(k, i).wait_recv()
            here = self.part(flips(self.me, kept))
            self.total[here, :] = self.held(k)[here, :].astype(F32) + self.in_buf[self.first[k] + i].astype(F32)

    def advance(self, k):
        if 0 < k <= len(self.steps):
            self.arrived(k - 1)
        if k < len(self.steps):
            self.start(k)

    def result(self):
        return self.total[self.part(self.me), :]

    def close(self):
        for k in range(len(self.steps)):
            for i in range(len(self.rest(k))):
                self.copy(k, i).wait_send()

    @staticmethod
    def scratch(count, rows, width):
        return [
            pltpu.VMEM((count * rows, width), F32),
            pltpu.VMEM((count - 1, rows, width), BF16),
            pltpu.VMEM((count - 1, rows, width), BF16),
            pltpu.SemaphoreType.DMA((2, count - 1)),
        ]


class ColumnGather:
    def __init__(self, full, chunks, sems):
        self.full, self.chunks, self.sems = full, chunks, sems
        self.me = lax.axis_index("col")
        self.rows = full.shape[1] // chunks

    def chunk(self, slot, j):
        return self.full.at[slot, pl.ds(j * self.rows, self.rows), :]

    def copy(self, kind, j, slot):
        peer = {"col": flip(self.me, 2 if kind == 1 else 1)}
        here = self.chunk(slot, j)
        return send_copy(here, here, self.sems.at[0, kind, j], self.sems.at[1, kind, j], peer)

    def start(self, j):
        for kind in (1, 0):
            copy = self.copy(kind, j, self.me)
            copy.start()

    def partner(self, j):
        self.copy(0, j, flip(self.me, 1)).wait_recv()

    def across(self, j):
        there = flip(self.me, 2)
        self.copy(1, j, there).wait_recv()
        copy = self.copy(2, j, there)
        copy.start()

    def diagonal(self, j):
        self.copy(2, j, flips(self.me, (1, 2))).wait_recv()

    def close(self):
        for j in range(self.chunks):
            for kind in range(3):
                self.copy(kind, j, self.me).wait_send()

    @staticmethod
    def semaphores(chunks):
        return pltpu.SemaphoreType.DMA((2, 3, chunks))


class ColumnScatter:
    def __init__(self, pair_out, pair_in, far_out, far_in, kept, chunks, sems):
        self.pair_out, self.pair_in, self.far_out, self.far_in = pair_out, pair_in, far_out, far_in
        self.kept, self.chunks, self.sems = kept, chunks, sems
        self.rows = kept.shape[0] // chunks
        me = lax.axis_index("col")
        self.near, self.far = {"col": flip(me, 1)}, {"col": flip(me, 2)}

    def at(self, j):
        return pl.ds(j * self.rows, self.rows)

    def pair(self, which, j):
        return send_copy(
            self.pair_out.at[which, self.at(j), :],
            self.pair_in.at[which, self.at(j), :],
            self.sems.at[0, which, j],
            self.sems.at[1, which, j],
            self.near,
        )

    def cross(self, j):
        return send_copy(
            self.far_out.at[self.at(j), :],
            self.far_in.at[self.at(j), :],
            self.sems.at[0, 2, j],
            self.sems.at[1, 2, j],
            self.far,
        )

    def begin(self, copy):
        copy.start()

    def give_diagonal(self, j, value):
        self.pair_out[1, self.at(j), :] = value.astype(BF16)
        self.begin(self.pair(1, j))

    def give_across(self, j, value):
        self.pair(1, j).wait_recv()
        self.far_out[self.at(j), :] = (value + self.pair_in[1, self.at(j), :].astype(F32)).astype(BF16)
        if self.far_in is not None:
            self.begin(self.cross(j))

    def give_partner(self, j, value):
        self.pair_out[0, self.at(j), :] = value.astype(BF16)
        self.begin(self.pair(0, j))

    def give_own(self, j, value):
        self.kept[self.at(j), :] = value

    def settle(self, j):
        self.pair(0, j).wait_recv()
        self.kept[self.at(j), :] = self.kept[self.at(j), :] + self.pair_in[0, self.at(j), :].astype(F32)

    def result(self, j):
        self.pair(0, j).wait_recv()
        self.cross(j).wait_recv()
        near = self.kept[self.at(j), :] + self.pair_in[0, self.at(j), :].astype(F32)
        return near + self.far_in[self.at(j), :].astype(F32)

    def close(self):
        for j in range(self.chunks):
            self.pair(0, j).wait_send()
            self.pair(1, j).wait_send()
            if self.far_in is not None:
                self.cross(j).wait_send()

    @staticmethod
    def scratch(rows, width, chunks):
        return [
            pltpu.VMEM((2, rows, width), BF16),
            pltpu.VMEM((2, rows, width), BF16),
            pltpu.VMEM((rows, width), BF16),
            pltpu.VMEM((rows, width), BF16),
            pltpu.VMEM((rows, width), F32),
            pltpu.SemaphoreType.DMA((2, 3, chunks)),
        ]


def other_peers(sizes):
    number = shard_number(sizes)
    total = sizes["dp"] * sizes["row"]
    bits = [stride for _, _, stride in doubling(sizes)]
    out = []
    for kept in subsets(bits)[1:]:
        peer = {}
        for axis, bit, stride in doubling(sizes):
            if stride in kept:
                peer[axis] = flip(peer.get(axis, lax.axis_index(axis)), bit)
        out.append((flips(number, kept), peer))
    assert len(out) == total - 1
    return out


def start_kernel(
    sizes, heads, chunks,
    condition, condition_weight, vectors, tokens, in_weight, out_weight, cosine, sine, cotangent, valid,
    modulation, normed, qkv, out_full, feed_back, bias_part, in_t, condition_all,
    in_shard, out_shard, pieces, arrived, in_full, out_t, unit, sems_tiny, sems_in, sems_out, sems_col,
):
    count = sizes["dp"] * sizes["row"]
    number = shard_number(sizes)
    rows, width = tokens.shape
    others = other_peers(sizes)
    in_shard[...] = jnp.concatenate([in_weight[t] for t in range(3)], axis=1).astype(BF16)
    out_shard[...] = out_weight[...].T.astype(BF16)
    greet([peer for _, peer in others] + col_peers())
    gather_in = ShardGather(sizes, in_shard, in_full, sems_in)
    gather_out = ShardGather(sizes, out_shard, out_t, sems_out)
    gather_col = ColumnGather(normed, chunks, sems_col)

    def condition_copy(i, slot):
        return send_copy(
            condition, condition_all.at[slot], sems_tiny.at[0, i], sems_tiny.at[1, i], others[i][1]
        )

    def piece_copy(i, mine, slot):
        return send_copy(
            pieces.at[mine], arrived.at[slot], sems_tiny.at[2, i], sems_tiny.at[3, i], others[i][1]
        )

    for i in range(count - 1):
        condition_copy(i, number).start()
    gather_in.start()
    gather_out.start()
    condition_all[number] = condition[...]
    gather_in.keep()
    gather_out.keep()
    size = rows // chunks

    def normal(j, _):
        here = block_at(j, size)
        unit[here, :] = layer_norm(tokens[here, :])
        return 0

    lax.fori_loop(0, chunks, normal, 0)
    for i in range(count - 1):
        condition_copy(i, others[i][0]).wait_recv()
    stacked = jnp.concatenate([condition_all[b] for b in range(count)], axis=0)
    product = contract(stacked.astype(BF16), condition_weight[...].astype(BF16), 1, 1)
    for b in range(count):
        pieces[b] = product[b : b + 1]
    for i in range(count - 1):
        piece_copy(i, others[i][0], number).start()
    arrived[number] = pieces[number]
    gather_in.advance(1)
    gather_out.advance(1)
    for i in range(count - 1):
        piece_copy(i, number, others[i][0]).wait_recv()
    line = jnp.concatenate([arrived[b] for b in range(count)], axis=1) + vectors[:, : 6 * width]
    parts = [line[:, t * width : (t + 1) * width] for t in range(6)]
    for t in range(6):
        modulation[t : t + 1, :] = parts[t]
    for j in range(chunks):
        here = pl.ds(j * size, size)
        value = unit[here, :] * (1.0 + parts[1]) + parts[0]
        normed[gather_col.me, here, :] = value.astype(BF16)
        gather_col.start(j)
    gather_in.advance(2)
    gather_out.advance(2)
    gather_in.advance(3)
    gather_out.advance(3)
    total = jnp.zeros((1, width), F32)
    for j in range(chunks):
        here = pl.ds(j * size, size)
        value = parts[5] * (cotangent[here, :] * valid[here, :])
        feed_back[here, :] = value.astype(BF16)
        total = total + jnp.sum(value, axis=0, keepdims=True)
    bias_part[...] = total
    for k in range(4, sizes["dp"]):
        gather_in.advance(k)
        gather_out.advance(k)
    gather_in.finish()
    gather_out.finish()
    in_t[...] = in_full[...].astype(F32).T.astype(BF16)
    out_full[...] = out_t[...].astype(F32).T.astype(BF16)

    def project(slot):
        here = pl.ds(pl.multiple_of(slot * rows, rows), rows)
        both = contract(in_t[...], normed[slot], 1, 1)
        half = HD // 2
        c, s = cosine[:, here], sine[:, here]
        for h in range(heads):
            for t in range(3):
                at = (t * heads + h) * HD
                a, b = both[at : at + half], both[at + half : at + HD]
                if t < 2:
                    a, b = a * c - b * s, b * c + a * s
                qkv[t * heads + h, :, here] = jnp.concatenate([a, b], axis=0).astype(BF16)

    me = gather_col.me
    far = flip(me, 2)

    def steps_of(i, _):
        @pl.when(i == 1)
        def _():
            for j in range(chunks):
                gather_col.partner(j)

        @pl.when(i == 2)
        def _():
            for j in range(chunks):
                gather_col.across(j)

        @pl.when(i == 3)
        def _():
            for j in range(chunks):
                gather_col.diagonal(j)

        project(flip_by(me, i))
        return 0

    lax.fori_loop(0, 4, steps_of, 0)
    for i in range(count - 1):
        condition_copy(i, number).wait_send()
        piece_copy(i, others[i][0], number).wait_send()
    gather_in.close()
    gather_out.close()
    gather_col.close()


def flip_by(index, pattern):
    out = 0
    for bit in (1, 2):
        a, b = lax.rem(lax.div(index, bit), 2), lax.rem(lax.div(pattern, bit), 2)
        out = out + bit * (a + b - 2 * a * b)
    return out


def start(sizes, heads, condition, condition_weight, vectors, tokens, in_weight, out_weight, cosine, sine, cotangent, valid):
    count = sizes["dp"] * sizes["row"]
    rows, width = tokens.shape
    length = cosine.shape[1]
    chunks = 2
    vmem = pl.BlockSpec(memory_space=pltpu.VMEM)
    piece = condition_weight.shape[0]
    local = heads * HD
    return pl.pallas_call(
        functools.partial(start_kernel, sizes, heads, chunks),
        out_shape=[
            jax.ShapeDtypeStruct((6, width), F32),
            jax.ShapeDtypeStruct((4, rows, width), BF16),
            jax.ShapeDtypeStruct((3 * heads, HD, length), BF16),
            jax.ShapeDtypeStruct((local, width), BF16),
            jax.ShapeDtypeStruct((rows, width), BF16),
            jax.ShapeDtypeStruct((1, width), F32),
            jax.ShapeDtypeStruct((3 * local, width), BF16),
            jax.ShapeDtypeStruct((count,) + condition.shape, F32),
        ],
        in_specs=[vmem] * 10,
        out_specs=[vmem] * 8,
        scratch_shapes=[
            pltpu.VMEM((width // count, 3 * local), BF16),
            pltpu.VMEM((width // count, local), BF16),
            pltpu.VMEM((count, 1, piece), F32),
            pltpu.VMEM((count, 1, piece), F32),
            pltpu.VMEM((width, 3 * local), BF16),
            pltpu.VMEM((width, local), BF16),
            pltpu.VMEM((rows, width), F32),
            pltpu.SemaphoreType.DMA((4, count - 1)),
            ShardGather.semaphores(sizes),
            ShardGather.semaphores(sizes),
            ColumnGather.semaphores(chunks),
        ],
        compiler_params=pltpu.CompilerParams(
            vmem_limit_bytes=VMEM_LIMIT, collective_id=0, has_side_effects=True
        ),
    )(condition, condition_weight, vectors, tokens, in_weight, out_weight, cosine, sine, cotangent, valid)


def attention_kernel(
    sizes, heads, chunks,
    qkv, bias, out_full, feed_back, up_shard, down_shard,
    attention, mixed_t, log_total, feed_back_all, up_full, down_t,
    query, key, up_low, down_low,
    pair_out, pair_in, far_out, far_in, kept, sems_scatter, sems_col, sems_up, sems_down,
):
    rows = feed_back.shape[0]
    length = qkv.shape[2]
    up_low[...] = up_shard[...].astype(BF16)
    down_low[...] = down_shard[...].astype(BF16)
    greet(neighbour_peers(sizes) + col_peers())
    gather_up = ShardGather(sizes, up_low, up_full, sems_up)
    gather_down = ShardGather(sizes, down_low, down_t, sems_down)
    gather_col = ColumnGather(feed_back_all, chunks, sems_col)
    scatter = ColumnScatter(pair_out, pair_in, far_out, far_in, kept, 1, sems_scatter)
    me = gather_col.me
    gather_up.start()
    gather_down.start()
    feed_back_all[me] = feed_back[...]
    for j in range(chunks):
        gather_col.start(j)
    gather_up.keep()
    gather_down.keep()

    def prepare(i, _):
        here = block_at(i, rows)
        one = jnp.ones((1, rows), F32)
        for h in range(heads):
            query[h, :, here] = augment(qkv[h, :, here].astype(F32), [one]).astype(BF16)
            keys = augment(qkv[heads + h, :, here].astype(F32), [bias[:, here], one, one, one])
            key[h, here, :] = keys.T.astype(BF16)
        return 0

    lax.fori_loop(0, length // rows, prepare, 0)

    def step(i, _):
        here = block_at(flip_by(me, 3 - i), rows)
        attend_block(heads, here, query, key, qkv.at[pl.ds(2 * heads, heads)], mixed_t, log_total)
        value = contract(mixed_t[:, :, here].reshape(heads * HD, rows), out_full[...], 0, 0)
        for order, give in enumerate(
            (scatter.give_diagonal, scatter.give_across, scatter.give_partner, scatter.give_own)
        ):

            @pl.when(i == order)
            def _():
                give(0, value)
                if order < 3:
                    gather_up.advance(order + 1)
                    gather_down.advance(order + 1)
                if order == 2:
                    for j in range(chunks):
                        gather_col.across(j)

        return 0

    lax.fori_loop(0, 4, step, 0)
    for k in range(4, sizes["dp"]):
        gather_up.advance(k)
        gather_down.advance(k)
    for j in range(chunks):
        gather_col.partner(j)
        gather_col.diagonal(j)
    gather_up.finish()
    gather_down.finish()
    attention[...] = scatter.result(0)
    gather_up.close()
    gather_down.close()
    gather_col.close()
    scatter.close()


def attend(sizes, heads, qkv, bias, out_full, feed_back, up_shard, down_shard):
    count = sizes["dp"] * sizes["row"]
    rows, width = feed_back.shape
    length = qkv.shape[2]
    chunks = 2
    hidden = up_shard.shape[1]
    vmem = pl.BlockSpec(memory_space=pltpu.VMEM)
    return pl.pallas_call(
        functools.partial(attention_kernel, sizes, heads, chunks),
        out_shape=[
            jax.ShapeDtypeStruct((rows, width), F32),
            jax.ShapeDtypeStruct((heads, HD, length), BF16),
            jax.ShapeDtypeStruct((heads, 1, length), F32),
            jax.ShapeDtypeStruct((4, rows, width), BF16),
            jax.ShapeDtypeStruct((width, hidden), BF16),
            jax.ShapeDtypeStruct((width, hidden), BF16),
        ],
        in_specs=[vmem] * 6,
        out_specs=[vmem] * 6,
        scratch_shapes=[
            pltpu.VMEM((heads, AUG, length), BF16),
            pltpu.VMEM((heads, length, AUG), BF16),
            pltpu.VMEM((width // count, hidden), BF16),
            pltpu.VMEM((width // count, hidden), BF16),
            *ColumnScatter.scratch(rows, width, 1),
            ColumnGather.semaphores(chunks),
            ShardGather.semaphores(sizes),
            ShardGather.semaphores(sizes),
        ],
        compiler_params=pltpu.CompilerParams(
            vmem_limit_bytes=VMEM_LIMIT, collective_id=1, has_side_effects=True
        ),
    )(qkv, bias, out_full, feed_back, up_shard, down_shard)


def feed_kernel(
    sizes, heads, chunks,
    tokens, attention, parts, vectors, valid, up_far, down_far, feed_back_far, cotangent_far, mixed_far, out_far,
    mixed_back, out_grad, up_part, sums, middle_to, middle_back_to, up_to, down_to, feed_far_to, feed_kept_to,
    second_all, hidden_all, before_all, back_all, second_sems, back_sems,
    pair_out, pair_in, far_out, far_in, kept, scatter_sems, feed_pair_out, feed_pair_in, feed_sems,
    up_full, down_t, feed_back_all, cotangent, mixed_t, out_full,
    middle, middle_back, up_grad, down_grad, feed_far, feed_kept, load_sems, store_sems,
):
    rows, width = tokens.shape
    size = rows // chunks
    loads = local_copies(
        (up_far, down_far, feed_back_far, cotangent_far, mixed_far, out_far),
        (up_full, down_t, feed_back_all, cotangent, mixed_t, out_full),
        load_sems,
    )
    stores = local_copies(
        (middle, feed_far, middle_back, up_grad, down_grad, feed_kept),
        (middle_to, feed_far_to, middle_back_to, up_to, down_to, feed_kept_to),
        store_sems,
    )
    for copy in loads:
        copy.start()
    length = 4 * rows
    greet(col_peers())
    gather = ColumnGather(second_all, chunks, second_sems)
    gather_back = ColumnGather(back_all, chunks, back_sems)
    scatter = ColumnScatter(pair_out, pair_in, far_out, far_in, kept, chunks, scatter_sems)
    feed = ColumnScatter(feed_pair_out, feed_pair_in, feed_far, None, feed_kept, chunks, feed_sems)
    me = gather.me
    for j in range(chunks):
        here = pl.ds(j * size, size)
        value = tokens[here, :] + parts[2:3, :] * attention[here, :]
        middle[here, :] = value
        second_all[me, here, :] = (layer_norm(value) * (1.0 + parts[4:5, :]) + parts[3:4, :]).astype(BF16)
        gather.start(j)
    up_part[...] = jnp.zeros_like(up_part)
    for copy in loads:
        copy.wait()

    def block(i, _):
        late = lax.div(i, 4)
        pattern = (1 - late) * lax.div(i, 2) + late * (3 - lax.rem(i, 2))
        j = (1 - late) * lax.rem(i, 2) + late * (lax.div(i, 2) - 2)
        slot = flip_by(me, pattern)
        here = pl.ds(pl.multiple_of(j * size, size), size)

        @pl.when(i == 2)
        def _():
            for c in range(chunks):
                gather.partner(c)

        @pl.when(i == 3)
        def _():
            gather.across(0)

        @pl.when(i == 4)
        def _():
            gather.diagonal(0)

        @pl.when(i == 6)
        def _():
            gather.diagonal(1)

        before = contract(second_all[slot, here, :], up_full[...], 1, 0) + vectors[:, 6 * width : 6 * width + up_part.shape[1]]
        bend = jnp.tanh(SLOPE * (before + CUBIC * before * before * before))
        hidden = (0.5 * before * (1.0 + bend)).astype(BF16)
        slope = 0.5 * (1.0 + bend) + 0.5 * before * (1.0 - bend * bend) * (SLOPE * (1.0 + 3.0 * CUBIC * before * before))
        hidden_back = contract(feed_back_all[slot, here, :], down_t[...], 1, 0)
        before_back = (hidden_back * slope).astype(BF16)
        hidden_all[slot, here, :] = hidden
        before_all[slot, here, :] = before_back
        up_part[...] += jnp.sum(before_back.astype(F32), axis=0, keepdims=True)
        back_value = contract(before_back, up_full[...], 1, 1)
        feed_value = contract(hidden, down_t[...], 1, 1)
        for at, (name, c) in enumerate(
            (("own", 0), ("own", 1), ("partner", 0), ("partner", 1), ("diagonal", 0), ("across", 0), ("diagonal", 1), ("across", 1))
        ):

            @pl.when(i == at)
            def _():
                getattr(scatter, "give_" + name)(c, back_value)
                getattr(feed, "give_" + name)(c, feed_value)
                if at == 5:
                    gather.across(1)

        return 0

    lax.fori_loop(0, 8, block, 0)
    stores[0].start()
    stores[1].start()
    gate_sum = jnp.zeros((1, width), F32)
    shift_sum = jnp.zeros((1, width), F32)
    scale_sum = jnp.zeros((1, width), F32)
    for j in range(chunks):
        here = pl.ds(j * size, size)
        own = middle[here, :]
        center = own - jnp.mean(own, axis=-1, keepdims=True)
        inverse = lax.rsqrt(jnp.mean(center * center, axis=-1, keepdims=True) + EPSILON)
        unit = center * inverse
        grad = scatter.result(j)
        scaled = grad * (1.0 + parts[4:5, :])
        inner = scaled - jnp.mean(scaled, axis=-1, keepdims=True) - unit * jnp.mean(scaled * unit, axis=-1, keepdims=True)
        total = cotangent[here, :] * valid[here, :] + inverse * inner
        middle_back[here, :] = total
        back_all[me, here, :] = (parts[2:3, :] * total).astype(BF16)
        gather_back.start(j)
        gate_sum = gate_sum + jnp.sum(total * attention[here, :], axis=0, keepdims=True)
        shift_sum = shift_sum + jnp.sum(grad, axis=0, keepdims=True)
        scale_sum = scale_sum + jnp.sum(grad * unit, axis=0, keepdims=True)
        if j == 0:
            up_grad[...] = contract(second_all[...].reshape(length, width), before_all[...].reshape(length, -1), 0, 0).astype(BF16)
        if j == 1:
            down_grad[...] = contract(feed_back_all[...].reshape(length, width), hidden_all[...].reshape(length, -1), 0, 0).astype(BF16)
    sums[...] = jnp.concatenate([gate_sum, shift_sum, scale_sum], axis=1)
    for j in range(chunks):
        feed.settle(j)
    gather_back.across(0)
    for copy in stores[2:5]:
        copy.start()

    def mix(i, _):
        @pl.when(i == 1)
        def _():
            for c in range(chunks):
                gather_back.partner(c)

        @pl.when(i == 2)
        def _():
            stores[5].start()
            gather_back.across(1)

        @pl.when(i == 3)
        def _():
            for c in range(chunks):
                gather_back.diagonal(c)

        slot = flip_by(me, i)
        here = block_at(slot, rows)
        value = contract(out_full[...], back_all[slot], 1, 1).astype(BF16)
        for h in range(heads):
            mixed_back[h, :, here] = value[h * HD : (h + 1) * HD]
        return 0

    lax.fori_loop(0, 4, mix, 0)
    out_grad[...] = contract(
        back_all[...].reshape(length, width), mixed_t[...].reshape(heads * HD, length), 0, 1
    ).astype(BF16)
    for copy in stores:
        copy.wait()
    gather.close()
    gather_back.close()
    scatter.close()
    feed.close()


def feed_forward(
    sizes, heads, tokens, attention, parts, up_full, down_t, vectors, feed_back_all, cotangent, valid, mixed_t, out_full
):
    rows, width = tokens.shape
    hidden = up_full.shape[1]
    length = 4 * rows
    local = heads * HD
    chunks = 2
    vmem = pl.BlockSpec(memory_space=pltpu.VMEM)
    far = pl.BlockSpec(memory_space=pl.ANY)
    own = jax.ShapeDtypeStruct((rows, width), F32)
    late = (up_full, down_t, feed_back_all, cotangent, mixed_t, out_full)
    return pl.pallas_call(
        functools.partial(feed_kernel, sizes, heads, chunks),
        out_shape=[
            jax.ShapeDtypeStruct((heads, HD, length), BF16),
            jax.ShapeDtypeStruct((width, local), BF16),
            jax.ShapeDtypeStruct((1, hidden), F32),
            jax.ShapeDtypeStruct((1, 3 * width), F32),
            own,
            own,
            jax.ShapeDtypeStruct((width, hidden), BF16),
            jax.ShapeDtypeStruct((width, hidden), BF16),
            jax.ShapeDtypeStruct((rows, width), BF16),
            own,
        ],
        in_specs=[vmem] * 5 + [far] * 6,
        out_specs=[vmem] * 4 + [far] * 6,
        scratch_shapes=[
            pltpu.VMEM((4, rows, width), BF16),
            pltpu.VMEM((4, rows, hidden), BF16),
            pltpu.VMEM((4, rows, hidden), BF16),
            pltpu.VMEM((4, rows, width), BF16),
            ColumnGather.semaphores(chunks),
            ColumnGather.semaphores(chunks),
            *ColumnScatter.scratch(rows, width, chunks),
            pltpu.VMEM((2, rows, width), BF16),
            pltpu.VMEM((2, rows, width), BF16),
            pltpu.SemaphoreType.DMA((2, 3, chunks)),
            *[pltpu.VMEM(one.shape, one.dtype) for one in late],
            pltpu.VMEM((rows, width), F32),
            pltpu.VMEM((rows, width), F32),
            pltpu.VMEM((width, hidden), BF16),
            pltpu.VMEM((width, hidden), BF16),
            pltpu.VMEM((rows, width), BF16),
            pltpu.VMEM((rows, width), F32),
            pltpu.SemaphoreType.DMA((6,)),
            pltpu.SemaphoreType.DMA((6,)),
        ],
        compiler_params=pltpu.CompilerParams(
            vmem_limit_bytes=VMEM_LIMIT, collective_id=3, has_side_effects=True
        ),
    )(tokens, attention, parts, vectors, valid, *late)


def contract_exact(left, right, left_axis, right_axis):
    return lax.dot_general(
        left,
        right,
        (((left_axis,), (right_axis,)), ((), ())),
        precision=lax.Precision.HIGHEST,
        preferred_element_type=F32,
    )


def finish_kernel(
    sizes, heads, chunks,
    qkv, bias, log_total, mixed_t, back_t, cosine, sine, up_source, down_source, out_source,
    parts, others, down_part, up_part, condition_all, condition_weight, feed_far, valid, vectors,
    normed_far, in_far, tokens_far, middle_back_far, middle_far, feed_kept_far, cotangent_far,
    output_to, tokens_back_to, condition_back, condition_grad, bias_grad, up_bias, down_bias, in_grad, out_grad, up_grad, down_grad,
    turned, query, key, value, back, key_sum, value_sum, in_source,
    in_total, in_out, in_in, in_sems, up_total, up_out, up_in, up_sems,
    down_total, down_out, down_in, down_sems, out_total, out_out, out_in, out_sems,
    pair_out, pair_in, far_out, far_in, kept, col_sems,
    line_out, line_in, up_all, pieces, arrived, backs, collected, tiny_sems, line_sems, feed_in, feed_sems,
    normed, in_t, tokens, middle_back, middle, feed_kept, cotangent, output, tokens_back, load_sems, store_sems,
    condition_low, weight_low,
):
    count = sizes["dp"] * sizes["row"]
    number = shard_number(sizes)
    length = qkv.shape[2]
    rows, width = tokens.shape
    half = HD // 2
    piece, cond = condition_weight.shape
    peers = other_peers(sizes)
    me = lax.axis_index("col")
    near, far = col_peers()
    greet([peer for _, peer in peers] + [near, far, {"col": flips(me, (1, 2))}])
    loads = local_copies(
        (normed_far, in_far, tokens_far, middle_back_far, middle_far, feed_kept_far, cotangent_far),
        (normed, in_t, tokens, middle_back, middle, feed_kept, cotangent),
        load_sems,
    )
    stores = local_copies((output, tokens_back), (output_to, tokens_back_to), store_sems)
    for copy in loads:
        copy.start()
    scatter_up = ShardScatter(sizes, up_source, up_total, up_out, up_in, up_sems)
    scatter_down = ShardScatter(sizes, down_source, down_total, down_out, down_in, down_sems)
    scatter_out = ShardScatter(sizes, out_source, out_total, out_out, out_in, out_sems)
    scatter_in = ShardScatter(sizes, in_source, in_total, in_out, in_in, in_sems)
    column = ColumnScatter(pair_out, pair_in, far_out, far_in, kept, chunks, col_sems)

    def tiny(kind, i, source, target):
        return send_copy(source, target, tiny_sems.at[0, kind, i], tiny_sems.at[1, kind, i], peers[i][1])

    def up_copy(i, slot):
        return tiny(0, i, up_part, up_all.at[slot])

    def piece_copy(i, mine, slot):
        return tiny(1, i, pieces.at[mine], arrived.at[slot])

    def back_copy(i, mine, slot):
        return tiny(2, i, backs.at[mine], collected.at[slot])

    def line_copy(k, arriving):
        other = flips(me, [bit for bit in (1, 2) if k & bit])
        slot = other if arriving else me
        return send_copy(
            line_out, line_in.at[slot], line_sems.at[0, k - 1], line_sems.at[1, k - 1], {"col": other}
        )

    feed_copy = send_copy(feed_far, feed_in, feed_sems.at[0], feed_sems.at[1], far)
    feed_copy.start()
    scatter_up.start(0)
    scatter_down.start(0)
    scatter_out.start(0)
    for i in range(count - 1):
        up_copy(i, number).start()
    up_all[number] = up_part[...]

    def turn_back(values, here):
        c, s = cosine[:, here], sine[:, here]
        a, b = values[:half], values[half:]
        return jnp.concatenate([a * c + b * s, b * c - a * s], axis=0)

    for h in range(heads):
        prepare_backward(heads, h, rows, length, qkv, bias, log_total, mixed_t, back_t, query, key, value, back)
    condition_low[...] = jnp.concatenate([condition_all[b] for b in range(count)], axis=0).astype(BF16)
    weight_low[...] = condition_weight[...].astype(BF16)
    key_sum[...] = jnp.zeros_like(key_sum)
    value_sum[...] = jnp.zeros_like(value_sum)

    def step(i, _):
        here = block_at(i, rows)
        for h in range(heads):
            q, d = query[h, :, here], back[h, :, here]
            weights = jnp.exp2(contract(key[h], q, 1, 0) * UNIT)
            grads = (weights * contract(value[h], d, 1, 0)).astype(BF16)
            value_sum[h] += contract(d[:HD], weights.astype(BF16), 1, 1)
            key_sum[h] += contract(q[:HD], grads, 1, 1)
            query_back = contract(qkv[heads + h], grads, 1, 0) * SCALE
            turned[h, :, here] = turn_back(query_back, here).astype(BF16)

        @pl.when(i == 1)
        def _():
            scatter_up.advance(1)

        @pl.when(i == 2)
        def _():
            scatter_down.advance(1)
            scatter_out.advance(1)
            scatter_up.advance(2)

        return 0

    lax.fori_loop(0, 4, step, 0)

    def finish_block(i, _):
        here = block_at(i, rows)
        for h in range(heads):
            turned[heads + h, :, here] = turn_back(key_sum[h, :, here] * SCALE, here).astype(BF16)
            turned[2 * heads + h, :, here] = value_sum[h, :, here].astype(BF16)
        return 0

    lax.fori_loop(0, 4, finish_block, 0)
    for copy in loads:
        copy.wait()
    size = rows // chunks

    def part_of(slot, j):
        start_at = pl.multiple_of(slot * rows + j * size, size)
        block = turned[:, :, pl.ds(start_at, size)].reshape(3 * heads * HD, size)
        return contract(block, in_t[...], 0, 0)

    for j in range(chunks + 1):
        if j < chunks:
            column.give_diagonal(j, part_of(flips(me, (1, 2)), j))
        if j > 0:
            column.give_across(j - 1, part_of(flip(me, 2), j - 1))
    scatter_down.advance(2)
    scatter_out.advance(2)
    in_source[...] = contract(
        turned[...].reshape(3 * heads * HD, length), normed[...], 1, 0
    ).T.astype(BF16)
    scatter_in.start(0)
    scatter_up.advance(3)
    for j in range(chunks):
        column.give_partner(j, part_of(flip(me, 1), j))
    for j in range(chunks):
        column.give_own(j, part_of(me, j))
    scatter_down.advance(3)
    scatter_out.advance(3)
    shift_sum = jnp.zeros((1, width), F32)
    scale_sum = jnp.zeros((1, width), F32)
    gate_sum = jnp.zeros((1, width), F32)
    feed_copy.wait_recv()
    for j in range(chunks):
        here = pl.ds(j * size, size)
        feed = feed_kept[here, :] + feed_in[here, :].astype(F32) + vectors[:, vectors.shape[1] - width :]
        output[here, :] = middle[here, :] + parts[5:6, :] * feed
        gate_sum = gate_sum + jnp.sum(cotangent[here, :] * valid[here, :] * feed, axis=0, keepdims=True)
    scatter_in.advance(1)
    for j in range(chunks):
        here = pl.ds(j * size, size)
        own = tokens[here, :]
        center = own - jnp.mean(own, axis=-1, keepdims=True)
        inverse = lax.rsqrt(jnp.mean(center * center, axis=-1, keepdims=True) + EPSILON)
        unit = center * inverse
        grad = column.result(j)
        scaled = grad * (1.0 + parts[1:2, :])
        inner = scaled - jnp.mean(scaled, axis=-1, keepdims=True) - unit * jnp.mean(scaled * unit, axis=-1, keepdims=True)
        tokens_back[here, :] = middle_back[here, :] + inverse * inner
        shift_sum = shift_sum + jnp.sum(grad, axis=0, keepdims=True)
        scale_sum = scale_sum + jnp.sum(grad * unit, axis=0, keepdims=True)
    line_out[...] = jnp.concatenate([shift_sum, scale_sum, others[...], gate_sum, down_part[...]], axis=1)
    for k in (2, 3, 1):
        line_copy(k, False).start()
    line_in[me] = line_out[...]
    scatter_in.advance(2)
    for copy in stores:
        copy.start()
    steps = len(scatter_in.steps)
    for k in range(4, steps + 1):
        for one in (scatter_up, scatter_down, scatter_out):
            one.advance(k)
    up_grad[...] = scatter_up.result()
    down_grad[...] = scatter_down.result()
    out_grad[...] = scatter_out.result()
    for i in range(count - 1):
        up_copy(i, peers[i][0]).wait_recv()
    up_bias[...] = jnp.sum(jnp.concatenate([up_all[b] for b in range(count)], axis=0), axis=0, keepdims=True)
    for k in (1, 2, 3):
        line_copy(k, True).wait_recv()
    line = (line_in[0] + line_in[1]) + (line_in[2] + line_in[3])
    split = 6 * width
    for b in range(count):
        pieces[b] = jnp.concatenate([line[:, b * piece : (b + 1) * piece], line[:, split:]], axis=1)
    for i in range(count - 1):
        piece_copy(i, peers[i][0], number).start()
    arrived[number] = pieces[number]
    for i in range(count - 1):
        piece_copy(i, number, peers[i][0]).wait_recv()
    stacked = jnp.concatenate([arrived[b] for b in range(count)], axis=0)
    mine = stacked[:, :piece]
    down_bias[...] = jnp.sum(stacked[:, piece:], axis=0, keepdims=True)
    bias_piece = jnp.sum(mine, axis=0, keepdims=True)
    back_rows = contract_exact(mine, weight_low[...].astype(F32), 1, 0)
    for b in range(count):
        backs[b] = jnp.concatenate([back_rows[b : b + 1], bias_piece], axis=1)
    for i in range(count - 1):
        back_copy(i, peers[i][0], number).start()
    collected[number] = backs[number]
    for k in range(3, steps + 1):
        scatter_in.advance(k)
    in_grad[...] = scatter_in.result()
    condition_grad[...] = contract_exact(condition_low[...].astype(F32), mine, 0, 0).T
    for i in range(count - 1):
        back_copy(i, number, peers[i][0]).wait_recv()
    gathered = [collected[b] for b in range(count)]
    bias_grad[...] = jnp.concatenate([one[:, cond:] for one in gathered], axis=1)
    condition_back[...] = jnp.sum(
        jnp.concatenate([one[:, :cond] for one in gathered], axis=0), axis=0, keepdims=True
    )
    for i in range(count - 1):
        up_copy(i, number).wait_send()
        piece_copy(i, peers[i][0], number).wait_send()
        back_copy(i, peers[i][0], number).wait_send()
    for k in (1, 2, 3):
        line_copy(k, False).wait_send()
    for copy in stores:
        copy.wait()
    feed_copy.wait_send()
    for one in (scatter_up, scatter_down, scatter_out, scatter_in):
        one.close()
    column.close()


def finish(sizes, heads, qkv, bias, log_total, mixed_t, back_t, cosine, sine, normed, in_t, up_source, down_source,
           out_source, tokens, middle_back, parts, others, down_part, up_part, condition_all, condition_weight,
           middle, feed_far, feed_kept, cotangent, valid, vectors):
    count = sizes["dp"] * sizes["row"]
    length = qkv.shape[2]
    rows, width = tokens.shape
    chunks = 4
    local = heads * HD
    hidden = up_source.shape[1]
    piece, cond = condition_weight.shape
    share = width // count
    late = (normed, in_t, tokens, middle_back, middle, feed_kept, cotangent)
    far = pl.BlockSpec(memory_space=pl.ANY)
    vmem = pl.BlockSpec(memory_space=pltpu.VMEM)
    return pl.pallas_call(
        functools.partial(finish_kernel, sizes, heads, chunks),
        out_shape=[
            jax.ShapeDtypeStruct((rows, width), F32),
            jax.ShapeDtypeStruct((rows, width), F32),
            jax.ShapeDtypeStruct((1, cond), F32),
            jax.ShapeDtypeStruct((piece, cond), F32),
            jax.ShapeDtypeStruct((1, 6 * width), F32),
            jax.ShapeDtypeStruct((1, hidden), F32),
            jax.ShapeDtypeStruct((1, width), F32),
            jax.ShapeDtypeStruct((share, 3 * local), F32),
            jax.ShapeDtypeStruct((share, local), F32),
            jax.ShapeDtypeStruct((share, hidden), F32),
            jax.ShapeDtypeStruct((share, hidden), F32),
        ],
        in_specs=[vmem] * 16 + [far] + [vmem] * 2 + [far] * len(late),
        out_specs=[far] * 2 + [vmem] * 9,
        scratch_shapes=[
            pltpu.VMEM((3 * heads, HD, length), BF16),
            pltpu.VMEM((heads, AUG, length), BF16),
            pltpu.VMEM((heads, length, AUG), BF16),
            pltpu.VMEM((heads, length, AUG), BF16),
            pltpu.VMEM((heads, AUG, length), BF16),
            pltpu.VMEM((heads, HD, length), F32),
            pltpu.VMEM((heads, HD, length), F32),
            pltpu.VMEM((width, 3 * local), BF16),
            *ShardScatter.scratch(count, share, 3 * local),
            *ShardScatter.scratch(count, share, hidden),
            *ShardScatter.scratch(count, share, hidden),
            *ShardScatter.scratch(count, share, local),
            *ColumnScatter.scratch(rows, width, chunks),
            pltpu.VMEM((1, 7 * width), F32),
            pltpu.VMEM((4, 1, 7 * width), F32),
            pltpu.VMEM((count, 1, hidden), F32),
            pltpu.VMEM((count, 1, piece + width), F32),
            pltpu.VMEM((count, 1, piece + width), F32),
            pltpu.VMEM((count, 1, cond + piece), F32),
            pltpu.VMEM((count, 1, cond + piece), F32),
            pltpu.SemaphoreType.DMA((2, 3, count - 1)),
            pltpu.SemaphoreType.DMA((2, 3)),
            pltpu.VMEM((rows, width), BF16),
            pltpu.SemaphoreType.DMA((2,)),
            *[pltpu.VMEM(one.shape, one.dtype) for one in late],
            pltpu.VMEM((rows, width), F32),
            pltpu.VMEM((rows, width), F32),
            pltpu.SemaphoreType.DMA((len(late),)),
            pltpu.SemaphoreType.DMA((2,)),
            pltpu.VMEM((count, cond), BF16),
            pltpu.VMEM((piece, cond), BF16),
        ],
        compiler_params=pltpu.CompilerParams(
            vmem_limit_bytes=VMEM_LIMIT, collective_id=2, has_side_effects=True
        ),
    )(qkv, bias, log_total, mixed_t, back_t, cosine, sine, up_source, down_source, out_source,
      parts, others, down_part, up_part, condition_all, condition_weight, feed_far, valid, vectors, *late)


def emit_kernel(heads, output, tokens_back, condition_grad, in_grad, out_grad, up_grad, down_grad, *rest):
    output_to, tokens_to, condition_to, in_to, out_to, up_to, down_to = rest[4:11]
    for one, to in zip(rest[:3], rest[11:14]):
        to[...] = one[...].reshape(to.shape)
    rest[14][...] = rest[3][...]
    output_to[...] = output[...]
    tokens_to[...] = tokens_back[...]
    condition_to[...] = condition_grad[...]
    local = heads * HD
    for t in range(3):
        in_to[t] = in_grad[:, t * local : (t + 1) * local]
    out_to[...] = out_grad[...].T
    up_to[...] = up_grad[...]
    down_to[...] = down_grad[...]


def emit(heads, *arrays):
    output, tokens_back, condition_grad, in_grad, out_grad, up_grad, down_grad = arrays[:7]
    share, local = out_grad.shape
    vmem = pl.BlockSpec(memory_space=pltpu.VMEM)
    shapes = [
        output.shape, tokens_back.shape, condition_grad.shape, (3, share, local), (local, share),
        up_grad.shape, down_grad.shape, *[one.shape[1:] for one in arrays[7:10]], arrays[10].shape,
    ]
    return pl.pallas_call(
        functools.partial(emit_kernel, heads),
        out_shape=[jax.ShapeDtypeStruct(one, F32) for one in shapes],
        in_specs=[vmem] * 11,
        out_specs=[vmem] * 11,
    )(*arrays)


def shards(
    sizes,
    tokens,
    condition,
    lengths,
    condition_weight,
    condition_bias,
    attention_in,
    attention_out,
    up_weight,
    up_bias,
    down_weight,
    down_bias,
    cotangent,
):
    columns = lax.axis_size("col")
    column_index = lax.axis_index("col")
    rows = tokens.shape[1]
    width = tokens.shape[2]
    length_all = rows * columns
    local_width = attention_in.shape[2]
    heads = local_width // HD
    own_rows = tokens[0]
    length = lengths[0]
    position = column_index * rows + jnp.arange(rows)
    valid = (position < length).astype(F32)
    bias = jnp.where(jnp.arange(length_all) < length, 0.0, MASKED).astype(F32)[None]
    cosine, sine = (jnp.asarray(table) for table in rotary_tables(length_all))
    hidden_cols = up_weight.shape[1]
    bias_part = lax.dynamic_slice_in_dim(up_bias, column_index * hidden_cols, hidden_cols)
    vectors = jnp.concatenate([condition_bias, bias_part, down_bias])[None]
    parts, normed_blocks, qkv, out_full, feed_back, down_bias_part, in_t, condition_all = start(
        sizes, heads, condition, condition_weight.T, vectors, own_rows,
        jnp.transpose(attention_in, (1, 0, 2)), attention_out, cosine, sine, cotangent[0], valid[:, None],
    )
    normed_all = normed_blocks.reshape(length_all, width)
    attention, mixed_t, log_total, feed_back_blocks, up_full, down_t = attend(
        sizes, heads, qkv, bias, out_full, feed_back, up_weight, down_weight.T
    )
    (
        mixed_back, out_grad, up_bias_part, others, middle, middle_back, up_grad, down_grad, feed_far, feed_kept
    ) = feed_forward(
        sizes, heads, own_rows, attention, parts, up_full, down_t, vectors, feed_back_blocks,
        cotangent[0], valid[:, None], mixed_t, out_full,
    )
    (
        result, tokens_back, condition_back, condition_grad, bias_grad, up_bias_grad, down_bias_grad,
        in_grad, out_grad, up_grad, down_grad,
    ) = finish(
        sizes, heads, qkv, bias, log_total, mixed_t, mixed_back,
        cosine, sine, normed_all, in_t, up_grad, down_grad, out_grad, own_rows, middle_back, parts,
        others, down_bias_part, up_bias_part, condition_all, condition_weight.T,
        middle, feed_far, feed_kept, cotangent[0], valid[:, None], vectors,
    )
    (
        result, tokens_back, condition_grad, in_grad, out_grad, up_grad, down_grad,
        bias_grad, up_bias_grad, down_bias_grad, condition_back,
    ) = emit(
        heads, result, tokens_back, condition_grad, in_grad, out_grad, up_grad, down_grad,
        bias_grad, up_bias_grad, down_bias_grad, condition_back,
    )
    return (
        result[None],
        tokens_back[None],
        condition_back,
        condition_grad.T,
        bias_grad,
        jnp.transpose(in_grad, (1, 0, 2)),
        out_grad,
        up_grad,
        up_bias_grad,
        down_grad.T,
        down_bias_grad,
    )


def solution(mesh):
    sizes = {axis: mesh.shape[axis] for axis in ("dp", "row", "col")}
    in_specs = (
        P(("dp", "row"), "col", None),
        P(("dp", "row"), None),
        P(("dp", "row")),
        P(None, ("dp", "row")),
        P(),
        P(("dp", "row"), None, "col"),
        P("col", ("dp", "row")),
        P(("dp", "row"), "col"),
        P(),
        P("col", ("dp", "row")),
        P(),
        P(("dp", "row"), "col", None),
    )
    out_specs = (
        P(("dp", "row"), "col", None),
        P(("dp", "row"), "col", None),
        P(("dp", "row"), None),
        P(None, ("dp", "row")),
        P(),
        P(("dp", "row"), None, "col"),
        P("col", ("dp", "row")),
        P(("dp", "row"), "col"),
        P("col"),
        P("col", ("dp", "row")),
        P(),
    )
    return jax.shard_map(functools.partial(shards, sizes), mesh=mesh, in_specs=in_specs, out_specs=out_specs, check_vma=False)
```
